128 devices in a mesh: leaf: 8 (over x, core), panel: 16 (over z, y).
Axes of the slice: x: 4, y: 4, z: 4, core: 2. Of those that a mesh axis runs over, the one named last changes fastest.
Arguments:
- live_tiles: int32 [15], replicated, may hold values from 8 to 16
- row_tiles: int32 [14, 8], replicated, may hold values from 0 to 47, as said below
- rhs0: float32 [256, 16384], P('panel', 'leaf'), may hold values from -6 to 6
- rhs1: float32 [256, 8192], P('panel', 'leaf'), may hold values from -6 to 6
- rhs2: float32 [256, 4096], P('panel', 'leaf'), may hold values from -6 to 6
- rhs3: float32 [256, 2048], P('panel', 'leaf'), may hold values from -6 to 6
- dinv0: float32 [16384, 2048], P('leaf', 'panel'), as said below
- dinv1: float32 [8192, 2048], P('leaf', 'panel'), as said below
- dinv2: float32 [4096, 2048], P('leaf', 'panel'), as said below
- dinv3: float32 [2048, 2048], P('leaf', 'panel'), as said below
- off0: float32 [8192, 2048], P('leaf', 'panel'), may hold values from -0.125 to 0.125
- off1: float32 [4096, 2048], P('leaf', 'panel'), may hold values from -0.125 to 0.125
- off2: float32 [2048, 2048], P('leaf', 'panel'), may hold values from -0.125 to 0.125
Outputs:
- sol0: float32 [256, 16384], P('panel', 'leaf')
- sol1: float32 [256, 8192], P('panel', 'leaf')
- sol2: float32 [256, 4096], P('panel', 'leaf')
- sol3: float32 [256, 2048], P('panel', 'leaf')
The draws below stay inside these ranges and needn't reach their ends.
Inputs may be any that keep to these rules, and one draw needn't show every extreme that they name: `row_tiles`: each row names 8 different tiles; for a supernode of level k every value is below (3 - k) * 16. `live_tiles`: counted level by level in the supernodes' order. `dinv0`: each 2048 x 2048 row block is lower triangular with diagonal entries from 0.5 to 2. `dinv1`: each 2048 x 2048 row block is lower triangular with diagonal entries from 0.5 to 2. `dinv2`: each 2048 x 2048 row block is lower triangular with diagonal entries from 0.5 to 2. `dinv3`: each 2048 x 2048 row block is lower triangular with diagonal entries from 0.5 to 2.
All inputs are finite; a program needn't handle non-finite values.
Results may differ from the reference program's by a relative error of at most 0.00028.
Values sent between devices are 32-bit elements; how exact they have to be, the bound alone decides.
No kernel may reach another device: no remote copies, remote signals or barrier semaphores. Data moves between devices by JAX's collectives and lax.ppermute only.
A program may use at most 64 MiB of HBM per device.

```python
import math
import jax
import jax.numpy as jnp
from jax import lax

B = 128
NT = 16
ORDER = 2048
RT = 8
R = 256
LEVELS = 4
NODES0 = 8
NODES1 = 4
NODES2 = 2
NODES3 = 1
NODES_ALL = 15


def lower_inverse(key, number):
    row_pos = (jnp.arange(number * ORDER, dtype=jnp.int32) % ORDER)[:, None]
    col_pos = jnp.arange(ORDER, dtype=jnp.int32)[None, :]
    first_key, second_key = jax.random.split(jax.random.fold_in(key, 91))
    spread = jax.random.normal(first_key, (number * ORDER, ORDER), jnp.float32)
    diagonal = jax.random.uniform(second_key, (number * ORDER, 1), jnp.float32, 0.6, 1.6)
    below_diagonal = (col_pos < row_pos).astype(jnp.float32)
    on_diagonal = (col_pos == row_pos).astype(jnp.float32)
    return below_diagonal * spread * (0.6 / math.sqrt(ORDER)) + on_diagonal * diagonal


def draw_dinv0(key, part):
    return lower_inverse(key, NODES0)


def draw_dinv1(key, part):
    return lower_inverse(key, NODES1)


def draw_dinv2(key, part):
    return lower_inverse(key, NODES2)


def draw_dinv3(key, part):
    return lower_inverse(key, NODES3)


def draw_row_tiles(key, part):
    numbers = [NODES0, NODES1, NODES2]
    row_list = []
    for height in range(LEVELS - 1):
        span = (LEVELS - 1 - height) * NT
        node_keys = jax.random.split(jax.random.fold_in(key, 17 + height), numbers[height])
        chosen = jax.vmap(lambda node_key: jax.random.permutation(node_key, span)[:RT])(node_keys)
        row_list.append(chosen.astype(jnp.int32))
    return jnp.concatenate(row_list, 0)


def place_ends(values, stream_key, smallest, high):
    longest = values.shape.index(max(values.shape))
    spots = []
    for shift in (0, 1):
        where = [jax.random.randint(jax.random.fold_in(stream_key, axis), (), 0, length) for axis, length in enumerate(values.shape)]
        where[longest] = (where[longest] + shift) % values.shape[longest]
        spots.append(tuple(where))
    return values.at[spots[0]].set(smallest).at[spots[1]].set(high)


def levels(rng, extent, shards, least, largest):
    level = 1.0
    for dim, shards_of in shards:
        steps = jax.random.uniform(jax.random.fold_in(jax.random.fold_in(rng, 6), dim), (shards_of,), jnp.float32, least / len(shards), largest / len(shards))
        level = level * jnp.repeat(jnp.exp(steps), extent[dim] // shards_of).reshape((-1,) + (1,) * (len(extent) - 1 - dim))
    return level


def centred(own_key, extent, scale, most, shards=(), held_as=jnp.bfloat16):
    values = jax.random.normal(own_key, extent, jnp.float32) * scale
    if len(shards) > 0:
        values = levels(own_key, extent, shards, -0.22, 0.18) * values
    return jnp.clip(values, min=-most, max=most).astype(held_as)


def setup_inputs(seed: int = 0) -> dict:
    arg_keys = jax.random.split(jax.random.key(seed), 14)
    return {
        "live_tiles": place_ends(jax.random.randint(arg_keys[0], (NODES_ALL,), NT // 2, NT + 1), jax.random.fold_in(arg_keys[0], 1), NT // 2, NT).astype(jnp.int32),
        "row_tiles": draw_row_tiles(jax.random.fold_in(arg_keys[13], 71), 0),
        "rhs0": centred(arg_keys[2], (R, NODES0 * ORDER), 1.0, 6.0, ((0, 16), (1, 8)), jnp.float32),
        "rhs1": centred(arg_keys[3], (R, NODES1 * ORDER), 1.0, 6.0, ((0, 16), (1, 8)), jnp.float32),
        "rhs2": centred(arg_keys[4], (R, NODES2 * ORDER), 1.0, 6.0, ((0, 16), (1, 8)), jnp.float32),
        "rhs3": centred(arg_keys[5], (R, NODES3 * ORDER), 1.0, 6.0, ((0, 16), (1, 8)), jnp.float32),
        "dinv0": draw_dinv0(jax.random.fold_in(arg_keys[13], 71), 0),
        "dinv1": draw_dinv1(jax.random.fold_in(arg_keys[13], 71), 0),
        "dinv2": draw_dinv2(jax.random.fold_in(arg_keys[13], 71), 0),
        "dinv3": draw_dinv3(jax.random.fold_in(arg_keys[13], 71), 0),
        "off0": centred(arg_keys[10], (NODES0 * RT * B, ORDER), ORDER ** -0.5, 0.125, ((0, 8), (1, 16)), jnp.float32),
        "off1": centred(arg_keys[11], (NODES1 * RT * B, ORDER), ORDER ** -0.5, 0.125, ((0, 8), (1, 16)), jnp.float32),
        "off2": centred(arg_keys[12], (NODES2 * RT * B, ORDER), ORDER ** -0.5, 0.125, ((0, 8), (1, 16)), jnp.float32),
    }


highest = lax.Precision.HIGHEST


def selector(targets, offset):
    return (targets[:, :, None] == offset + jnp.arange(NT, dtype=jnp.int32)[None, None, :]).astype(jnp.float32)


def reference(live_tiles, row_tiles, rhs0, rhs1, rhs2, rhs3, dinv0, dinv1, dinv2, dinv3, off0, off1, off2):
    right_sides = [rhs0, rhs1, rhs2, rhs3]
    inverses = [dinv0, dinv1, dinv2, dinv3]
    off_rows = [off0, off1, off2]
    counts = [NODES0, NODES1, NODES2, NODES3]
    starts = [0, NODES0, NODES0 + NODES1, NODES0 + NODES1 + NODES2]
    updates = [jnp.zeros((counts[height], R, ORDER), jnp.float32) for height in range(LEVELS)]
    solved = []
    row_masks = []
    for height in range(LEVELS):
        number = counts[height]
        live_count = live_tiles[starts[height]:starts[height] + number]
        row_mask = (jnp.arange(ORDER, dtype=jnp.int32)[None, :] < live_count[:, None] * B).astype(jnp.float32)[:, None, :]
        right = right_sides[height].reshape(R, number, ORDER).transpose(1, 0, 2) - updates[height]
        inverse = inverses[height].reshape(number, ORDER, ORDER)
        result = row_mask * jnp.einsum("nrc,nic->nri", row_mask * right, inverse, precision=highest)
        solved.append(result)
        row_masks.append(row_mask)
        if height < LEVELS - 1:
            blocks = off_rows[height].reshape(number, RT, B, ORDER)
            update = jnp.einsum("nrc,ntbc->ntrb", result, blocks, precision=highest)
            targets = row_tiles[starts[height]:starts[height] + number]
            for ancestor in range(height + 1, LEVELS):
                picked = selector(targets, (ancestor - height - 1) * NT)
                contribution = jnp.einsum("ntrb,ntc->nrcb", update, picked, precision=highest).reshape(number, R, ORDER)
                group_size = 2 ** (ancestor - height)
                updates[ancestor] = updates[ancestor] + contribution.reshape(counts[ancestor], group_size, R, ORDER).sum(1)
    finals = [None] * LEVELS
    for height in reversed(range(LEVELS)):
        number = counts[height]
        result = solved[height]
        if height < LEVELS - 1:
            blocks = off_rows[height].reshape(number, RT * B, ORDER)
            targets = row_tiles[starts[height]:starts[height] + number]
            gathered = jnp.zeros((number, R, RT, B), jnp.float32)
            for ancestor in range(height + 1, LEVELS):
                picked = selector(targets, (ancestor - height - 1) * NT)
                ancestor_x = jnp.repeat(finals[ancestor], 2 ** (ancestor - height), axis=0).reshape(number, R, NT, B)
                gathered = gathered + jnp.einsum("nrcb,ntc->nrtb", ancestor_x, picked, precision=highest)
            result = result - jnp.einsum("nrk,nkc->nrc", gathered.reshape(number, R, RT * B), blocks, precision=highest)
        inverse = inverses[height].reshape(number, ORDER, ORDER)
        finals[height] = row_masks[height] * jnp.einsum("nri,nic->nrc", row_masks[height] * result, inverse, precision=highest)
    return (finals[0].transpose(1, 0, 2).reshape(R, NODES0 * ORDER),
            finals[1].transpose(1, 0, 2).reshape(R, NODES1 * ORDER),
            finals[2].transpose(1, 0, 2).reshape(R, NODES2 * ORDER),
            finals[3].transpose(1, 0, 2).reshape(R, NODES3 * ORDER))
```

```python
import functools
import jax
import jax.numpy as jnp
from jax import lax
from jax.experimental import pallas as pl
from jax.experimental.pallas import tpu as pltpu
from jax.sharding import Mesh, PartitionSpec as P

B = 128
ORDER = 2048
NT = 16
f32 = jnp.float32
bf16 = jnp.bfloat16

ZI, YI, CI, X0, X1 = 0, 1, 2, 3, 4
LIVE = 5
TILES = 16


def own_tiles(level):
    return TILES + 16 * level


def partner_tiles(level):
    return TILES + 16 * level + 8


def shift(v, axis, s):
    return lax.ppermute(v, axis, [(i, (i + s) % 4) for i in range(4)])


def flip(v, axis):
    return lax.ppermute(v, axis, [(0, 1), (1, 0)])


def gather4(v, axis):
    return [v] + [shift(v, axis, s) for s in (1, 2, 3)]


def scatter4(parts, axis):
    return [parts[0]] + [shift(parts[s], axis, -s) for s in (1, 2, 3)]


def ring(v, axis, dim):
    h = v.shape[dim] // 2
    a = shift(v, axis, 1)
    b = shift(v, axis, -1)
    c = shift(lax.slice_in_dim(a, 0, h, axis=dim), axis, 1)
    d = shift(lax.slice_in_dim(b, h, 2 * h, axis=dim), axis, -1)
    return [v, a, b, c, d]


def ordered(mine, other, bit, dim):
    return jnp.where(
        bit == 0, jnp.concatenate([mine, other], dim), jnp.concatenate([other, mine], dim)
    )


def halves(v, bit):
    h = v.shape[0] // 2
    return (
        jnp.where(bit == 0, v[:h], v[h:]),
        jnp.where(bit == 0, v[h:], v[:h]),
    )


def stacked(v):
    hi = v.astype(bf16).astype(f32)
    return jnp.concatenate([hi, v - hi], 0).astype(bf16)


def product(left, w, dims):
    hi = w.astype(bf16)
    lo = (w - hi.astype(f32)).astype(bf16)
    r = lax.dot_general(left, hi, (dims, ((), ())), preferred_element_type=f32)
    r = r + lax.dot_general(left, lo, (dims, ((), ())), preferred_element_type=f32)
    n = left.shape[0] // 2
    return r[:n] + r[n:]


NTD = ((1,), (1,))
NND = ((1,), (0,))


def copies_first(meta, e, f, ev, fv, sems):
    zi = meta[ZI]
    out_e, out_f = [], []
    spots = [zi, lax.rem(zi + 3, 4), lax.rem(zi + 1, 4)]
    far = lax.rem(zi + 2, 4)
    k = 0

    def tile(t):
        return pl.ds(pl.multiple_of(t * B, B), B)

    for ref, w in zip(e[:3], spots):
        for s in range(4):
            out_e.append(pltpu.make_async_copy(ref.at[s], ev.at[:, tile(w * 4 + s)], sems.at[k]))
            k += 1
    for ref, base in ((e[3], 0), (e[4], 2)):
        for s in range(2):
            out_e.append(
                pltpu.make_async_copy(ref.at[s], ev.at[:, tile(far * 4 + base + s)], sems.at[k])
            )
            k += 1
    for ref, w in zip(f[:3], spots):
        out_f.append(pltpu.make_async_copy(ref, fv.at[:, tile(w)], sems.at[k]))
        k += 1
    for ref, base in ((f[3], 0), (f[4], 512)):
        out_f.append(pltpu.make_async_copy(ref, fv.at[pl.ds(base, 512), tile(far)], sems.at[k]))
        k += 1
    return out_e, out_f


def copies_upper(meta, bufs, ev, fv, sems):
    ci = meta[CI]
    out_e, out_f = [], []
    k = 0
    for ref, q in ((bufs[0], ci), (bufs[1], 1 - ci)):
        rows = pl.ds(pl.multiple_of(q * 256, 256), 256)
        for w in range(4):
            for s in range(4):
                out_e.append(
                    pltpu.make_async_copy(
                        ref.at[w, pl.ds(s * 256, 256)],
                        ev.at[rows, pl.ds((4 * s + w) * B, B)],
                        sems.at[k],
                    )
                )
                k += 1
    if fv is not None:
        for ref, q in ((bufs[0], ci), (bufs[1], 1 - ci)):
            rows = pl.ds(pl.multiple_of(q * 512, 512), 512)
            for w in range(4):
                out_f.append(
                    pltpu.make_async_copy(
                        ref.at[w, pl.ds(1024, 512)], fv.at[rows, pl.ds(w * B, B)], sems.at[k]
                    )
                )
                k += 1
    return out_e, out_f


def column_mask(meta, level, n):
    col = lax.broadcasted_iota(jnp.int32, (n, ORDER), 1)
    return col < meta[LIVE + level] * B


def row_mask(meta, level, n):
    own = lax.broadcasted_iota(jnp.int32, (n, 512), 1) // B
    tile = 4 * own + meta[YI] if level == 0 else 4 * meta[ZI] + own
    return tile < meta[LIVE + level]


def solve_rows(ev, cs, put):
    def body(j, carry):
        rows = pl.ds(pl.multiple_of(j * 256, 256), 256)
        put(rows, product(cs, ev[rows, :], NTD))
        return carry

    lax.fori_loop(0, 2, body, 0)


def forward_kernel(level, n, mode, meta, *refs):
    count = 10 if level == 0 else 2
    c_refs, refs = refs[:4], refs[4:]
    w_refs, refs = refs[:count], refs[count:]
    if mode == "rs":
        y_out, u_out = refs[:2]
        refs = refs[2:]
    else:
        y_out, keep_out, give_out = refs[:3]
        refs = refs[3:]
    ev, fv, cv, yv, uv, sems = refs
    if level == 0:
        ce, cf = copies_first(meta, w_refs[:5], w_refs[5:], ev, fv, sems)
    else:
        ce, cf = copies_upper(meta, w_refs, ev, fv, sems)
    for c in ce + cf:
        c.start()
    r = n // 4
    if level < 2:
        for s in range(4):
            cv[pl.ds(s * r, r), :] = c_refs[s][...]
        c = cv[...]
    else:
        c = summed(c_refs, r)
    c = jnp.where(column_mask(meta, level, n), c, 0.0)
    cs = stacked(c)
    for c in ce:
        c.wait()
    mask = row_mask(meta, level, n)

    def put_y(rows, v):
        yv[:, rows] = v

    solve_rows(ev, cs, put_y)
    y = jnp.where(mask, yv[...], 0.0)
    y_out[...] = y
    ys = stacked(y)
    for c in cf:
        c.wait()

    def body(j, carry):
        rows = pl.ds(pl.multiple_of(j * 256, 256), 256)
        uv[:, rows] = product(ys, fv[rows, :], NTD)
        return carry

    lax.fori_loop(0, 4, body, 0)
    if mode == "rs":
        for s in range(4):
            u_out[s] = uv[pl.ds(s * r, r), :]
    else:
        split_rows(uv, r, meta[X0] if level == 1 else meta[X1], keep_out, give_out)


def split_rows(v, r, bit, keep_out, give_out):
    h = r // 2
    for s in range(4):
        low = v[pl.ds(s * r, h), :]
        high = v[pl.ds(s * r + h, h), :]
        keep_out[pl.ds(s * h, h), :] = jnp.where(bit == 0, low, high)
        give_out[pl.ds(s * h, h), :] = jnp.where(bit == 0, high, low)


def summed(refs, r):
    parts = []
    for s in range(4):
        total = refs[0][pl.ds(s * r, r), :]
        for d in (1, 2, 3):
            total = total + refs[d][pl.ds((s - d) % 4 * r, r), :]
        parts.append(total)
    return jnp.concatenate(parts, 0)


def add_tiles(meta, at, src, acc):
    for t in range(8):
        v = meta[at + t]
        cols = pl.ds(pl.multiple_of(lax.rem(v, NT) * B, B), B)
        lev = lax.div(v, NT)
        acc[lev, :, cols] = acc[lev, :, cols] + src[:, t * B : (t + 1) * B]


def take_tiles(meta, at, anc, dst):
    for t in range(8):
        v = meta[at + t]
        cols = pl.ds(pl.multiple_of(lax.rem(v, NT) * B, B), B)
        dst[:, t * B : (t + 1) * B] = anc[lax.div(v, NT), :, cols]


def s01_kernel(meta, keep, recv, b1, c1, pk, pg, acc):
    acc[...] = jnp.zeros_like(acc)
    add_tiles(meta, own_tiles(0), keep, acc)
    add_tiles(meta, partner_tiles(0), recv, acc)
    c1[...] = b1[...] - acc[0]
    for i in (0, 1):
        low, high = acc[i + 1, 0:4, :], acc[i + 1, 4:8, :]
        pk[i] = jnp.where(meta[X0] == 0, low, high)
        pg[i] = jnp.where(meta[X0] == 0, high, low)


def s12_kernel(meta, keep, recv, b2, pk, pr, part, keep3, give3, acc):
    acc[...] = jnp.zeros_like(acc)
    add_tiles(meta, own_tiles(1), keep, acc)
    add_tiles(meta, partner_tiles(1), recv, acc)
    part[...] = -acc[0]
    part[0:4, :] = part[0:4, :] + (b2[...] - (pk[0] + pr[0]))
    acc[1, 0:4, :] = acc[1, 0:4, :] + (pk[1] + pr[1])
    split_rows(acc.at[1], 4, meta[X1], keep3, give3)


def s23_kernel(meta, keep, recv, b3, keep3, recv3, part, acc):
    acc[...] = jnp.zeros_like(acc)
    add_tiles(meta, own_tiles(2), keep, acc)
    add_tiles(meta, partner_tiles(2), recv, acc)
    part[...] = -(acc[0] + (keep3[...] + recv3[...]))
    part[0:2, :] = part[0:2, :] + b3[...]


def top_kernel(meta, c0, c1, c2, c3, wa, wb, x_out, ev, yv, sems):
    ce, _ = copies_upper(meta, (wa, wb), ev, None, sems)
    for c in ce:
        c.start()
    c = summed((c0, c1, c2, c3), 2)
    keep = column_mask(meta, 3, 8)
    cs = stacked(jnp.where(keep, c, 0.0))
    for c in ce:
        c.wait()

    def put_y(rows, v):
        yv[:, rows] = v

    solve_rows(ev, cs, put_y)
    y = jnp.where(row_mask(meta, 3, 8), yv[...], 0.0)
    back(meta, 3, 8, ev, y, x_out)


def back(meta, level, n, ev, z, x_out):
    zs = stacked(z)
    live = meta[LIVE + level] * B

    def body(j, carry):
        cols = pl.ds(pl.multiple_of(j * 512, 512), 512)
        v = product(zs, ev[:, cols], NND)
        col = lax.broadcasted_iota(jnp.int32, (n, 512), 1) + j * 512
        x_out[:, cols] = jnp.where(col < live, v, 0.0)
        return carry

    lax.fori_loop(0, 4, body, 0)


def x3_kernel(meta, c0, c1, c2, c3, x_out, give, anc):
    x = summed((c0, c1, c2, c3), 2)
    x_out[...] = x
    anc[0] = x
    take_tiles(meta, partner_tiles(2), anc, give)


def merged(a, b, h, bit):
    parts = []
    for s in range(4):
        u, v = a[s * h : (s + 1) * h, :], b[s * h : (s + 1) * h, :]
        parts += [jnp.where(bit == 0, u, v), jnp.where(bit == 0, v, u)]
    return jnp.concatenate(parts, 0)


def x2_kernel(meta, c0, c1, c2, c3, x3, x3r, anc_out, give):
    anc_out[0] = summed((c0, c1, c2, c3), 4)
    anc_out[1] = merged(x3[...], x3r[...], 2, meta[X1])
    take_tiles(meta, partner_tiles(1), anc_out, give)


def x1_kernel(meta, c0, c1, c2, c3, a_mine, a_other, anc_out, give, own):
    anc_out[0] = (c0[...] + c1[...]) + (c2[...] + c3[...])
    for i in (0, 1):
        u, v = a_mine[i], a_other[i]
        bit = meta[X0]
        anc_out[i + 1, 0:4, :] = jnp.where(bit == 0, u, v)
        anc_out[i + 1, 4:8, :] = jnp.where(bit == 0, v, u)
    take_tiles(meta, partner_tiles(0), anc_out, give)
    take_tiles(meta, own_tiles(0), anc_out, own)


def backward_kernel(level, n, meta, *refs):
    count = 10 if level == 0 else 2
    if level == 0:
        g_refs, refs = refs[:4], refs[4:]
    else:
        (anc, recv), refs = refs[:2], refs[2:]
    y_ref, refs = refs[0], refs[1:]
    w_refs, refs = refs[:count], refs[count:]
    x_out, ev, fv, gv, ov, sems = refs
    if level == 0:
        ce, cf = copies_first(meta, w_refs[:5], w_refs[5:], ev, fv, sems)
    else:
        ce, cf = copies_upper(meta, w_refs, ev, fv, sems)
    for c in cf + ce:
        c.start()
    r = n // 4
    if level == 0:
        for s in range(4):
            gv[pl.ds(s * r, r), :] = g_refs[s][...]
        g = gv[...]
    else:
        take_tiles(meta, own_tiles(level), anc, ov)
        bit = meta[X0] if level == 1 else meta[X1]
        g = merged(ov[...], recv[...], r // 2, bit)
    gs = stacked(g)
    for c in cf:
        c.wait()
    z = y_ref[...] - product(gs, fv[...], NND)
    z = jnp.where(row_mask(meta, level, n), z, 0.0)
    for c in ce:
        c.wait()
    back(meta, level, n, ev, z, x_out)


SMEM = pl.BlockSpec(memory_space=pltpu.SMEM)
VMEM = pl.BlockSpec(memory_space=pltpu.VMEM)
ANY = pl.BlockSpec(memory_space=pl.ANY)


def call(kernel, name, shapes, scratch, meta, small, weights=(), flops=0):
    moved = sum(w.size * 4 for w in weights) + sum(v.size * 4 for v in small)
    return pl.pallas_call(
        kernel,
        out_shape=[jax.ShapeDtypeStruct(s, f32) for s in shapes],
        in_specs=[SMEM] + [VMEM] * len(small) + [ANY] * len(weights),
        out_specs=[VMEM] * len(shapes),
        scratch_shapes=scratch,
        compiler_params=pltpu.CompilerParams(vmem_limit_bytes=24 * 2**20),
        cost_estimate=pl.CostEstimate(flops=flops, bytes_accessed=moved, transcendentals=0),
        name=name,
    )(meta, *small, *weights)


def local(
    live_tiles, row_tiles, rhs0, rhs1, rhs2, rhs3, dinv0, dinv1, dinv2, dinv3, off0, off1, off2
):
    zi, yi = lax.axis_index("z"), lax.axis_index("y")
    ci, x0, x1 = lax.axis_index("core"), lax.axis_index("x0"), lax.axis_index("x1")
    leaf = x1 * 4 + x0 * 2 + ci
    first = [0, 8, 12, 14]
    nodes = [first[k] + leaf // 2**k for k in range(4)]
    partners = [first[k] + (leaf // 2**k ^ 1) for k in range(3)]
    lives = [live_tiles[n] for n in nodes]
    tables = []
    for k in range(3):
        tables += [row_tiles[nodes[k]], row_tiles[partners[k]]]
    head = jnp.stack([zi, yi, ci, x0, x1, *lives] + [jnp.int32(0)] * 7).astype(jnp.int32)
    meta = jnp.concatenate([head, *tables])

    e0 = jnp.swapaxes(dinv0.reshape(4, 4, B, B), 0, 1).reshape(4, 512, B)
    f0 = ring(off0, "z", 0)
    e0 = lax.all_to_all(e0, "y", 0, 0, tiled=True)
    e0 = ring(e0, "z", 0)
    w0 = e0 + f0

    def upper(dinv, off, bits):
        e, f = dinv, off
        for axis, bit in bits:
            e = ordered(e, flip(e, axis), bit, 0)
            if f is not None:
                f = ordered(f, flip(f, axis), bit, 0)
        e = lax.dynamic_index_in_dim(e.reshape(4, 2, 256, B), ci, 1, keepdims=False)
        e = lax.all_to_all(e, "z", 0, 0, tiled=True).reshape(1024, B)
        if f is not None:
            e = jnp.concatenate([e, lax.dynamic_slice_in_dim(f, ci * 512, 512)], 0)
        mine = lax.all_gather(e, "y", axis=0, tiled=False)
        return mine, flip(mine, "core")

    bits = [("core", ci), ("x0", x0), ("x1", x1)]
    w1 = upper(dinv1, off1, bits[:1])
    w2 = upper(dinv2, off2, bits[:2])
    w3 = upper(dinv3, None, bits)

    def spread(rhs, levels):
        v = rhs
        for axis, bit in bits[:levels]:
            keep, give = halves(v, bit)
            v = ordered(keep, flip(give, axis), bit, 1)
        return v

    b1, b2, b3 = spread(rhs1, 1), spread(rhs2, 2), spread(rhs3, 3)

    dma = pltpu.SemaphoreType.DMA
    ev, fv = pltpu.VMEM((512, ORDER), f32), pltpu.VMEM((1024, 512), f32)

    def work(n):
        return [pltpu.VMEM((n, ORDER), f32), pltpu.VMEM((n, 512), f32), pltpu.VMEM((n, 1024), f32)]

    def flops(n):
        return 2 * n * 512 * (2048 + 1024) * 12

    y0, u = call(
        functools.partial(forward_kernel, 0, 64, "rs"), "f0", [(64, 512), (4, 16, 1024)],
        [ev, fv, *work(64), dma((24,))], meta, gather4(rhs0, "y"), w0, flops(64),
    )
    parts = scatter4([u[s] for s in range(4)], "y")
    u = (parts[0] + parts[1]) + (parts[2] + parts[3])
    keep, give = halves(u, ci)
    c1, pk, pg = call(
        s01_kernel, "s01", [(8, ORDER), (2, 4, ORDER), (2, 4, ORDER)],
        [pltpu.VMEM((3, 8, ORDER), f32)], meta, [keep, flip(give, "core"), b1],
    )
    pr = flip(pg, "x0")
    y1, keep, give = call(
        functools.partial(forward_kernel, 1, 32, "ar"), "f1", [(32, 512), (16, 1024), (16, 1024)],
        [ev, fv, *work(32), dma((40,))], meta, gather4(c1, "z"), w1, flops(32),
    )
    part, keep3, give3 = call(
        s12_kernel, "s12", [(16, ORDER), (8, ORDER), (8, ORDER)],
        [pltpu.VMEM((2, 16, ORDER), f32)], meta, [keep, flip(give, "x0"), b2, pk, pr],
    )
    recv3 = flip(give3, "x1")
    y2, keep, give = call(
        functools.partial(forward_kernel, 2, 16, "ar"), "f2", [(16, 512), (8, 1024), (8, 1024)],
        [ev, fv, *work(16), dma((40,))], meta, gather4(part, "z"), w2, flops(16),
    )
    (part,) = call(
        s23_kernel, "s23", [(8, ORDER)],
        [pltpu.VMEM((1, 8, ORDER), f32)], meta, [keep, flip(give, "x1"), b3, keep3, recv3],
    )

    (part,) = call(
        top_kernel, "top", [(8, ORDER)], [ev, pltpu.VMEM((8, 512), f32), dma((32,))],
        meta, gather4(part, "z"), w3, flops(8),
    )
    x3, give = call(
        x3_kernel, "x3", [(8, ORDER), (8, 1024)], [pltpu.VMEM((1, 8, ORDER), f32)],
        meta, gather4(part, "z"),
    )
    recv = flip(give, "x1")
    x3r = flip(x3, "x1")

    def rest(n, small):
        return [ev, fv, pltpu.VMEM((n, 1024), f32), pltpu.VMEM((n // 2, 1024), f32), dma((40,))]

    (part,) = call(
        functools.partial(backward_kernel, 2, 16), "b2", [(16, ORDER)], rest(16, 0),
        meta, [x3[None], recv, y2], w2, flops(16),
    )
    anc, give = call(
        x2_kernel, "x2", [(2, 16, ORDER), (16, 1024)], [],
        meta, gather4(part, "z") + [x3, x3r],
    )
    recv = flip(give, "x0")
    a_mine = anc[:, :4]
    a_other = flip(a_mine, "x0")
    (part,) = call(
        functools.partial(backward_kernel, 1, 32), "b1", [(32, ORDER)], rest(32, 0),
        meta, [anc, recv, y1], w1, flops(32),
    )
    anc, give, own = call(
        x1_kernel, "x1", [(3, 8, ORDER), (8, 1024), (8, 1024)], [],
        meta, scatter4([part[8 * s : 8 * s + 8] for s in range(4)], "z") + [a_mine, a_other],
    )
    g = ordered(own, flip(give, "core"), ci, 0)
    (part,) = call(
        functools.partial(backward_kernel, 0, 64), "b0", [(64, ORDER)], rest(64, 0),
        meta, gather4(g, "y") + [y0], w0, flops(64),
    )
    parts = scatter4([part[16 * s : 16 * s + 16] for s in range(4)], "y")
    sol0 = (parts[0] + parts[1]) + (parts[2] + parts[3])

    outs = [sol0]
    for k in (1, 2, 3):
        width = ORDER // 2**k
        place = leaf % 2**k
        mine = lax.dynamic_slice_in_dim(anc[k - 1], place * width, width, 1)
        give = lax.dynamic_slice_in_dim(anc[k - 1], (place ^ 1) * width, width, 1)
        outs.append(ordered(mine, flip(give, "core"), ci, 0))
    return tuple(outs)


def solution(mesh):
    fine = Mesh(mesh.devices.reshape(2, 2, 2, 4, 4), ("x1", "x0", "core", "z", "y"))
    leaf, panel = ("x1", "x0", "core"), ("z", "y")
    return jax.shard_map(
        local,
        mesh=fine,
        in_specs=(P(), P()) + (P(panel, leaf),) * 4 + (P(leaf, panel),) * 7,
        out_specs=(P(panel, leaf),) * 4,
        check_vma=False,
    )
```

```python
import functools
import jax
import jax.numpy as jnp
from jax import lax
from jax.experimental import pallas as pl
from jax.experimental.pallas import tpu as pltpu
from jax.sharding import Mesh, PartitionSpec as P

B = 128
ORDER = 2048
NT = 16
f32 = jnp.float32
bf16 = jnp.bfloat16

ZI, YI, CI, X0, X1 = 0, 1, 2, 3, 4
LIVE = 5
TILES = 16


def own_tiles(level):
    return TILES + 16 * level


def partner_tiles(level):
    return TILES + 16 * level + 8


def shift(v, axis, s):
    return lax.ppermute(v, axis, [(i, (i + s) % 4) for i in range(4)])


def flip(v, axis):
    return lax.ppermute(v, axis, [(0, 1), (1, 0)])


def gather4(v, axis):
    return [v] + [shift(v, axis, s) for s in (1, 2, 3)]


def scatter4(parts, axis):
    return [parts[0]] + [shift(parts[s], axis, -s) for s in (1, 2, 3)]


def ring(v, axis, dim):
    h = v.shape[dim] // 2
    a = shift(v, axis, 1)
    b = shift(v, axis, -1)
    c = shift(lax.slice_in_dim(a, 0, h, axis=dim), axis, 1)
    d = shift(lax.slice_in_dim(b, h, 2 * h, axis=dim), axis, -1)
    return [v, a, b, c, d]


def ordered(mine, other, bit, dim):
    return jnp.where(
        bit == 0, jnp.concatenate([mine, other], dim), jnp.concatenate([other, mine], dim)
    )


def halves(v, bit):
    h = v.shape[0] // 2
    return (
        jnp.where(bit == 0, v[:h], v[h:]),
        jnp.where(bit == 0, v[h:], v[:h]),
    )


def stacked(v):
    hi = v.astype(bf16).astype(f32)
    return jnp.concatenate([hi, v - hi], 0).astype(bf16)


def product(left, w, dims):
    hi = w.astype(bf16)
    lo = (w - hi.astype(f32)).astype(bf16)
    r = lax.dot_general(left, hi, (dims, ((), ())), preferred_element_type=f32)
    r = r + lax.dot_general(left, lo, (dims, ((), ())), preferred_element_type=f32)
    n = left.shape[0] // 2
    return r[:n] + r[n:]


NTD = ((1,), (1,))
NND = ((1,), (0,))


def copies_first(meta, e, f, ev, fv, sems):
    zi = meta[ZI]
    out_e, out_f = [], []
    spots = [zi, lax.rem(zi + 3, 4), lax.rem(zi + 1, 4)]
    far = lax.rem(zi + 2, 4)
    k = 0

    def tile(t):
        return pl.ds(pl.multiple_of(t * B, B), B)

    for ref, w in zip(e[:3], spots):
        for s in range(4):
            out_e.append(pltpu.make_async_copy(ref.at[s], ev.at[:, tile(w * 4 + s)], sems.at[k]))
            k += 1
    for ref, base in ((e[3], 0), (e[4], 2)):
        for s in range(2):
            out_e.append(
                pltpu.make_async_copy(ref.at[s], ev.at[:, tile(far * 4 + base + s)], sems.at[k])
            )
            k += 1
    for ref, w in zip(f[:3], spots):
        out_f.append(pltpu.make_async_copy(ref, fv.at[:, tile(w)], sems.at[k]))
        k += 1
    for ref, base in ((f[3], 0), (f[4], 512)):
        out_f.append(pltpu.make_async_copy(ref, fv.at[pl.ds(base, 512), tile(far)], sems.at[k]))
        k += 1
    return out_e, out_f


def copies_upper(meta, bufs, ev, fv, sems):
    ci, yi = meta[CI], meta[YI]
    sources = []
    for i, q in ((0, ci), (1, 1 - ci)):
        if len(bufs) == 2:
            sources += [(bufs[i].at[w], q, w) for w in range(4)]
        else:
            sources += [(bufs[4 * i + d], q, lax.rem(yi + 4 - d, 4)) for d in range(4)]
    out_e, out_f = [], []
    k = 0
    for ref, q, w in sources:
        rows = pl.ds(pl.multiple_of(q * 256, 256), 256)
        for s in range(4):
            cols = pl.ds(pl.multiple_of((4 * s + w) * B, B), B)
            out_e.append(
                pltpu.make_async_copy(ref.at[pl.ds(s * 256, 256)], ev.at[rows, cols], sems.at[k])
            )
            k += 1
    if fv is not None:
        for ref, q, w in sources:
            rows = pl.ds(pl.multiple_of(q * 512, 512), 512)
            cols = pl.ds(pl.multiple_of(w * B, B), B)
            out_f.append(
                pltpu.make_async_copy(ref.at[pl.ds(1024, 512)], fv.at[rows, cols], sems.at[k])
            )
            k += 1
    return out_e, out_f


def column_mask(meta, level, n):
    col = lax.broadcasted_iota(jnp.int32, (n, ORDER), 1)
    return col < meta[LIVE + level] * B


def row_mask(meta, level, n):
    own = lax.broadcasted_iota(jnp.int32, (n, 512), 1) // B
    tile = 4 * own + meta[YI] if level == 0 else 4 * meta[ZI] + own
    return tile < meta[LIVE + level]


def solve_rows(ev, cs, put):
    def body(j, carry):
        rows = pl.ds(pl.multiple_of(j * 256, 256), 256)
        put(rows, product(cs, ev[rows, :], NTD))
        return carry

    lax.fori_loop(0, 2, body, 0)


WEIGHTS = (10, 2, 8, 2)


def forward_kernel(level, n, mode, meta, *refs):
    count = WEIGHTS[level]
    c_refs, refs = refs[:4], refs[4:]
    w_refs, refs = refs[:count], refs[count:]
    if mode == "rs":
        y_out, u_out = refs[0], refs[1:5]
        refs = refs[5:]
    else:
        y_out, keep_out, give_out = refs[:3]
        refs = refs[3:]
    ev, fv, cv, yv, uv, sems = refs
    if level == 0:
        ce, cf = copies_first(meta, w_refs[:5], w_refs[5:], ev, fv, sems)
    else:
        ce, cf = copies_upper(meta, w_refs, ev, fv, sems)
    for c in ce + cf:
        c.start()
    r = n // 4
    if level < 2:
        for s in range(4):
            cv[pl.ds(s * r, r), :] = c_refs[s][...]
        c = cv[...]
    else:
        c = summed(c_refs, r)
    c = jnp.where(column_mask(meta, level, n), c, 0.0)
    cs = stacked(c)
    for c in ce:
        c.wait()
    mask = row_mask(meta, level, n)

    def put_y(rows, v):
        yv[:, rows] = v

    solve_rows(ev, cs, put_y)
    y = jnp.where(mask, yv[...], 0.0)
    y_out[...] = y
    ys = stacked(y)
    for c in cf:
        c.wait()

    def body(j, carry):
        rows = pl.ds(pl.multiple_of(j * 256, 256), 256)
        uv[:, rows] = product(ys, fv[rows, :], NTD)
        return carry

    lax.fori_loop(0, 4, body, 0)
    if mode == "rs":
        for s in range(4):
            u_out[s][...] = uv[pl.ds(s * r, r), :]
    else:
        split_rows(uv, r, meta[X0] if level == 1 else meta[X1], keep_out, give_out)


def split_rows(v, r, bit, keep_out, give_out):
    h = r // 2
    for s in range(4):
        low = v[pl.ds(s * r, h), :]
        high = v[pl.ds(s * r + h, h), :]
        keep_out[pl.ds(s * h, h), :] = jnp.where(bit == 0, low, high)
        give_out[pl.ds(s * h, h), :] = jnp.where(bit == 0, high, low)


def summed(refs, r):
    parts = []
    for s in range(4):
        total = refs[0][pl.ds(s * r, r), :]
        for d in (1, 2, 3):
            total = total + refs[d][pl.ds((s - d) % 4 * r, r), :]
        parts.append(total)
    return jnp.concatenate(parts, 0)


def add_tiles(meta, at, src, acc):
    for t in range(8):
        v = meta[at + t]
        cols = pl.ds(pl.multiple_of(lax.rem(v, NT) * B, B), B)
        lev = lax.div(v, NT)
        acc[lev, :, cols] = acc[lev, :, cols] + src[:, t * B : (t + 1) * B]


def take_tiles(meta, at, anc, dst):
    for t in range(8):
        v = meta[at + t]
        cols = pl.ds(pl.multiple_of(lax.rem(v, NT) * B, B), B)
        dst[:, t * B : (t + 1) * B] = anc[lax.div(v, NT), :, cols]


def s01_kernel(meta, keep, recv, b1, c1, pk, pg, acc):
    acc[...] = jnp.zeros_like(acc)
    add_tiles(meta, own_tiles(0), keep, acc)
    add_tiles(meta, partner_tiles(0), recv, acc)
    c1[...] = b1[...] - acc[0]
    for i in (0, 1):
        low, high = acc[i + 1, 0:4, :], acc[i + 1, 4:8, :]
        pk[i] = jnp.where(meta[X0] == 0, low, high)
        pg[i] = jnp.where(meta[X0] == 0, high, low)


def s12_kernel(meta, keep, recv, b2, pk, pr, part, keep3, give3, acc):
    acc[...] = jnp.zeros_like(acc)
    add_tiles(meta, own_tiles(1), keep, acc)
    add_tiles(meta, partner_tiles(1), recv, acc)
    part[...] = -acc[0]
    part[0:4, :] = part[0:4, :] + (b2[...] - (pk[0] + pr[0]))
    acc[1, 0:4, :] = acc[1, 0:4, :] + (pk[1] + pr[1])
    split_rows(acc.at[1], 4, meta[X1], keep3, give3)


def s23_kernel(meta, keep, recv, b3, keep3, recv3, part, acc):
    acc[...] = jnp.zeros_like(acc)
    add_tiles(meta, own_tiles(2), keep, acc)
    add_tiles(meta, partner_tiles(2), recv, acc)
    part[...] = -(acc[0] + (keep3[...] + recv3[...]))
    part[0:2, :] = part[0:2, :] + b3[...]


def top_kernel(meta, c0, c1, c2, c3, wa, wb, x_out, ev, yv, sems):
    ce, _ = copies_upper(meta, (wa, wb), ev, None, sems)
    for c in ce:
        c.start()
    c = summed((c0, c1, c2, c3), 2)
    keep = column_mask(meta, 3, 8)
    cs = stacked(jnp.where(keep, c, 0.0))
    for c in ce:
        c.wait()

    def put_y(rows, v):
        yv[:, rows] = v

    solve_rows(ev, cs, put_y)
    y = jnp.where(row_mask(meta, 3, 8), yv[...], 0.0)
    back(meta, 3, 8, ev, y, [x_out])


def back(meta, level, n, ev, z, x_out):
    zs = stacked(z)
    live = meta[LIVE + level] * B

    def body(j, carry):
        cols = pl.ds(pl.multiple_of(j * 512, 512), 512)
        v = product(zs, ev[:, cols], NND)
        col = lax.broadcasted_iota(jnp.int32, (n, 512), 1) + j * 512
        v = jnp.where(col < live, v, 0.0)
        r = n // len(x_out)
        for s, out in enumerate(x_out):
            out[:, cols] = v[s * r : (s + 1) * r]
        return carry

    lax.fori_loop(0, 4, body, 0)


def x3_kernel(meta, c0, c1, c2, c3, x_out, give, anc):
    x = summed((c0, c1, c2, c3), 2)
    x_out[...] = x
    anc[0] = x
    take_tiles(meta, partner_tiles(2), anc, give)


def merged(a, b, h, bit):
    parts = []
    for s in range(4):
        u, v = a[s * h : (s + 1) * h, :], b[s * h : (s + 1) * h, :]
        parts += [jnp.where(bit == 0, u, v), jnp.where(bit == 0, v, u)]
    return jnp.concatenate(parts, 0)


def x2_kernel(meta, c0, c1, c2, c3, x3, x3r, anc_out, give):
    anc_out[0] = summed((c0, c1, c2, c3), 4)
    anc_out[1] = merged(x3[...], x3r[...], 2, meta[X1])
    take_tiles(meta, partner_tiles(1), anc_out, give)


def x1_kernel(meta, c0, c1, c2, c3, a_mine, a_other, anc_out, give, own):
    anc_out[0] = (c0[...] + c1[...]) + (c2[...] + c3[...])
    for i in (0, 1):
        u, v = a_mine[i], a_other[i]
        bit = meta[X0]
        anc_out[i + 1, 0:4, :] = jnp.where(bit == 0, u, v)
        anc_out[i + 1, 4:8, :] = jnp.where(bit == 0, v, u)
    take_tiles(meta, partner_tiles(0), anc_out, give)
    take_tiles(meta, own_tiles(0), anc_out, own)


def backward_kernel(level, n, meta, *refs):
    count = WEIGHTS[level]
    if level == 0:
        g_refs, refs = refs[:4], refs[4:]
    else:
        (anc, recv), refs = refs[:2], refs[2:]
    y_ref, refs = refs[0], refs[1:]
    w_refs, refs = refs[:count], refs[count:]
    x_out, (ev, fv, gv, ov, sems) = refs[:-5], refs[-5:]
    if level == 0:
        ce, cf = copies_first(meta, w_refs[:5], w_refs[5:], ev, fv, sems)
    else:
        ce, cf = copies_upper(meta, w_refs, ev, fv, sems)
    for c in cf + ce:
        c.start()
    r = n // 4
    if level == 0:
        for s in range(4):
            gv[pl.ds(s * r, r), :] = g_refs[s][...]
        g = gv[...]
    else:
        take_tiles(meta, own_tiles(level), anc, ov)
        bit = meta[X0] if level == 1 else meta[X1]
        g = merged(ov[...], recv[...], r // 2, bit)
    gs = stacked(g)
    for c in cf:
        c.wait()
    z = y_ref[...] - product(gs, fv[...], NND)
    z = jnp.where(row_mask(meta, level, n), z, 0.0)
    for c in ce:
        c.wait()
    back(meta, level, n, ev, z, x_out)


SMEM = pl.BlockSpec(memory_space=pltpu.SMEM)
VMEM = pl.BlockSpec(memory_space=pltpu.VMEM)
ANY = pl.BlockSpec(memory_space=pl.ANY)


def call(kernel, name, shapes, scratch, meta, small, weights=(), flops=0):
    if name != "f0":
        weights = [pltpu.with_memory_space_constraint(w, pltpu.HBM) for w in weights]
    moved = sum(w.size * 4 for w in weights) + sum(v.size * 4 for v in small)
    return pl.pallas_call(
        kernel,
        out_shape=[jax.ShapeDtypeStruct(s, f32) for s in shapes],
        in_specs=[SMEM] + [VMEM] * len(small) + [ANY] * len(weights),
        out_specs=[VMEM] * len(shapes),
        scratch_shapes=scratch,
        compiler_params=pltpu.CompilerParams(vmem_limit_bytes=(14 if flops else 3) * 2**20),
        cost_estimate=pl.CostEstimate(flops=flops, bytes_accessed=moved, transcendentals=0),
        name=name,
    )(meta, *small, *weights)


def local(
    live_tiles, row_tiles, rhs0, rhs1, rhs2, rhs3, dinv0, dinv1, dinv2, dinv3, off0, off1, off2
):
    zi, yi = lax.axis_index("z"), lax.axis_index("y")
    ci, x0, x1 = lax.axis_index("core"), lax.axis_index("x0"), lax.axis_index("x1")
    leaf = x1 * 4 + x0 * 2 + ci
    first = [0, 8, 12, 14]
    nodes = [first[k] + leaf // 2**k for k in range(4)]
    partners = [first[k] + (leaf // 2**k ^ 1) for k in range(3)]
    lives = [live_tiles[n] for n in nodes]
    tables = []
    for k in range(3):
        tables += [row_tiles[nodes[k]], row_tiles[partners[k]]]
    head = jnp.stack([zi, yi, ci, x0, x1, *lives] + [jnp.int32(0)] * 7).astype(jnp.int32)
    meta = jnp.concatenate([head, *tables])

    e0 = jnp.swapaxes(dinv0.reshape(4, 4, B, B), 0, 1).reshape(4, 512, B)
    f0 = ring(off0, "z", 0)
    e0 = lax.all_to_all(e0, "y", 0, 0, tiled=True)

    bits = [("core", ci), ("x0", x0), ("x1", x1)]

    def grouped(v, levels):
        for axis, bit in bits[:levels]:
            v = ordered(v, flip(v, axis), bit, 0)
        return v

    def half_block(e, levels):
        e = grouped(e, levels)
        return lax.dynamic_index_in_dim(e.reshape(4, 2, 256, B), ci, 1, keepdims=False)

    def packed(e, f, levels):
        e = e.reshape(1024, B)
        if f is None:
            return e
        return jnp.concatenate([e, lax.dynamic_slice_in_dim(grouped(f, levels), ci * 512, 512)], 0)

    def gathered(e):
        mine = lax.all_gather(e, "y", axis=0, tiled=False)
        return mine, flip(mine, "core")

    e1 = half_block(dinv1, 1)
    e0, e1 = lax.optimization_barrier((e0, e1))
    e0 = ring(e0, "z", 0)
    e1 = lax.all_to_all(e1, "z", 0, 0, tiled=True)
    w0 = e0 + f0
    w1 = gathered(packed(e1, off1, 1))
    near, e1, dinv2, off2, dinv3, rhs1, rhs2, rhs3 = lax.optimization_barrier(
        (e0[1], e1, dinv2, off2, dinv3, rhs1, rhs2, rhs3)
    )
    e2 = lax.all_to_all(half_block(dinv2, 2), "z", 0, 0, tiled=True)
    pieces = gather4(packed(e2, off2, 2), "y")
    w2 = pieces + [flip(v, "core") for v in pieces]
    e3 = half_block(dinv3, 3)
    e2, e3 = lax.optimization_barrier((e2, e3))
    w3 = gathered(packed(lax.all_to_all(e3, "z", 0, 0, tiled=True), None, 3))

    def spread(rhs, levels):
        v = rhs
        for axis, bit in bits[:levels]:
            keep, give = halves(v, bit)
            v = ordered(keep, flip(give, axis), bit, 1)
        return v

    b1, b2, b3 = spread(rhs1, 1), spread(rhs2, 2), spread(rhs3, 3)

    dma = pltpu.SemaphoreType.DMA
    ev, fv = pltpu.VMEM((512, ORDER), f32), pltpu.VMEM((1024, 512), f32)

    def work(n):
        return [pltpu.VMEM((n, ORDER), f32), pltpu.VMEM((n, 512), f32), pltpu.VMEM((n, 1024), f32)]

    def flops(n):
        return 2 * n * 512 * (2048 + 1024) * 12

    y0, *u = call(
        functools.partial(forward_kernel, 0, 64, "rs"), "f0", [(64, 512)] + [(16, 1024)] * 4,
        [ev, fv, *work(64), dma((24,))], meta, gather4(rhs0, "y"), w0, flops(64),
    )
    parts = scatter4(u, "y")
    u = (parts[0] + parts[1]) + (parts[2] + parts[3])
    keep, give = halves(u, ci)
    c1, pk, pg = call(
        s01_kernel, "s01", [(8, ORDER), (2, 4, ORDER), (2, 4, ORDER)],
        [pltpu.VMEM((3, 8, ORDER), f32)], meta, [keep, flip(give, "core"), b1],
    )
    pr = flip(pg, "x0")
    y1, keep, give = call(
        functools.partial(forward_kernel, 1, 32, "ar"), "f1", [(32, 512), (16, 1024), (16, 1024)],
        [ev, fv, *work(32), dma((40,))], meta, gather4(c1, "z"), w1, flops(32),
    )
    part, keep3, give3 = call(
        s12_kernel, "s12", [(16, ORDER), (8, ORDER), (8, ORDER)],
        [pltpu.VMEM((2, 16, ORDER), f32)], meta, [keep, flip(give, "x0"), b2, pk, pr],
    )
    recv3 = flip(give3, "x1")
    y2, keep, give = call(
        functools.partial(forward_kernel, 2, 16, "ar"), "f2", [(16, 512), (8, 1024), (8, 1024)],
        [ev, fv, *work(16), dma((40,))], meta, gather4(part, "z"), w2, flops(16),
    )
    (part,) = call(
        s23_kernel, "s23", [(8, ORDER)],
        [pltpu.VMEM((1, 8, ORDER), f32)], meta, [keep, flip(give, "x1"), b3, keep3, recv3],
    )

    (part,) = call(
        top_kernel, "top", [(8, ORDER)], [ev, pltpu.VMEM((8, 512), f32), dma((32,))],
        meta, gather4(part, "z"), w3, flops(8),
    )
    x3, give = call(
        x3_kernel, "x3", [(8, ORDER), (8, 1024)], [pltpu.VMEM((1, 8, ORDER), f32)],
        meta, gather4(part, "z"),
    )
    recv = flip(give, "x1")
    x3r = flip(x3, "x1")

    def rest(n, small):
        return [ev, fv, pltpu.VMEM((n, 1024), f32), pltpu.VMEM((n // 2, 1024), f32), dma((40,))]

    (part,) = call(
        functools.partial(backward_kernel, 2, 16), "b2", [(16, ORDER)], rest(16, 0),
        meta, [x3[None], recv, y2], w2, flops(16),
    )
    anc, give = call(
        x2_kernel, "x2", [(2, 16, ORDER), (16, 1024)], [],
        meta, gather4(part, "z") + [x3, x3r],
    )
    recv = flip(give, "x0")
    a_mine = anc[:, :4]
    a_other = flip(a_mine, "x0")
    parts = call(
        functools.partial(backward_kernel, 1, 32), "b1", [(8, ORDER)] * 4, rest(32, 0),
        meta, [anc, recv, y1], w1, flops(32),
    )
    anc, give, own = call(
        x1_kernel, "x1", [(3, 8, ORDER), (8, 1024), (8, 1024)], [],
        meta, scatter4(parts, "z") + [a_mine, a_other],
    )
    g = ordered(own, flip(give, "core"), ci, 0)
    parts = call(
        functools.partial(backward_kernel, 0, 64), "b0", [(16, ORDER)] * 4, rest(64, 0),
        meta, gather4(g, "y") + [y0], w0, flops(64),
    )
    parts = scatter4(parts, "y")
    sol0 = (parts[0] + parts[1]) + (parts[2] + parts[3])

    outs = [sol0]
    for k in (1, 2, 3):
        width = ORDER // 2**k
        place = leaf % 2**k
        mine = lax.dynamic_slice_in_dim(anc[k - 1], place * width, width, 1)
        give = lax.dynamic_slice_in_dim(anc[k - 1], (place ^ 1) * width, width, 1)
        outs.append(ordered(mine, flip(give, "core"), ci, 0))
    return tuple(outs)


def solution(mesh):
    fine = Mesh(mesh.devices.reshape(2, 2, 2, 4, 4), ("x1", "x0", "core", "z", "y"))
    leaf, panel = ("x1", "x0", "core"), ("z", "y")
    return jax.shard_map(
        local,
        mesh=fine,
        in_specs=(P(), P()) + (P(panel, leaf),) * 4 + (P(leaf, panel),) * 7,
        out_specs=(P(panel, leaf),) * 4,
        check_vma=False,
    )
```

```python
import functools
import jax
import jax.numpy as jnp
from jax import lax
from jax.experimental import pallas as pl
from jax.experimental.pallas import tpu as pltpu
from jax.sharding import Mesh, PartitionSpec as P

B = 128
ORDER = 2048
NT = 16
f32 = jnp.float32
bf16 = jnp.bfloat16

ZI, YI, CI, X0, X1 = 0, 1, 2, 3, 4
LIVE = 5
TILES = 16


def own_tiles(level):
    return TILES + 16 * level


def partner_tiles(level):
    return TILES + 16 * level + 8


def shift(v, axis, s):
    return lax.ppermute(v, axis, [(i, (i + s) % 4) for i in range(4)])


def flip(v, axis):
    return lax.ppermute(v, axis, [(0, 1), (1, 0)])


def gather4(v, axis):
    return [v] + [shift(v, axis, s) for s in (1, 2, 3)]


def scatter4(parts, axis):
    return [parts[0]] + [shift(parts[s], axis, -s) for s in (1, 2, 3)]


def ring(v, axis, dim):
    h = v.shape[dim] // 2
    a = shift(v, axis, 1)
    b = shift(v, axis, -1)
    c = shift(lax.slice_in_dim(a, 0, h, axis=dim), axis, 1)
    d = shift(lax.slice_in_dim(b, h, 2 * h, axis=dim), axis, -1)
    return [v, a, b, c, d]


def ordered(mine, other, bit, dim):
    return jnp.where(
        bit == 0, jnp.concatenate([mine, other], dim), jnp.concatenate([other, mine], dim)
    )


def halves(v, bit):
    h = v.shape[0] // 2
    return (
        jnp.where(bit == 0, v[:h], v[h:]),
        jnp.where(bit == 0, v[h:], v[:h]),
    )


def stacked(v):
    hi = v.astype(bf16).astype(f32)
    return jnp.concatenate([hi, v - hi], 0).astype(bf16)


def product(left, w, dims):
    hi = w.astype(bf16)
    lo = (w - hi.astype(f32)).astype(bf16)
    r = lax.dot_general(left, hi, (dims, ((), ())), preferred_element_type=f32)
    r = r + lax.dot_general(left, lo, (dims, ((), ())), preferred_element_type=f32)
    n = left.shape[0] // 2
    return r[:n] + r[n:]


NTD = ((1,), (1,))
NND = ((1,), (0,))


def copies_first(meta, e, f, ev, fv, sems):
    zi = meta[ZI]
    out_e, out_f = [], []
    spots = [zi, lax.rem(zi + 3, 4), lax.rem(zi + 1, 4)]
    far = lax.rem(zi + 2, 4)
    k = 0

    def tile(t):
        return pl.ds(pl.multiple_of(t * B, B), B)

    for ref, w in zip(e[:3], spots):
        for s in range(4):
            out_e.append(pltpu.make_async_copy(ref.at[s], ev.at[:, tile(w * 4 + s)], sems.at[k]))
            k += 1
    for ref, base in ((e[3], 0), (e[4], 2)):
        for s in range(2):
            out_e.append(
                pltpu.make_async_copy(ref.at[s], ev.at[:, tile(far * 4 + base + s)], sems.at[k])
            )
            k += 1
    for ref, w in zip(f[:3], spots):
        out_f.append(pltpu.make_async_copy(ref, fv.at[:, tile(w)], sems.at[k]))
        k += 1
    for ref, base in ((f[3], 0), (f[4], 512)):
        out_f.append(pltpu.make_async_copy(ref, fv.at[pl.ds(base, 512), tile(far)], sems.at[k]))
        k += 1
    return out_e, out_f


def copies_upper(meta, bufs, ev, fv, sems):
    ci, yi = meta[CI], meta[YI]
    sources = []
    for i, q in ((0, ci), (1, 1 - ci)):
        if len(bufs) == 2:
            sources += [(bufs[i].at[w], q, w) for w in range(4)]
        else:
            sources += [(bufs[4 * i + d], q, lax.rem(yi + 4 - d, 4)) for d in range(4)]
    out_e, out_f = [], []
    k = 0
    for ref, q, w in sources:
        rows = pl.ds(pl.multiple_of(q * 256, 256), 256)
        for s in range(4):
            cols = pl.ds(pl.multiple_of((4 * s + w) * B, B), B)
            out_e.append(
                pltpu.make_async_copy(ref.at[pl.ds(s * 256, 256)], ev.at[rows, cols], sems.at[k])
            )
            k += 1
    if fv is not None:
        for ref, q, w in sources:
            rows = pl.ds(pl.multiple_of(q * 512, 512), 512)
            cols = pl.ds(pl.multiple_of(w * B, B), B)
            out_f.append(
                pltpu.make_async_copy(ref.at[pl.ds(1024, 512)], fv.at[rows, cols], sems.at[k])
            )
            k += 1
    return out_e, out_f


def column_mask(meta, level, n):
    col = lax.broadcasted_iota(jnp.int32, (n, ORDER), 1)
    return col < meta[LIVE + level] * B


def row_mask(meta, level, n):
    own = lax.broadcasted_iota(jnp.int32, (n, 512), 1) // B
    tile = 4 * own + meta[YI] if level == 0 else 4 * meta[ZI] + own
    return tile < meta[LIVE + level]


def solve_rows(ev, cs, put):
    def body(j, carry):
        rows = pl.ds(pl.multiple_of(j * 256, 256), 256)
        put(rows, product(cs, ev[rows, :], NTD))
        return carry

    lax.fori_loop(0, 2, body, 0)


WEIGHTS = (10, 2, 2, 8)


def forward_kernel(level, n, mode, meta, *refs):
    count = WEIGHTS[level]
    c_refs, refs = refs[:4], refs[4:]
    w_refs, refs = refs[:count], refs[count:]
    if mode == "rs":
        y_out, u_out = refs[0], refs[1:5]
        refs = refs[5:]
    else:
        y_out, keep_out, give_out = refs[:3]
        refs = refs[3:]
    ev, fv, cv, yv, uv, sems = refs
    if level == 0:
        ce, cf = copies_first(meta, w_refs[:5], w_refs[5:], ev, fv, sems)
    else:
        ce, cf = copies_upper(meta, w_refs, ev, fv, sems)
    for c in ce + cf:
        c.start()
    r = n // 4
    if level < 2:
        for s in range(4):
            cv[pl.ds(s * r, r), :] = c_refs[s][...]
        c = cv[...]
    else:
        c = summed(c_refs, r)
    c = jnp.where(column_mask(meta, level, n), c, 0.0)
    cs = stacked(c)
    for c in ce:
        c.wait()
    mask = row_mask(meta, level, n)

    def put_y(rows, v):
        yv[:, rows] = v

    solve_rows(ev, cs, put_y)
    y = jnp.where(mask, yv[...], 0.0)
    y_out[...] = y
    ys = stacked(y)
    for c in cf:
        c.wait()

    def body(j, carry):
        rows = pl.ds(pl.multiple_of(j * 256, 256), 256)
        uv[:, rows] = product(ys, fv[rows, :], NTD)
        return carry

    lax.fori_loop(0, 4, body, 0)
    if mode == "rs":
        for s in range(4):
            u_out[s][...] = uv[pl.ds(s * r, r), :]
    else:
        split_rows(uv, r, meta[X0] if level == 1 else meta[X1], keep_out, give_out)


def split_rows(v, r, bit, keep_out, give_out):
    h = r // 2
    for s in range(4):
        low = v[pl.ds(s * r, h), :]
        high = v[pl.ds(s * r + h, h), :]
        keep_out[pl.ds(s * h, h), :] = jnp.where(bit == 0, low, high)
        give_out[pl.ds(s * h, h), :] = jnp.where(bit == 0, high, low)


def summed(refs, r):
    parts = []
    for s in range(4):
        total = refs[0][pl.ds(s * r, r), :]
        for d in (1, 2, 3):
            total = total + refs[d][pl.ds((s - d) % 4 * r, r), :]
        parts.append(total)
    return jnp.concatenate(parts, 0)


def add_tiles(meta, at, src, acc):
    for t in range(8):
        v = meta[at + t]
        cols = pl.ds(pl.multiple_of(lax.rem(v, NT) * B, B), B)
        lev = lax.div(v, NT)
        acc[lev, :, cols] = acc[lev, :, cols] + src[:, t * B : (t + 1) * B]


def take_tiles(meta, at, anc, dst):
    for t in range(8):
        v = meta[at + t]
        cols = pl.ds(pl.multiple_of(lax.rem(v, NT) * B, B), B)
        dst[:, t * B : (t + 1) * B] = anc[lax.div(v, NT), :, cols]


def s01_kernel(meta, keep, recv, b1, c1, pk, pg, acc):
    acc[...] = jnp.zeros_like(acc)
    add_tiles(meta, own_tiles(0), keep, acc)
    add_tiles(meta, partner_tiles(0), recv, acc)
    c1[...] = b1[...] - acc[0]
    for i in (0, 1):
        low, high = acc[i + 1, 0:4, :], acc[i + 1, 4:8, :]
        pk[i] = jnp.where(meta[X0] == 0, low, high)
        pg[i] = jnp.where(meta[X0] == 0, high, low)


def s12_kernel(meta, keep, recv, b2, pk, pr, part, keep3, give3, acc):
    acc[...] = jnp.zeros_like(acc)
    add_tiles(meta, own_tiles(1), keep, acc)
    add_tiles(meta, partner_tiles(1), recv, acc)
    part[...] = -acc[0]
    part[0:4, :] = part[0:4, :] + (b2[...] - (pk[0] + pr[0]))
    acc[1, 0:4, :] = acc[1, 0:4, :] + (pk[1] + pr[1])
    split_rows(acc.at[1], 4, meta[X1], keep3, give3)


def s23_kernel(meta, keep, recv, b3, keep3, recv3, part, acc):
    acc[...] = jnp.zeros_like(acc)
    add_tiles(meta, own_tiles(2), keep, acc)
    add_tiles(meta, partner_tiles(2), recv, acc)
    part[...] = -(acc[0] + (keep3[...] + recv3[...]))
    part[0:2, :] = part[0:2, :] + b3[...]


def top_kernel(meta, c0, c1, c2, c3, *refs):
    w_refs, (x_out, ev, yv, sems) = refs[:8], refs[8:]
    ce, _ = copies_upper(meta, w_refs, ev, None, sems)
    for c in ce:
        c.start()
    c = summed((c0, c1, c2, c3), 2)
    keep = column_mask(meta, 3, 8)
    cs = stacked(jnp.where(keep, c, 0.0))
    for c in ce:
        c.wait()

    def put_y(rows, v):
        yv[:, rows] = v

    solve_rows(ev, cs, put_y)
    y = jnp.where(row_mask(meta, 3, 8), yv[...], 0.0)
    back(meta, 3, 8, ev, y, [x_out])


def back(meta, level, n, ev, z, x_out):
    zs = stacked(z)
    live = meta[LIVE + level] * B

    def body(j, carry):
        cols = pl.ds(pl.multiple_of(j * 512, 512), 512)
        v = product(zs, ev[:, cols], NND)
        col = lax.broadcasted_iota(jnp.int32, (n, 512), 1) + j * 512
        v = jnp.where(col < live, v, 0.0)
        r = n // len(x_out)
        for s, out in enumerate(x_out):
            out[:, cols] = v[s * r : (s + 1) * r]
        return carry

    lax.fori_loop(0, 4, body, 0)


def x3_kernel(meta, c0, c1, c2, c3, x_out, give, anc):
    x = summed((c0, c1, c2, c3), 2)
    x_out[...] = x
    anc[0] = x
    take_tiles(meta, partner_tiles(2), anc, give)


def merged(a, b, h, bit):
    parts = []
    for s in range(4):
        u, v = a[s * h : (s + 1) * h, :], b[s * h : (s + 1) * h, :]
        parts += [jnp.where(bit == 0, u, v), jnp.where(bit == 0, v, u)]
    return jnp.concatenate(parts, 0)


def x2_kernel(meta, c0, c1, c2, c3, x3, x3r, anc_out, give):
    anc_out[0] = summed((c0, c1, c2, c3), 4)
    anc_out[1] = merged(x3[...], x3r[...], 2, meta[X1])
    take_tiles(meta, partner_tiles(1), anc_out, give)


def x1_kernel(meta, c0, c1, c2, c3, a_mine, a_other, anc_out, give, own):
    anc_out[0] = (c0[...] + c1[...]) + (c2[...] + c3[...])
    for i in (0, 1):
        u, v = a_mine[i], a_other[i]
        bit = meta[X0]
        anc_out[i + 1, 0:4, :] = jnp.where(bit == 0, u, v)
        anc_out[i + 1, 4:8, :] = jnp.where(bit == 0, v, u)
    take_tiles(meta, partner_tiles(0), anc_out, give)
    take_tiles(meta, own_tiles(0), anc_out, own)


def backward_kernel(level, n, meta, *refs):
    count = WEIGHTS[level]
    if level == 0:
        g_refs, refs = refs[:4], refs[4:]
    else:
        (anc, recv), refs = refs[:2], refs[2:]
    y_ref, refs = refs[0], refs[1:]
    w_refs, refs = refs[:count], refs[count:]
    x_out, (ev, fv, gv, ov, sems) = refs[:-5], refs[-5:]
    if level == 0:
        ce, cf = copies_first(meta, w_refs[:5], w_refs[5:], ev, fv, sems)
    else:
        ce, cf = copies_upper(meta, w_refs, ev, fv, sems)
    for c in cf + ce:
        c.start()
    r = n // 4
    if level == 0:
        for s in range(4):
            gv[pl.ds(s * r, r), :] = g_refs[s][...]
        g = gv[...]
    else:
        take_tiles(meta, own_tiles(level), anc, ov)
        bit = meta[X0] if level == 1 else meta[X1]
        g = merged(ov[...], recv[...], r // 2, bit)
    gs = stacked(g)
    for c in cf:
        c.wait()
    z = y_ref[...] - product(gs, fv[...], NND)
    z = jnp.where(row_mask(meta, level, n), z, 0.0)
    for c in ce:
        c.wait()
    back(meta, level, n, ev, z, x_out)


SMEM = pl.BlockSpec(memory_space=pltpu.SMEM)
VMEM = pl.BlockSpec(memory_space=pltpu.VMEM)
ANY = pl.BlockSpec(memory_space=pl.ANY)


def call(kernel, name, shapes, scratch, meta, small, weights=(), flops=0):
    if name != "f0":
        weights = [pltpu.with_memory_space_constraint(w, pltpu.HBM) for w in weights]
    moved = sum(w.size * 4 for w in weights) + sum(v.size * 4 for v in small)
    return pl.pallas_call(
        kernel,
        out_shape=[jax.ShapeDtypeStruct(s, f32) for s in shapes],
        in_specs=[SMEM] + [VMEM] * len(small) + [ANY] * len(weights),
        out_specs=[VMEM] * len(shapes),
        scratch_shapes=scratch,
        compiler_params=pltpu.CompilerParams(vmem_limit_bytes=(14 if flops else 3) * 2**20),
        cost_estimate=pl.CostEstimate(flops=flops, bytes_accessed=moved, transcendentals=0),
        name=name,
    )(meta, *small, *weights)


def local(
    live_tiles, row_tiles, rhs0, rhs1, rhs2, rhs3, dinv0, dinv1, dinv2, dinv3, off0, off1, off2
):
    zi, yi = lax.axis_index("z"), lax.axis_index("y")
    ci, x0, x1 = lax.axis_index("core"), lax.axis_index("x0"), lax.axis_index("x1")
    leaf = x1 * 4 + x0 * 2 + ci
    first = [0, 8, 12, 14]
    nodes = [first[k] + leaf // 2**k for k in range(4)]
    partners = [first[k] + (leaf // 2**k ^ 1) for k in range(3)]
    lives = [live_tiles[n] for n in nodes]
    tables = []
    for k in range(3):
        tables += [row_tiles[nodes[k]], row_tiles[partners[k]]]
    head = jnp.stack([zi, yi, ci, x0, x1, *lives] + [jnp.int32(0)] * 7).astype(jnp.int32)
    meta = jnp.concatenate([head, *tables])

    bits = [("core", ci), ("x0", x0), ("x1", x1)]

    def joined(v, i):
        axis, bit = bits[i]
        return None if v is None else ordered(v, flip(v, axis), bit, 0)

    def half_block(e):
        return lax.dynamic_index_in_dim(e.reshape(4, 2, 256, B), ci, 1, keepdims=False)

    def half_rows(f):
        return lax.dynamic_slice_in_dim(f, ci * 512, 512)

    def rows_to_z(e):
        return lax.all_to_all(e, "z", 0, 0, tiled=True).reshape(1024, B)

    def gathered(e, f):
        return lax.all_gather(jnp.concatenate([e, f], 0), "y", axis=0, tiled=False)

    def spread(v, i):
        axis, bit = bits[i]
        keep, give = halves(v, bit)
        return ordered(keep, flip(give, axis), bit, 1)

    gate = lax.optimization_barrier
    e0 = jnp.swapaxes(dinv0.reshape(4, 4, B, B), 0, 1).reshape(4, 512, B)
    e0 = lax.all_to_all(e0, "y", 0, 0, tiled=True)
    fa, fb = shift(off0, "z", 1), shift(off0, "z", -1)
    e1 = rows_to_z(half_block(joined(dinv1, 0)))
    f1 = half_rows(joined(off1, 0))
    e2, f2 = joined(dinv2, 0), joined(off2, 0)
    e3 = joined(joined(joined(dinv3, 2), 1), 0).reshape(2, 2, 2, 256, B)
    e3 = half_block(e3.transpose(2, 1, 0, 3, 4))
    e0, fa, fb, e1, f1, e2, f2, e3 = gate((e0, fa, fb, e1, f1, e2, f2, e3))
    m1 = gathered(e1, f1)

    ea, eb = shift(e0, "z", 1), shift(e0, "z", -1)
    fc, fd = shift(fa[:512], "z", 1), shift(fb[512:], "z", -1)
    e2, f2 = half_block(joined(e2, 1)), half_rows(joined(f2, 1))
    e3 = rows_to_z(e3)
    b1, b2, b3 = spread(rhs1, 0), spread(rhs2, 0), spread(rhs3, 0)
    ea, eb, fc, fd, e2, f2, e3, b1, b2, b3 = gate((ea, eb, fc, fd, e2, f2, e3, b1, b2, b3))

    ec, ed = shift(ea[:2], "z", 1), shift(eb[2:], "z", -1)
    e2 = rows_to_z(e2)
    w3 = gather4(e3, "y")
    b2, b3 = spread(b2, 1), spread(b3, 1)
    c0 = gather4(rhs0, "y")
    ec, ed, e2, b2, b3, c0, w3 = gate((ec, ed, e2, b2, b3, c0, w3))
    w0 = [e0, ea, eb, ec, ed, off0, fa, fb, fc, fd]
    m2 = gathered(e2, f2)
    b3 = spread(b3, 2)
    w3 = w3 + [flip(v, "core") for v in w3]

    dma = pltpu.SemaphoreType.DMA
    ev, fv = pltpu.VMEM((512, ORDER), f32), pltpu.VMEM((1024, 512), f32)

    def work(n):
        return [pltpu.VMEM((n, ORDER), f32), pltpu.VMEM((n, 512), f32), pltpu.VMEM((n, 1024), f32)]

    def flops(n):
        return 2 * n * 512 * (2048 + 1024) * 12

    y0, *u = call(
        functools.partial(forward_kernel, 0, 64, "rs"), "f0", [(64, 512)] + [(16, 1024)] * 4,
        [ev, fv, *work(64), dma((24,))], meta, c0, w0, flops(64),
    )
    m1, _ = gate((m1, y0))
    w1 = m1, flip(m1, "core")
    parts = scatter4(u, "y")
    u = (parts[0] + parts[1]) + (parts[2] + parts[3])
    keep, give = halves(u, ci)
    c1, pk, pg = call(
        s01_kernel, "s01", [(8, ORDER), (2, 4, ORDER), (2, 4, ORDER)],
        [pltpu.VMEM((3, 8, ORDER), f32)], meta, [keep, flip(give, "core"), b1],
    )
    pr = flip(pg, "x0")
    y1, keep, give = call(
        functools.partial(forward_kernel, 1, 32, "ar"), "f1", [(32, 512), (16, 1024), (16, 1024)],
        [ev, fv, *work(32), dma((40,))], meta, gather4(c1, "z"), w1, flops(32),
    )
    part, keep3, give3 = call(
        s12_kernel, "s12", [(16, ORDER), (8, ORDER), (8, ORDER)],
        [pltpu.VMEM((2, 16, ORDER), f32)], meta, [keep, flip(give, "x0"), b2, pk, pr],
    )
    m2, _ = gate((m2, part))
    w2 = m2, flip(m2, "core")
    recv3 = flip(give3, "x1")
    y2, keep, give = call(
        functools.partial(forward_kernel, 2, 16, "ar"), "f2", [(16, 512), (8, 1024), (8, 1024)],
        [ev, fv, *work(16), dma((40,))], meta, gather4(part, "z"), w2, flops(16),
    )
    (part,) = call(
        s23_kernel, "s23", [(8, ORDER)],
        [pltpu.VMEM((1, 8, ORDER), f32)], meta, [keep, flip(give, "x1"), b3, keep3, recv3],
    )

    (part,) = call(
        top_kernel, "top", [(8, ORDER)], [ev, pltpu.VMEM((8, 512), f32), dma((32,))],
        meta, gather4(part, "z"), w3, flops(8),
    )
    x3, give = call(
        x3_kernel, "x3", [(8, ORDER), (8, 1024)], [pltpu.VMEM((1, 8, ORDER), f32)],
        meta, gather4(part, "z"),
    )
    recv = flip(give, "x1")
    x3r = flip(x3, "x1")

    def rest(n, small):
        return [ev, fv, pltpu.VMEM((n, 1024), f32), pltpu.VMEM((n // 2, 1024), f32), dma((40,))]

    (part,) = call(
        functools.partial(backward_kernel, 2, 16), "b2", [(16, ORDER)], rest(16, 0),
        meta, [x3[None], recv, y2], w2, flops(16),
    )
    anc, give = call(
        x2_kernel, "x2", [(2, 16, ORDER), (16, 1024)], [],
        meta, gather4(part, "z") + [x3, x3r],
    )
    recv = flip(give, "x0")
    a_mine = anc[:, :4]
    a_other = flip(a_mine, "x0")
    parts = call(
        functools.partial(backward_kernel, 1, 32), "b1", [(8, ORDER)] * 4, rest(32, 0),
        meta, [anc, recv, y1], w1, flops(32),
    )
    anc, give, own = call(
        x1_kernel, "x1", [(3, 8, ORDER), (8, 1024), (8, 1024)], [],
        meta, scatter4(parts, "z") + [a_mine, a_other],
    )
    g = ordered(own, flip(give, "core"), ci, 0)
    parts = call(
        functools.partial(backward_kernel, 0, 64), "b0", [(16, ORDER)] * 4, rest(64, 0),
        meta, gather4(g, "y") + [y0], w0, flops(64),
    )
    parts = scatter4(parts, "y")
    sol0 = (parts[0] + parts[1]) + (parts[2] + parts[3])

    outs = [sol0]
    for k in (1, 2, 3):
        width = ORDER // 2**k
        place = leaf % 2**k
        mine = lax.dynamic_slice_in_dim(anc[k - 1], place * width, width, 1)
        give = lax.dynamic_slice_in_dim(anc[k - 1], (place ^ 1) * width, width, 1)
        outs.append(ordered(mine, flip(give, "core"), ci, 0))
    return tuple(outs)


def solution(mesh):
    fine = Mesh(mesh.devices.reshape(2, 2, 2, 4, 4), ("x1", "x0", "core", "z", "y"))
    leaf, panel = ("x1", "x0", "core"), ("z", "y")
    return jax.shard_map(
        local,
        mesh=fine,
        in_specs=(P(), P()) + (P(panel, leaf),) * 4 + (P(leaf, panel),) * 7,
        out_specs=(P(panel, leaf),) * 4,
        check_vma=False,
    )
```

```python
import functools
import jax
import jax.numpy as jnp
from jax import lax
from jax.experimental import pallas as pl
from jax.experimental.pallas import tpu as pltpu
from jax.sharding import Mesh, PartitionSpec as P

B = 128
ORDER = 2048
NT = 16
f32 = jnp.float32
bf16 = jnp.bfloat16

FIRST = (0, 8, 12, 14)


class Place:
    def __init__(self, meta):
        self.meta = meta
        self.leaf = meta[0] >> 4
        self.zi, self.yi = (meta[0] >> 2) & 3, meta[0] & 3
        self.ci, self.x0, self.x1 = self.leaf & 1, (self.leaf >> 1) & 1, self.leaf >> 2

    def live(self, level):
        return self.meta[1 + FIRST[level] + (self.leaf >> level)]

    def own(self, level):
        return 16 + 8 * (FIRST[level] + (self.leaf >> level))

    def partner(self, level):
        return 16 + 8 * (FIRST[level] + ((self.leaf >> level) ^ 1))

    def bit(self, level):
        return (self.ci, self.x0, self.x1)[level]


def shift(v, axis, s):
    return lax.ppermute(v, axis, [(i, (i + s) % 4) for i in range(4)])


def flip(v, axis):
    return lax.ppermute(v, axis, [(0, 1), (1, 0)])


def gather4(v, axis):
    return [v] + [shift(v, axis, s) for s in (1, 2, 3)]


def scatter4(parts, axis):
    return [parts[0]] + [shift(parts[s], axis, -s) for s in (1, 2, 3)]


def ring(v, axis, dim):
    h = v.shape[dim] // 2
    a = shift(v, axis, 1)
    b = shift(v, axis, -1)
    c = shift(lax.slice_in_dim(a, 0, h, axis=dim), axis, 1)
    d = shift(lax.slice_in_dim(b, h, 2 * h, axis=dim), axis, -1)
    return [v, a, b, c, d]


def ordered(mine, other, bit, dim):
    return jnp.where(
        bit == 0, jnp.concatenate([mine, other], dim), jnp.concatenate([other, mine], dim)
    )


def halves(v, bit):
    h = v.shape[0] // 2
    return (
        jnp.where(bit == 0, v[:h], v[h:]),
        jnp.where(bit == 0, v[h:], v[:h]),
    )


def stacked(v):
    hi = v.astype(bf16).astype(f32)
    return jnp.concatenate([hi, v - hi], 0).astype(bf16)


def product(left, w, dims):
    hi = w.astype(bf16)
    lo = (w - hi.astype(f32)).astype(bf16)
    r = lax.dot_general(left, hi, (dims, ((), ())), preferred_element_type=f32)
    r = r + lax.dot_general(left, lo, (dims, ((), ())), preferred_element_type=f32)
    n = left.shape[0] // 2
    return r[:n] + r[n:]


NTD = ((1,), (1,))
NND = ((1,), (0,))


def copies_first(meta, e, f, ev, fv, sems):
    zi = Place(meta).zi
    out_e, out_f = [], []
    spots = [zi, lax.rem(zi + 3, 4), lax.rem(zi + 1, 4)]
    far = lax.rem(zi + 2, 4)
    k = 0

    def tile(t):
        return pl.ds(pl.multiple_of(t * B, B), B)

    for ref, w in zip(e[:3], spots):
        for s in range(4):
            out_e.append(pltpu.make_async_copy(ref.at[s], ev.at[:, tile(w * 4 + s)], sems.at[k]))
            k += 1
    for ref, base in ((e[3], 0), (e[4], 2)):
        for s in range(2):
            out_e.append(
                pltpu.make_async_copy(ref.at[s], ev.at[:, tile(far * 4 + base + s)], sems.at[k])
            )
            k += 1
    for ref, w in zip(f[:3], spots):
        out_f.append(pltpu.make_async_copy(ref, fv.at[:, tile(w)], sems.at[k]))
        k += 1
    for ref, base in ((f[3], 0), (f[4], 512)):
        out_f.append(pltpu.make_async_copy(ref, fv.at[pl.ds(base, 512), tile(far)], sems.at[k]))
        k += 1
    return out_e, out_f


def copies_upper(level, meta, bufs, ev, fv, sems):
    ci = Place(meta).ci
    sources = [(bufs[i].at[w], q, w) for i, q in ((0, ci), (1, 1 - ci)) for w in range(4)]
    out_e, out_f = [], []
    k = 0
    for ref, q, w in sources:
        rows = pl.ds(pl.multiple_of(q * 256, 256), 256)
        for s in range(4):
            cols = pl.ds(pl.multiple_of((4 * s + w) * B, B), B)
            out_e.append(
                pltpu.make_async_copy(ref.at[pl.ds(s * 256, 256)], ev.at[rows, cols], sems.at[k])
            )
            k += 1
    if fv is not None:
        for ref, q, w in sources:
            for h in range(level):
                n = 512 // level
                rows = pl.ds(pl.multiple_of(h * 512 + q * n, n), n)
                cols = pl.ds(pl.multiple_of(w * B, B), B)
                out_f.append(
                    pltpu.make_async_copy(
                        ref.at[pl.ds(1024 + h * n, n)], fv.at[rows, cols], sems.at[k]
                    )
                )
                k += 1
    return out_e, out_f


def column_mask(meta, level, n):
    col = lax.broadcasted_iota(jnp.int32, (n, ORDER), 1)
    return col < Place(meta).live(level) * B


def row_mask(meta, level, n):
    own = lax.broadcasted_iota(jnp.int32, (n, 512), 1) // B
    place = Place(meta)
    tile = 4 * own + place.yi if level == 0 else 4 * place.zi + own
    return tile < Place(meta).live(level)


def solve_rows(ev, cs, put):
    def body(j, carry):
        rows = pl.ds(pl.multiple_of(j * 256, 256), 256)
        put(rows, product(cs, ev[rows, :], NTD))
        return carry

    lax.fori_loop(0, 2, body, 0)


WEIGHTS = (10, 2, 2, 2)


def forward_kernel(level, n, mode, meta, *refs):
    count = WEIGHTS[level]
    c_refs, refs = refs[:4], refs[4:]
    w_refs, refs = refs[:count], refs[count:]
    if mode == "rs":
        y_out, u_out = refs[0], refs[1:5]
        refs = refs[5:]
    else:
        y_out, keep_out, give_out = refs[:3]
        refs = refs[3:]
    ev, fv, cv, yv, uv, sems = refs
    if level == 0:
        ce, cf = copies_first(meta, w_refs[:5], w_refs[5:], ev, fv, sems)
    else:
        ce, cf = copies_upper(level, meta, w_refs, ev, fv, sems)
    for c in ce + cf:
        c.start()
    r = n // 4
    if level < 2:
        for s in range(4):
            cv[pl.ds(s * r, r), :] = c_refs[s][...]
        c = cv[...]
    else:
        c = summed(c_refs, r)
    c = jnp.where(column_mask(meta, level, n), c, 0.0)
    cs = stacked(c)
    for c in ce:
        c.wait()
    mask = row_mask(meta, level, n)

    def put_y(rows, v):
        yv[:, rows] = v

    solve_rows(ev, cs, put_y)
    y = jnp.where(mask, yv[...], 0.0)
    y_out[...] = y
    ys = stacked(y)
    for c in cf:
        c.wait()

    def body(j, carry):
        rows = pl.ds(pl.multiple_of(j * 256, 256), 256)
        uv[:, rows] = product(ys, fv[rows, :], NTD)
        return carry

    lax.fori_loop(0, 4, body, 0)
    if mode == "rs":
        for s in range(4):
            u_out[s][...] = uv[pl.ds(s * r, r), :]
    else:
        split_rows(uv, r, Place(meta).bit(level), keep_out, give_out)


def split_rows(v, r, bit, keep_out, give_out):
    h = r // 2
    for s in range(4):
        low = v[pl.ds(s * r, h), :]
        high = v[pl.ds(s * r + h, h), :]
        keep_out[pl.ds(s * h, h), :] = jnp.where(bit == 0, low, high)
        give_out[pl.ds(s * h, h), :] = jnp.where(bit == 0, high, low)


def summed(refs, r):
    parts = []
    for s in range(4):
        total = refs[0][pl.ds(s * r, r), :]
        for d in (1, 2, 3):
            total = total + refs[d][pl.ds((s - d) % 4 * r, r), :]
        parts.append(total)
    return jnp.concatenate(parts, 0)


def add_tiles(meta, at, src, acc):
    for t in range(8):
        v = meta[at + t]
        cols = pl.ds(pl.multiple_of(lax.rem(v, NT) * B, B), B)
        lev = lax.div(v, NT)
        acc[lev, :, cols] = acc[lev, :, cols] + src[:, t * B : (t + 1) * B]


def take_tiles(meta, at, anc, dst):
    for t in range(8):
        v = meta[at + t]
        cols = pl.ds(pl.multiple_of(lax.rem(v, NT) * B, B), B)
        dst[:, t * B : (t + 1) * B] = anc[lax.div(v, NT), :, cols]


def s01_kernel(meta, keep, recv, b1, c1, pk, pg, acc):
    acc[...] = jnp.zeros_like(acc)
    add_tiles(meta, Place(meta).own(0), keep, acc)
    add_tiles(meta, Place(meta).partner(0), recv, acc)
    c1[...] = b1[...] - acc[0]
    for i in (0, 1):
        low, high = acc[i + 1, 0:4, :], acc[i + 1, 4:8, :]
        pk[i] = jnp.where(Place(meta).x0 == 0, low, high)
        pg[i] = jnp.where(Place(meta).x0 == 0, high, low)


def s12_kernel(meta, keep, recv, b2, pk, pr, part, keep3, give3, acc):
    acc[...] = jnp.zeros_like(acc)
    add_tiles(meta, Place(meta).own(1), keep, acc)
    add_tiles(meta, Place(meta).partner(1), recv, acc)
    part[...] = -acc[0]
    part[0:4, :] = part[0:4, :] + (b2[...] - (pk[0] + pr[0]))
    acc[1, 0:4, :] = acc[1, 0:4, :] + (pk[1] + pr[1])
    split_rows(acc.at[1], 4, Place(meta).x1, keep3, give3)


def s23_kernel(meta, keep, recv, b3, keep3, recv3, part, acc):
    acc[...] = jnp.zeros_like(acc)
    add_tiles(meta, Place(meta).own(2), keep, acc)
    add_tiles(meta, Place(meta).partner(2), recv, acc)
    part[...] = -(acc[0] + (keep3[...] + recv3[...]))
    part[0:2, :] = part[0:2, :] + b3[...]


def top_kernel(meta, c0, c1, c2, c3, *refs):
    w_refs, (x_out, ev, yv, sems) = refs[:2], refs[2:]
    ce, _ = copies_upper(3, meta, w_refs, ev, None, sems)
    for c in ce:
        c.start()
    c = summed((c0, c1, c2, c3), 2)
    keep = column_mask(meta, 3, 8)
    cs = stacked(jnp.where(keep, c, 0.0))
    for c in ce:
        c.wait()

    def put_y(rows, v):
        yv[:, rows] = v

    solve_rows(ev, cs, put_y)
    y = jnp.where(row_mask(meta, 3, 8), yv[...], 0.0)
    back(meta, 3, 8, ev, y, [x_out])


def back(meta, level, n, ev, z, x_out):
    zs = stacked(z)
    live = Place(meta).live(level) * B

    def body(j, carry):
        cols = pl.ds(pl.multiple_of(j * 512, 512), 512)
        v = product(zs, ev[:, cols], NND)
        col = lax.broadcasted_iota(jnp.int32, (n, 512), 1) + j * 512
        v = jnp.where(col < live, v, 0.0)
        r = n // len(x_out)
        for s, out in enumerate(x_out):
            out[:, cols] = v[s * r : (s + 1) * r]
        return carry

    lax.fori_loop(0, 4, body, 0)


def x3_kernel(meta, c0, c1, c2, c3, x_out, give, anc):
    x = summed((c0, c1, c2, c3), 2)
    x_out[...] = x
    anc[0] = x
    take_tiles(meta, Place(meta).partner(2), anc, give)


def merged(a, b, h, bit):
    parts = []
    for s in range(4):
        u, v = a[s * h : (s + 1) * h, :], b[s * h : (s + 1) * h, :]
        parts += [jnp.where(bit == 0, u, v), jnp.where(bit == 0, v, u)]
    return jnp.concatenate(parts, 0)


def x2_kernel(meta, c0, c1, c2, c3, x3, x3r, anc_out, give):
    anc_out[0] = summed((c0, c1, c2, c3), 4)
    anc_out[1] = merged(x3[...], x3r[...], 2, Place(meta).x1)
    take_tiles(meta, Place(meta).partner(1), anc_out, give)


def x1_kernel(meta, c0, c1, c2, c3, a_mine, a_other, anc_out, give, own):
    anc_out[0] = (c0[...] + c1[...]) + (c2[...] + c3[...])
    for i in (0, 1):
        u, v = a_mine[i], a_other[i]
        bit = Place(meta).x0
        anc_out[i + 1, 0:4, :] = jnp.where(bit == 0, u, v)
        anc_out[i + 1, 4:8, :] = jnp.where(bit == 0, v, u)
    take_tiles(meta, Place(meta).partner(0), anc_out, give)
    take_tiles(meta, Place(meta).own(0), anc_out, own)


def backward_kernel(level, n, meta, *refs):
    count = WEIGHTS[level]
    if level == 0:
        g_refs, refs = refs[:4], refs[4:]
    else:
        (anc, recv), refs = refs[:2], refs[2:]
    y_ref, refs = refs[0], refs[1:]
    w_refs, refs = refs[:count], refs[count:]
    x_out, (ev, fv, gv, ov, sems) = refs[:-5], refs[-5:]
    if level == 0:
        ce, cf = copies_first(meta, w_refs[:5], w_refs[5:], ev, fv, sems)
    else:
        ce, cf = copies_upper(level, meta, w_refs, ev, fv, sems)
    for c in cf + ce:
        c.start()
    r = n // 4
    if level == 0:
        for s in range(4):
            gv[pl.ds(s * r, r), :] = g_refs[s][...]
        g = gv[...]
    else:
        take_tiles(meta, Place(meta).own(level), anc, ov)
        bit = Place(meta).bit(level)
        g = merged(ov[...], recv[...], r // 2, bit)
    gs = stacked(g)
    for c in cf:
        c.wait()
    z = y_ref[...] - product(gs, fv[...], NND)
    z = jnp.where(row_mask(meta, level, n), z, 0.0)
    for c in ce:
        c.wait()
    back(meta, level, n, ev, z, x_out)


SMEM = pl.BlockSpec(memory_space=pltpu.SMEM)
VMEM = pl.BlockSpec(memory_space=pltpu.VMEM)
ANY = pl.BlockSpec(memory_space=pl.ANY)


def call(kernel, name, shapes, scratch, meta, small, weights=(), flops=0):
    weights = [pltpu.with_memory_space_constraint(w, pltpu.HBM) for w in weights]
    moved = sum(w.size * 4 for w in weights) + sum(v.size * 4 for v in small)
    return pl.pallas_call(
        kernel,
        out_shape=[jax.ShapeDtypeStruct(s, f32) for s in shapes],
        in_specs=[SMEM] + [VMEM] * len(small) + [ANY] * len(weights),
        out_specs=[VMEM] * len(shapes),
        scratch_shapes=scratch,
        compiler_params=pltpu.CompilerParams(vmem_limit_bytes=(14 if flops else 3) * 2**20),
        cost_estimate=pl.CostEstimate(flops=flops, bytes_accessed=moved, transcendentals=0),
        name=name,
    )(meta, *small, *weights)


def local(
    live_tiles, row_tiles, rhs0, rhs1, rhs2, rhs3, dinv0, dinv1, dinv2, dinv3, off0, off1, off2
):
    ci, x0, x1 = lax.axis_index("core"), lax.axis_index("x0"), lax.axis_index("x1")
    leaf = x1 * 4 + x0 * 2 + ci
    here = leaf * 16 + lax.axis_index("z") * 4 + lax.axis_index("y")
    meta = jnp.concatenate([here.reshape(1), live_tiles, row_tiles.reshape(-1)])
    bits = [("core", ci), ("x0", x0), ("x1", x1)]

    def joined(v, i, dim=0):
        axis, bit = bits[i]
        return ordered(v, flip(v, axis), bit, dim)

    def swapped(pair, dim):
        mine = lax.dynamic_index_in_dim(pair, ci, dim, keepdims=False)
        give = lax.dynamic_index_in_dim(pair, 1 - ci, dim, keepdims=False)
        return mine, flip(give, "core")

    def rows_to_z(e):
        return lax.all_to_all(e, "z", 0, 0, tiled=True).reshape(1024, B)

    def gathered(e):
        return lax.all_gather(e, "y", axis=0, tiled=False)

    def spread(v, levels):
        for axis, bit in bits[:levels]:
            keep, give = halves(v, bit)
            v = ordered(keep, flip(give, axis), bit, 1)
        return v

    gate = lax.optimization_barrier
    e0 = jnp.swapaxes(dinv0.reshape(4, 4, B, B), 0, 1).reshape(4, 512, B)
    e0, dinv1, off0 = gate((e0, dinv1, off0))
    e0 = lax.all_to_all(e0, "y", 0, 0, tiled=True)
    fa, fb = shift(off0, "z", 1), shift(off0, "z", -1)
    e1 = ordered(*swapped(dinv1.reshape(2, 2, 256, B), 1), ci, 0)
    e1, fa, fb = gate((e1, fa, fb))
    e1 = rows_to_z(e1)
    e0, fa, fb, e1, dinv2, off2, dinv3 = gate((e0, fa, fb, e1, dinv2, off2, dinv3))
    m1 = gathered(jnp.concatenate([e1, off1], 0))

    ea, eb = shift(e0, "z", 1), shift(e0, "z", -1)
    fc, fd = shift(fa[:512], "z", 1), shift(fb[512:], "z", -1)
    e2 = joined(ordered(*(v[None] for v in swapped(dinv2.reshape(2, 256, B), 0)), ci, 0), 1)
    f2 = joined(off2, 1)
    e3 = joined(joined(dinv3[None], 1), 2)
    e2, e3 = rows_to_z(e2), rows_to_z(e3)
    c0 = gather4(rhs0, "y")
    ea, eb, fc, fd, e2, f2, e3, c0 = gate((ea, eb, fc, fd, e2, f2, e3, c0))
    ec, ed = shift(ea[:2], "z", 1), shift(eb[2:], "z", -1)
    w0 = [e0, ea, eb, ec, ed, off0, fa, fb, fc, fd]
    m2 = gathered(jnp.concatenate([e2, f2], 0))
    m3 = gathered(e3)

    dma = pltpu.SemaphoreType.DMA
    ev, fv = pltpu.VMEM((512, ORDER), f32), pltpu.VMEM((1024, 512), f32)

    def work(n):
        return [pltpu.VMEM((n, ORDER), f32), pltpu.VMEM((n, 512), f32), pltpu.VMEM((n, 1024), f32)]

    def flops(n):
        return 2 * n * 512 * (2048 + 1024) * 12

    y0, *u = call(
        functools.partial(forward_kernel, 0, 64, "rs"), "f0", [(64, 512)] + [(16, 1024)] * 4,
        [ev, fv, *work(64), dma((24,))], meta, c0, w0, flops(64),
    )
    m1, rhs1, rhs2, rhs3, _ = gate((m1, rhs1, rhs2, rhs3, y0))
    b1, b2, b3 = spread(rhs1, 1), spread(rhs2, 2), spread(rhs3, 3)
    w1 = m1, flip(m1, "core")
    parts = scatter4(u, "y")
    u = (parts[0] + parts[1]) + (parts[2] + parts[3])
    keep, give = halves(u, ci)
    c1, pk, pg = call(
        s01_kernel, "s01", [(8, ORDER), (2, 4, ORDER), (2, 4, ORDER)],
        [pltpu.VMEM((3, 8, ORDER), f32)], meta, [keep, flip(give, "core"), b1],
    )
    pr = flip(pg, "x0")
    y1, keep, give = call(
        functools.partial(forward_kernel, 1, 32, "ar"), "f1", [(32, 512), (16, 1024), (16, 1024)],
        [ev, fv, *work(32), dma((48,))], meta, gather4(c1, "z"), w1, flops(32),
    )
    part, keep3, give3 = call(
        s12_kernel, "s12", [(16, ORDER), (8, ORDER), (8, ORDER)],
        [pltpu.VMEM((2, 16, ORDER), f32)], meta, [keep, flip(give, "x0"), b2, pk, pr],
    )
    m2, _ = gate((m2, part))
    w2 = m2, flip(m2, "core")
    recv3 = flip(give3, "x1")
    y2, keep, give = call(
        functools.partial(forward_kernel, 2, 16, "ar"), "f2", [(16, 512), (8, 1024), (8, 1024)],
        [ev, fv, *work(16), dma((48,))], meta, gather4(part, "z"), w2, flops(16),
    )
    (part,) = call(
        s23_kernel, "s23", [(8, ORDER)],
        [pltpu.VMEM((1, 8, ORDER), f32)], meta, [keep, flip(give, "x1"), b3, keep3, recv3],
    )

    m3, _ = gate((m3, part))
    w3 = m3, flip(m3, "core")
    (part,) = call(
        top_kernel, "top", [(8, ORDER)], [ev, pltpu.VMEM((8, 512), f32), dma((32,))],
        meta, gather4(part, "z"), w3, flops(8),
    )
    x3, give = call(
        x3_kernel, "x3", [(8, ORDER), (8, 1024)], [pltpu.VMEM((1, 8, ORDER), f32)],
        meta, gather4(part, "z"),
    )
    recv = flip(give, "x1")
    x3r = flip(x3, "x1")

    def rest(n, small):
        return [ev, fv, pltpu.VMEM((n, 1024), f32), pltpu.VMEM((n // 2, 1024), f32), dma((48,))]

    (part,) = call(
        functools.partial(backward_kernel, 2, 16), "b2", [(16, ORDER)], rest(16, 0),
        meta, [x3[None], recv, y2], w2, flops(16),
    )
    anc, give = call(
        x2_kernel, "x2", [(2, 16, ORDER), (16, 1024)], [],
        meta, gather4(part, "z") + [x3, x3r],
    )
    recv = flip(give, "x0")
    a_mine = anc[:, :4]
    a_other = flip(a_mine, "x0")
    parts = call(
        functools.partial(backward_kernel, 1, 32), "b1", [(8, ORDER)] * 4, rest(32, 0),
        meta, [anc, recv, y1], w1, flops(32),
    )
    anc, give, own = call(
        x1_kernel, "x1", [(3, 8, ORDER), (8, 1024), (8, 1024)], [],
        meta, scatter4(parts, "z") + [a_mine, a_other],
    )
    g = ordered(own, flip(give, "core"), ci, 0)
    parts = call(
        functools.partial(backward_kernel, 0, 64), "b0", [(16, ORDER)] * 4, rest(64, 0),
        meta, gather4(g, "y") + [y0], w0, flops(64),
    )
    parts = scatter4(parts, "y")
    sol0 = (parts[0] + parts[1]) + (parts[2] + parts[3])

    outs = [sol0]
    for k in (1, 2, 3):
        width = ORDER // 2**k
        place = leaf % 2**k
        mine = lax.dynamic_slice_in_dim(anc[k - 1], place * width, width, 1)
        give = lax.dynamic_slice_in_dim(anc[k - 1], (place ^ 1) * width, width, 1)
        outs.append(ordered(mine, flip(give, "core"), ci, 0))
    return tuple(outs)


def solution(mesh):
    fine = Mesh(mesh.devices.reshape(2, 2, 2, 4, 4), ("x1", "x0", "core", "z", "y"))
    leaf, panel = ("x1", "x0", "core"), ("z", "y")
    return jax.shard_map(
        local,
        mesh=fine,
        in_specs=(P(), P()) + (P(panel, leaf),) * 4 + (P(leaf, panel),) * 7,
        out_specs=(P(panel, leaf),) * 4,
        check_vma=False,
    )
```

```python
import functools
import jax
import jax.numpy as jnp
from jax import lax
from jax.experimental import pallas as pl
from jax.experimental.pallas import tpu as pltpu
from jax.sharding import Mesh, PartitionSpec as P

B = 128
ORDER = 2048
NT = 16
f32 = jnp.float32
bf16 = jnp.bfloat16

FIRST = (0, 8, 12, 14)


class Place:
    def __init__(self, meta):
        self.meta = meta
        self.leaf = meta[0] >> 4
        self.zi, self.yi = (meta[0] >> 2) & 3, meta[0] & 3
        self.ci, self.x0, self.x1 = self.leaf & 1, (self.leaf >> 1) & 1, self.leaf >> 2

    def live(self, level):
        return self.meta[1 + FIRST[level] + (self.leaf >> level)]

    def own(self, level):
        return 16 + 8 * (FIRST[level] + (self.leaf >> level))

    def partner(self, level):
        return 16 + 8 * (FIRST[level] + ((self.leaf >> level) ^ 1))

    def bit(self, level):
        return (self.ci, self.x0, self.x1)[level]


def shift(v, axis, s):
    return lax.ppermute(v, axis, [(i, (i + s) % 4) for i in range(4)])


def flip(v, axis):
    return lax.ppermute(v, axis, [(0, 1), (1, 0)])


def gather4(v, axis):
    return [v] + [shift(v, axis, s) for s in (1, 2, 3)]


def scatter4(parts, axis):
    return [parts[0]] + [shift(parts[s], axis, -s) for s in (1, 2, 3)]


def ring(v, axis, dim):
    h = v.shape[dim] // 2
    a = shift(v, axis, 1)
    b = shift(v, axis, -1)
    c = shift(lax.slice_in_dim(a, 0, h, axis=dim), axis, 1)
    d = shift(lax.slice_in_dim(b, h, 2 * h, axis=dim), axis, -1)
    return [v, a, b, c, d]


def ordered(mine, other, bit, dim):
    return jnp.where(
        bit == 0, jnp.concatenate([mine, other], dim), jnp.concatenate([other, mine], dim)
    )


def halves(v, bit):
    h = v.shape[0] // 2
    return (
        jnp.where(bit == 0, v[:h], v[h:]),
        jnp.where(bit == 0, v[h:], v[:h]),
    )


def stacked(v):
    hi = v.astype(bf16).astype(f32)
    return jnp.concatenate([hi, v - hi], 0).astype(bf16)


def product(left, w, dims):
    hi = w.astype(bf16)
    lo = (w - hi.astype(f32)).astype(bf16)
    r = lax.dot_general(left, hi, (dims, ((), ())), preferred_element_type=f32)
    r = r + lax.dot_general(left, lo, (dims, ((), ())), preferred_element_type=f32)
    n = left.shape[0] // 2
    return r[:n] + r[n:]


NTD = ((1,), (1,))
NND = ((1,), (0,))


def copies_first(meta, refs, ev, fv, sems):
    e, f = refs[:5], refs[5:]
    zi = Place(meta).zi
    spots = [zi, lax.rem(zi + 3, 4), lax.rem(zi + 1, 4)]
    far = lax.rem(zi + 2, 4)
    pairs_e = [(ref, ev.at[w]) for ref, w in zip(e[:3], spots)]
    pairs_e += [(e[3], ev.at[far, 0:2]), (e[4], ev.at[far, 2:4])]
    pairs_f = [(ref, fv.at[w]) for ref, w in zip(f[:3], spots)]
    pairs_f += [(f[3], fv.at[far, 0:2]), (f[4], fv.at[far, 2:4])]
    made = [
        pltpu.make_async_copy(src, dst, sems.at[k]) for k, (src, dst) in enumerate(pairs_e + pairs_f)
    ]
    return made[:5], [], made[5:]


def copies_upper(level, meta, bufs, ev, fv, sems):
    place = Place(meta)
    groups = ([], [], [])
    k = 0
    for i, q in ((0, place.ci), (1, 1 - place.ci)):
        rows = pl.ds(pl.multiple_of(q * 256, 256), 256)
        pairs = [(bufs[i].at[:, s], ev.at[:, lax.rem(place.zi + 4 - s, 4), rows]) for s in range(4)]
        late = []
        if level == 1:
            late = [(bufs[i].at[:, 4:6], fv.at[:, pl.ds(2 * q, 2)])]
        elif level == 2:
            late = [(bufs[i].at[:, 4 + h], fv.at[:, 2 * h + q]) for h in (0, 1)]
        for group, some in ((groups[i], pairs), (groups[2], late)):
            for src, dst in some:
                group.append(pltpu.make_async_copy(src, dst, sems.at[k]))
                k += 1
    return groups


def copies(level, meta, refs, ev, fv, sems):
    if level == 0:
        return copies_first(meta, refs, ev, fv, sems)
    return copies_upper(level, meta, refs, ev, fv, sems)


def finish(group):
    for c in group:
        c.wait()


def tiles_in_order(level):
    if level == 0:
        return [(t // 4, t % 4) for t in range(NT)]
    return [(t % 4, t // 4) for t in range(NT)]


def column_mask(meta, level, n):
    col = lax.broadcasted_iota(jnp.int32, (n, ORDER), 1)
    return col < Place(meta).live(level) * B


def row_mask(meta, level, n):
    own = lax.broadcasted_iota(jnp.int32, (n, 512), 1) // B
    place = Place(meta)
    tile = 4 * own + place.yi if level == 0 else 4 * place.zi + own
    return tile < Place(meta).live(level)


def solve_rows(level, meta, ev, yv, cs, late):
    first = Place(meta).ci if level else 0

    def body(j, carry):
        @pl.when(j == 1)
        def _():
            finish(late)

        at = pl.multiple_of(jnp.where(j == 0, first, 1 - first) * 256, 256)
        rows = pl.ds(at, 256)
        w = jnp.concatenate([ev[w, s, rows, :] for w, s in tiles_in_order(level)], 1)
        yv[:, rows] = product(cs, w, NTD)
        return carry

    lax.fori_loop(0, 2, body, 0)


WEIGHTS = (10, 2, 2, 2)


def forward_kernel(level, n, mode, meta, *refs):
    count = WEIGHTS[level]
    c_refs, refs = refs[:4], refs[4:]
    w_refs, refs = refs[:count], refs[count:]
    if mode == "rs":
        y_out, u_out = refs[0], refs[1:5]
        refs = refs[5:]
    else:
        y_out, keep_out, give_out = refs[:3]
        refs = refs[3:]
    ev, fv, cv, yv, uv, sems = refs
    early, late, last = copies(level, meta, w_refs, ev, fv, sems)
    for c in [*early, *late, *last]:
        c.start()
    r = n // 4
    if level < 2:
        for s in range(4):
            cv[pl.ds(s * r, r), :] = c_refs[s][...]
        c = cv[...]
    else:
        c = summed(c_refs, r)
    cs = stacked(jnp.where(column_mask(meta, level, n), c, 0.0))
    finish(early)
    solve_rows(level, meta, ev, yv, cs, late)
    y = jnp.where(row_mask(meta, level, n), yv[...], 0.0)
    y_out[...] = y
    ys = stacked(y)
    finish(last)

    def body(j, carry):
        w = jnp.concatenate([fv[w, j] for w in range(4)], 1)
        uv[:, pl.ds(pl.multiple_of(j * 256, 256), 256)] = product(ys, w, NTD)
        return carry

    lax.fori_loop(0, 4, body, 0)
    if mode == "rs":
        for s in range(4):
            u_out[s][...] = uv[pl.ds(s * r, r), :]
    else:
        split_rows(uv, r, Place(meta).bit(level), keep_out, give_out)


def split_rows(v, r, bit, keep_out, give_out):
    h = r // 2
    for s in range(4):
        low = v[pl.ds(s * r, h), :]
        high = v[pl.ds(s * r + h, h), :]
        keep_out[pl.ds(s * h, h), :] = jnp.where(bit == 0, low, high)
        give_out[pl.ds(s * h, h), :] = jnp.where(bit == 0, high, low)


def summed(refs, r):
    parts = []
    for s in range(4):
        total = refs[0][pl.ds(s * r, r), :]
        for d in (1, 2, 3):
            total = total + refs[d][pl.ds((s - d) % 4 * r, r), :]
        parts.append(total)
    return jnp.concatenate(parts, 0)


def add_tiles(meta, at, src, acc):
    for t in range(8):
        v = meta[at + t]
        cols = pl.ds(pl.multiple_of(lax.rem(v, NT) * B, B), B)
        lev = lax.div(v, NT)
        acc[lev, :, cols] = acc[lev, :, cols] + src[:, t * B : (t + 1) * B]


def take_tiles(meta, at, anc, dst):
    for t in range(8):
        v = meta[at + t]
        cols = pl.ds(pl.multiple_of(lax.rem(v, NT) * B, B), B)
        dst[:, t * B : (t + 1) * B] = anc[lax.div(v, NT), :, cols]


def s01_kernel(meta, keep, recv, b_mine, b_other, c1, pk, pg, acc):
    place = Place(meta)
    acc[...] = jnp.zeros_like(acc)
    add_tiles(meta, place.own(0), keep, acc)
    add_tiles(meta, place.partner(0), recv, acc)
    group = (0, place.x0, place.leaf >> 1)
    for ref, c in ((b_mine, place.ci), (b_other, 1 - place.ci)):
        at = 0
        for i in range(3):
            width = 1024 >> i
            cols = pl.ds(pl.multiple_of((2 * group[i] + c) * width, width), width)
            acc[i, :, cols] = acc[i, :, cols] - ref[:, at : at + width]
            at += width
    c1[...] = -acc[0]
    for i in (0, 1):
        low, high = acc[i + 1, 0:4, :], acc[i + 1, 4:8, :]
        pk[i] = jnp.where(place.x0 == 0, low, high)
        pg[i] = jnp.where(place.x0 == 0, high, low)


def s12_kernel(meta, keep, recv, pk, pr, part, keep3, give3, acc):
    place = Place(meta)
    acc[...] = jnp.zeros_like(acc)
    add_tiles(meta, place.own(1), keep, acc)
    add_tiles(meta, place.partner(1), recv, acc)
    for i in (0, 1):
        acc[i, 0:4, :] = acc[i, 0:4, :] + (pk[i] + pr[i])
    part[...] = -acc[0]
    split_rows(acc.at[1], 4, place.x1, keep3, give3)


def s23_kernel(meta, keep, recv, keep3, recv3, part, acc):
    place = Place(meta)
    acc[...] = jnp.zeros_like(acc)
    add_tiles(meta, place.own(2), keep, acc)
    add_tiles(meta, place.partner(2), recv, acc)
    part[...] = -(acc[0] + (keep3[...] + recv3[...]))


def top_kernel(meta, c0, c1, c2, c3, *refs):
    w_refs, (x_out, ev, yv, sems) = refs[:2], refs[2:]
    early, late, _ = copies(3, meta, w_refs, ev, None, sems)
    for c in [*early, *late]:
        c.start()
    c = summed((c0, c1, c2, c3), 2)
    cs = stacked(jnp.where(column_mask(meta, 3, 8), c, 0.0))
    finish(early)
    solve_rows(3, meta, ev, yv, cs, late)
    back(meta, 3, 8, ev, jnp.where(row_mask(meta, 3, 8), yv[...], 0.0), [x_out])


def back(meta, level, n, ev, z, x_out):
    zs = stacked(z)
    live = Place(meta).live(level) * B

    def body(j, carry):
        cols = pl.ds(pl.multiple_of(j * 512, 512), 512)
        w = jnp.concatenate([ev[j, i] if level == 0 else ev[i, j] for i in range(4)], 1)
        v = product(zs, w, NND)
        col = lax.broadcasted_iota(jnp.int32, (n, 512), 1) + j * 512
        v = jnp.where(col < live, v, 0.0)
        r = n // len(x_out)
        for s, out in enumerate(x_out):
            out[:, cols] = v[s * r : (s + 1) * r]
        return carry

    lax.fori_loop(0, 4, body, 0)


def x3_kernel(meta, c0, c1, c2, c3, x_out, give, anc):
    x = summed((c0, c1, c2, c3), 2)
    x_out[...] = x
    anc[0] = x
    take_tiles(meta, Place(meta).partner(2), anc, give)


def merged(a, b, h, bit):
    parts = []
    for s in range(4):
        u, v = a[s * h : (s + 1) * h, :], b[s * h : (s + 1) * h, :]
        parts += [jnp.where(bit == 0, u, v), jnp.where(bit == 0, v, u)]
    return jnp.concatenate(parts, 0)


def x2_kernel(meta, c0, c1, c2, c3, x3, x3r, anc_out, give):
    anc_out[0] = summed((c0, c1, c2, c3), 4)
    anc_out[1] = merged(x3[...], x3r[...], 2, Place(meta).x1)
    take_tiles(meta, Place(meta).partner(1), anc_out, give)


def x1_kernel(meta, c0, c1, c2, c3, a_mine, a_other, anc_out, give, own):
    anc_out[0] = (c0[...] + c1[...]) + (c2[...] + c3[...])
    for i in (0, 1):
        u, v = a_mine[i], a_other[i]
        bit = Place(meta).x0
        anc_out[i + 1, 0:4, :] = jnp.where(bit == 0, u, v)
        anc_out[i + 1, 4:8, :] = jnp.where(bit == 0, v, u)
    take_tiles(meta, Place(meta).partner(0), anc_out, give)
    take_tiles(meta, Place(meta).own(0), anc_out, own)


def backward_kernel(level, n, meta, *refs):
    count = WEIGHTS[level]
    if level == 0:
        g_refs, refs = refs[:4], refs[4:]
    else:
        (anc, recv), refs = refs[:2], refs[2:]
    y_ref, refs = refs[0], refs[1:]
    w_refs, refs = refs[:count], refs[count:]
    x_out, (ev, fv, gv, ov, sems) = refs[:-5], refs[-5:]
    early, late, first = copies(level, meta, w_refs, ev, fv, sems)
    for c in [*first, *early, *late]:
        c.start()
    r = n // 4
    if level == 0:
        for s in range(4):
            gv[pl.ds(s * r, r), :] = g_refs[s][...]
        g = gv[...]
    else:
        take_tiles(meta, Place(meta).own(level), anc, ov)
        g = merged(ov[...], recv[...], r // 2, Place(meta).bit(level))
    gs = stacked(g)
    finish(first)
    w = jnp.concatenate([fv[w].reshape(1024, B) for w in range(4)], 1)
    z = y_ref[...] - product(gs, w, NND)
    z = jnp.where(row_mask(meta, level, n), z, 0.0)
    finish(early)
    finish(late)
    back(meta, level, n, ev, z, x_out)


SMEM = pl.BlockSpec(memory_space=pltpu.SMEM)
VMEM = pl.BlockSpec(memory_space=pltpu.VMEM)
ANY = pl.BlockSpec(memory_space=pl.ANY)


def call(kernel, name, shapes, scratch, meta, small, weights=(), flops=0):
    weights = [pltpu.with_memory_space_constraint(w, pltpu.HBM) for w in weights]
    moved = sum(w.size * 4 for w in weights) + sum(v.size * 4 for v in small)
    return pl.pallas_call(
        kernel,
        out_shape=[jax.ShapeDtypeStruct(s, f32) for s in shapes],
        in_specs=[SMEM] + [VMEM] * len(small) + [ANY] * len(weights),
        out_specs=[VMEM] * len(shapes),
        scratch_shapes=scratch,
        compiler_params=pltpu.CompilerParams(vmem_limit_bytes=(14 if flops else 3) * 2**20),
        cost_estimate=pl.CostEstimate(flops=flops, bytes_accessed=moved, transcendentals=0),
        name=name,
    )(meta, *small, *weights)


def local(
    live_tiles, row_tiles, rhs0, rhs1, rhs2, rhs3, dinv0, dinv1, dinv2, dinv3, off0, off1, off2
):
    ci, x0, x1 = lax.axis_index("core"), lax.axis_index("x0"), lax.axis_index("x1")
    zi = lax.axis_index("z")
    leaf = x1 * 4 + x0 * 2 + ci
    here = leaf * 16 + zi * 4 + lax.axis_index("y")
    meta = jnp.concatenate([here.reshape(1), live_tiles, row_tiles.reshape(-1)])
    bits = [("core", ci), ("x0", x0), ("x1", x1)]

    def joined(v, i, dim=0):
        axis, bit = bits[i]
        return ordered(v, flip(v, axis), bit, dim)

    def pick(v, i, dim=0):
        return lax.dynamic_index_in_dim(v, i, dim, keepdims=False)

    def for_z(pair, other, bit):
        blocks = []
        for s in range(4):
            z = (zi + s) % 4
            blocks.append(jnp.where(z // 2 == bit, pick(pair, z % 2), pick(other, z % 2)))
        return [blocks[0]] + [shift(blocks[s], "z", s) for s in (1, 2, 3)]

    def gathered(blocks, f):
        parts = [v[None] for v in blocks] + ([] if f is None else [f.reshape(2, 256, B)])
        return lax.all_gather(jnp.concatenate(parts, 0), "y", axis=0, tiled=False)

    gate = lax.optimization_barrier
    e0 = jnp.swapaxes(dinv0.reshape(4, 4, B, B), 0, 1).reshape(4, 512, B)
    e0, dinv1, off0 = gate((e0, dinv1, off0.reshape(4, 256, B)))
    e0 = lax.all_to_all(e0, "y", 0, 0, tiled=True)
    fa, fb = shift(off0, "z", 1), shift(off0, "z", -1)
    e1 = dinv1.reshape(2, 2, 256, B)
    e1 = for_z(pick(e1, ci, 1), flip(pick(e1, 1 - ci, 1), "core"), ci)
    e0, fa, fb, e1, dinv2, off2, dinv3 = gate((e0, fa, fb, e1, dinv2, off2, dinv3))
    m1 = gathered(e1, off1)

    ea, eb = shift(e0, "z", 1), shift(e0, "z", -1)
    fc, fd = shift(fa[:2], "z", 1), shift(fb[2:], "z", -1)
    e2 = dinv2.reshape(2, 256, B)
    e2 = ordered(pick(e2, ci)[None], flip(pick(e2, 1 - ci)[None], "core"), ci, 0)
    e2 = for_z(e2, flip(e2, "x0"), x0)
    f2 = joined(off2, 1)
    e3 = joined(dinv3[None], 1)
    e3 = for_z(e3, flip(e3, "x1"), x1)
    c0 = gather4(rhs0, "y")
    ea, eb, fc, fd, e2, f2, e3, c0 = gate((ea, eb, fc, fd, e2, f2, e3, c0))
    ec, ed = shift(ea[:2], "z", 1), shift(eb[2:], "z", -1)
    b_mine, b_other = halves(jnp.concatenate([rhs1, rhs2, rhs3], 1), ci)
    b_other = flip(b_other, "core")
    ec, ed, b_mine, b_other = gate((ec, ed, b_mine, b_other))
    w0 = [e0, ea, eb, ec, ed, off0, fa, fb, fc, fd]
    m2 = gathered(e2, f2)
    m3 = gathered(e3, None)

    dma = pltpu.SemaphoreType.DMA
    ev, fv = pltpu.VMEM((4, 4, 512, B), f32), pltpu.VMEM((4, 4, 256, B), f32)

    def work(n):
        return [pltpu.VMEM((n, ORDER), f32), pltpu.VMEM((n, 512), f32), pltpu.VMEM((n, 1024), f32)]

    def flops(n):
        return 2 * n * 512 * (2048 + 1024) * 12

    y0, *u = call(
        functools.partial(forward_kernel, 0, 64, "rs"), "f0", [(64, 512)] + [(16, 1024)] * 4,
        [ev, fv, *work(64), dma((10,))], meta, c0, w0, flops(64),
    )
    m1, _ = gate((m1, y0))
    w1 = m1, flip(m1, "core")
    parts = scatter4(u, "y")
    u = (parts[0] + parts[1]) + (parts[2] + parts[3])
    keep, give = halves(u, ci)
    c1, pk, pg = call(
        s01_kernel, "s01", [(8, ORDER), (2, 4, ORDER), (2, 4, ORDER)],
        [pltpu.VMEM((3, 8, ORDER), f32)], meta, [keep, flip(give, "core"), b_mine, b_other],
    )
    pr = flip(pg, "x0")
    y1, keep, give = call(
        functools.partial(forward_kernel, 1, 32, "ar"), "f1", [(32, 512), (16, 1024), (16, 1024)],
        [ev, fv, *work(32), dma((12,))], meta, gather4(c1, "z"), w1, flops(32),
    )
    part, keep3, give3 = call(
        s12_kernel, "s12", [(16, ORDER), (8, ORDER), (8, ORDER)],
        [pltpu.VMEM((2, 16, ORDER), f32)], meta, [keep, flip(give, "x0"), pk, pr],
    )
    m2, _ = gate((m2, part))
    w2 = m2, flip(m2, "core")
    recv3 = flip(give3, "x1")
    y2, keep, give = call(
        functools.partial(forward_kernel, 2, 16, "ar"), "f2", [(16, 512), (8, 1024), (8, 1024)],
        [ev, fv, *work(16), dma((12,))], meta, gather4(part, "z"), w2, flops(16),
    )
    (part,) = call(
        s23_kernel, "s23", [(8, ORDER)],
        [pltpu.VMEM((1, 8, ORDER), f32)], meta, [keep, flip(give, "x1"), keep3, recv3],
    )

    m3, _ = gate((m3, part))
    w3 = m3, flip(m3, "core")
    (part,) = call(
        top_kernel, "top", [(8, ORDER)], [ev, pltpu.VMEM((8, 512), f32), dma((8,))],
        meta, gather4(part, "z"), w3, flops(8),
    )
    x3, give = call(
        x3_kernel, "x3", [(8, ORDER), (8, 1024)], [pltpu.VMEM((1, 8, ORDER), f32)],
        meta, gather4(part, "z"),
    )
    recv = flip(give, "x1")
    x3r = flip(x3, "x1")

    def rest(n, small):
        return [ev, fv, pltpu.VMEM((n, 1024), f32), pltpu.VMEM((n // 2, 1024), f32), dma((12,))]

    (part,) = call(
        functools.partial(backward_kernel, 2, 16), "b2", [(16, ORDER)], rest(16, 0),
        meta, [x3[None], recv, y2], w2, flops(16),
    )
    anc, give = call(
        x2_kernel, "x2", [(2, 16, ORDER), (16, 1024)], [],
        meta, gather4(part, "z") + [x3, x3r],
    )
    recv = flip(give, "x0")
    a_mine = anc[:, :4]
    a_other = flip(a_mine, "x0")
    parts = call(
        functools.partial(backward_kernel, 1, 32), "b1", [(8, ORDER)] * 4, rest(32, 0),
        meta, [anc, recv, y1], w1, flops(32),
    )
    anc, give, own = call(
        x1_kernel, "x1", [(3, 8, ORDER), (8, 1024), (8, 1024)], [],
        meta, scatter4(parts, "z") + [a_mine, a_other],
    )
    g = ordered(own, flip(give, "core"), ci, 0)
    parts = call(
        functools.partial(backward_kernel, 0, 64), "b0", [(16, ORDER)] * 4, rest(64, 0),
        meta, gather4(g, "y") + [y0], w0, flops(64),
    )
    parts = scatter4(parts, "y")
    sol0 = (parts[0] + parts[1]) + (parts[2] + parts[3])

    outs = [sol0]
    for k in (1, 2, 3):
        width = ORDER // 2**k
        place = leaf % 2**k
        mine = lax.dynamic_slice_in_dim(anc[k - 1], place * width, width, 1)
        give = lax.dynamic_slice_in_dim(anc[k - 1], (place ^ 1) * width, width, 1)
        outs.append(ordered(mine, flip(give, "core"), ci, 0))
    return tuple(outs)


def solution(mesh):
    fine = Mesh(mesh.devices.reshape(2, 2, 2, 4, 4), ("x1", "x0", "core", "z", "y"))
    leaf, panel = ("x1", "x0", "core"), ("z", "y")
    return jax.shard_map(
        local,
        mesh=fine,
        in_specs=(P(), P()) + (P(panel, leaf),) * 4 + (P(leaf, panel),) * 7,
        out_specs=(P(panel, leaf),) * 4,
        check_vma=False,
    )
```

```python
import functools
import jax
import jax.numpy as jnp
from jax import lax
from jax.experimental import pallas as pl
from jax.experimental.pallas import tpu as pltpu
from jax.sharding import Mesh, PartitionSpec as P

B = 128
ORDER = 2048
NT = 16
f32 = jnp.float32
bf16 = jnp.bfloat16

FIRST = (0, 8, 12, 14)


class Place:
    def __init__(self, meta):
        self.meta = meta
        self.leaf = meta[0] >> 4
        self.zi, self.yi = (meta[0] >> 2) & 3, meta[0] & 3
        self.ci, self.x0, self.x1 = self.leaf & 1, (self.leaf >> 1) & 1, self.leaf >> 2

    def live(self, level):
        return self.meta[1 + FIRST[level] + (self.leaf >> level)]

    def own(self, level):
        return 16 + 8 * (FIRST[level] + (self.leaf >> level))

    def partner(self, level):
        return 16 + 8 * (FIRST[level] + ((self.leaf >> level) ^ 1))

    def bit(self, level):
        return (self.ci, self.x0, self.x1)[level]


def shift(v, axis, s):
    return lax.ppermute(v, axis, [(i, (i + s) % 4) for i in range(4)])


def flip(v, axis):
    return lax.ppermute(v, axis, [(0, 1), (1, 0)])


def gather4(v, axis):
    far = shift(v, axis, 2)
    return [v, shift(v, axis, 1), far, shift(v, axis, 3)]


def scatter4(parts, axis):
    far = shift(parts[2], axis, 2)
    return [parts[0], shift(parts[1], axis, -1), far, shift(parts[3], axis, 1)]


def ring(v, axis, dim):
    h = v.shape[dim] // 2
    a = shift(v, axis, 1)
    b = shift(v, axis, -1)
    c = shift(lax.slice_in_dim(a, 0, h, axis=dim), axis, 1)
    d = shift(lax.slice_in_dim(b, h, 2 * h, axis=dim), axis, -1)
    return [v, a, b, c, d]


def ordered(mine, other, bit, dim):
    return jnp.where(
        bit == 0, jnp.concatenate([mine, other], dim), jnp.concatenate([other, mine], dim)
    )


def halves(v, bit):
    h = v.shape[0] // 2
    return (
        jnp.where(bit == 0, v[:h], v[h:]),
        jnp.where(bit == 0, v[h:], v[:h]),
    )


def stacked(v):
    hi = v.astype(bf16).astype(f32)
    return jnp.concatenate([hi, v - hi], 0).astype(bf16)


def product(left, w, dims):
    hi = w.astype(bf16)
    lo = (w - hi.astype(f32)).astype(bf16)
    r = lax.dot_general(left, hi, (dims, ((), ())), preferred_element_type=f32)
    r = r + lax.dot_general(left, lo, (dims, ((), ())), preferred_element_type=f32)
    n = left.shape[0] // 2
    return r[:n] + r[n:]


NTD = ((1,), (1,))
NND = ((1,), (0,))


def copies_first(meta, refs, ev, fv, sems):
    e, f = refs[:5], refs[5:]
    zi = Place(meta).zi
    spots = [zi, lax.rem(zi + 3, 4), lax.rem(zi + 1, 4)]
    far = lax.rem(zi + 2, 4)
    pairs_e = [(ref, ev.at[w]) for ref, w in zip(e[:3], spots)]
    pairs_e += [(e[3], ev.at[far, 0:2]), (e[4], ev.at[far, 2:4])]
    pairs_f = [(ref, fv.at[w]) for ref, w in zip(f[:3], spots)]
    pairs_f += [(f[3], fv.at[far, 0:2]), (f[4], fv.at[far, 2:4])]
    made = [
        pltpu.make_async_copy(src, dst, sems.at[k]) for k, (src, dst) in enumerate(pairs_e + pairs_f)
    ]
    return made[:5], [], made[5:]


def copies_upper(level, meta, bufs, ev, fv, sems):
    place = Place(meta)
    groups = ([], [], [])
    k = 0
    for i, q in ((0, place.ci), (1, 1 - place.ci)):
        rows = pl.ds(pl.multiple_of(q * 256, 256), 256)
        pairs = [(bufs[i].at[:, s], ev.at[:, lax.rem(place.zi + 4 - s, 4), rows]) for s in range(4)]
        late = []
        if level == 1:
            late = [(bufs[i].at[:, 4:6], fv.at[:, pl.ds(2 * q, 2)])]
        elif level == 2:
            late = [(bufs[i].at[:, 4 + h], fv.at[:, 2 * h + q]) for h in (0, 1)]
        for group, some in ((groups[i], pairs), (groups[2], late)):
            for src, dst in some:
                group.append(pltpu.make_async_copy(src, dst, sems.at[k]))
                k += 1
    return groups


def copies(level, meta, refs, ev, fv, sems):
    if level == 0:
        return copies_first(meta, refs, ev, fv, sems)
    return copies_upper(level, meta, refs, ev, fv, sems)


def finish(group):
    for c in group:
        c.wait()


def tiles_in_order(level):
    if level == 0:
        return [(t // 4, t % 4) for t in range(NT)]
    return [(t % 4, t // 4) for t in range(NT)]


def column_mask(meta, level, n):
    col = lax.broadcasted_iota(jnp.int32, (n, ORDER), 1)
    return col < Place(meta).live(level) * B


def row_mask(meta, level, n):
    own = lax.broadcasted_iota(jnp.int32, (n, 512), 1) // B
    place = Place(meta)
    tile = 4 * own + place.yi if level == 0 else 4 * place.zi + own
    return tile < Place(meta).live(level)


def solve_rows(level, meta, ev, yv, cs, late):
    first = Place(meta).ci if level else 0

    def body(j, carry):
        @pl.when(j == 1)
        def _():
            finish(late)

        at = pl.multiple_of(jnp.where(j == 0, first, 1 - first) * 256, 256)
        rows = pl.ds(at, 256)
        w = jnp.concatenate([ev[w, s, rows, :] for w, s in tiles_in_order(level)], 1)
        yv[:, rows] = product(cs, w, NTD)
        return carry

    lax.fori_loop(0, 2, body, 0)


WEIGHTS = (10, 2, 2, 2)


def forward_kernel(level, n, mode, meta, *refs):
    count = WEIGHTS[level]
    c_refs, refs = refs[:4], refs[4:]
    w_refs, refs = refs[:count], refs[count:]
    if mode == "rs":
        y_out, u_out = refs[0], refs[1:5]
        refs = refs[5:]
    else:
        y_out, keep_out, give_out = refs[:3]
        refs = refs[3:]
    ev, fv, cv, yv, uv, sems = refs
    early, late, last = copies(level, meta, w_refs, ev, fv, sems)
    for c in [*early, *late, *last]:
        c.start()
    r = n // 4
    if level < 2:
        for s in range(4):
            cv[pl.ds(s * r, r), :] = c_refs[s][...]
        c = cv[...]
    else:
        c = summed(c_refs, r)
    cs = stacked(jnp.where(column_mask(meta, level, n), c, 0.0))
    finish(early)
    solve_rows(level, meta, ev, yv, cs, late)
    y = jnp.where(row_mask(meta, level, n), yv[...], 0.0)
    y_out[...] = y
    ys = stacked(y)
    finish(last)

    def body(j, carry):
        w = jnp.concatenate([fv[w, j] for w in range(4)], 1)
        uv[:, pl.ds(pl.multiple_of(j * 256, 256), 256)] = product(ys, w, NTD)
        return carry

    lax.fori_loop(0, 4, body, 0)
    if mode == "rs":
        for s in range(4):
            u_out[s][...] = uv[pl.ds(s * r, r), :]
    else:
        split_rows(uv, r, Place(meta).bit(level), keep_out, give_out)


def split_rows(v, r, bit, keep_out, give_out):
    h = r // 2
    for s in range(4):
        low = v[pl.ds(s * r, h), :]
        high = v[pl.ds(s * r + h, h), :]
        keep_out[pl.ds(s * h, h), :] = jnp.where(bit == 0, low, high)
        give_out[pl.ds(s * h, h), :] = jnp.where(bit == 0, high, low)


def summed(refs, r):
    parts = []
    for s in range(4):
        total = refs[0][pl.ds(s * r, r), :]
        for d in (1, 2, 3):
            total = total + refs[d][pl.ds((s - d) % 4 * r, r), :]
        parts.append(total)
    return jnp.concatenate(parts, 0)


def add_tiles(meta, at, src, acc):
    for t in range(8):
        v = meta[at + t]
        cols = pl.ds(pl.multiple_of(lax.rem(v, NT) * B, B), B)
        lev = lax.div(v, NT)
        acc[lev, :, cols] = acc[lev, :, cols] + src[:, t * B : (t + 1) * B]


def take_tiles(meta, at, anc, dst):
    for t in range(8):
        v = meta[at + t]
        cols = pl.ds(pl.multiple_of(lax.rem(v, NT) * B, B), B)
        dst[:, t * B : (t + 1) * B] = anc[lax.div(v, NT), :, cols]


def s01_kernel(meta, keep, recv, b_mine, b_other, c1, pk, pg, acc):
    place = Place(meta)
    acc[...] = jnp.zeros_like(acc)
    add_tiles(meta, place.own(0), keep, acc)
    add_tiles(meta, place.partner(0), recv, acc)
    group = (0, place.x0, place.leaf >> 1)
    for ref, c in ((b_mine, place.ci), (b_other, 1 - place.ci)):
        at = 0
        for i in range(3):
            width = 1024 >> i
            cols = pl.ds(pl.multiple_of((2 * group[i] + c) * width, width), width)
            acc[i, :, cols] = acc[i, :, cols] - ref[:, at : at + width]
            at += width
    c1[...] = -acc[0]
    for i in (0, 1):
        low, high = acc[i + 1, 0:4, :], acc[i + 1, 4:8, :]
        pk[i] = jnp.where(place.x0 == 0, low, high)
        pg[i] = jnp.where(place.x0 == 0, high, low)


def s12_kernel(meta, keep, recv, pk, pr, part, keep3, give3, acc):
    place = Place(meta)
    acc[...] = jnp.zeros_like(acc)
    add_tiles(meta, place.own(1), keep, acc)
    add_tiles(meta, place.partner(1), recv, acc)
    for i in (0, 1):
        acc[i, 0:4, :] = acc[i, 0:4, :] + (pk[i] + pr[i])
    part[...] = -acc[0]
    split_rows(acc.at[1], 4, place.x1, keep3, give3)


def s23_kernel(meta, keep, recv, keep3, recv3, part, acc):
    place = Place(meta)
    acc[...] = jnp.zeros_like(acc)
    add_tiles(meta, place.own(2), keep, acc)
    add_tiles(meta, place.partner(2), recv, acc)
    part[...] = -(acc[0] + (keep3[...] + recv3[...]))


def top_kernel(meta, c0, c1, c2, c3, *refs):
    w_refs, (x_out, ev, yv, sems) = refs[:2], refs[2:]
    early, late, _ = copies(3, meta, w_refs, ev, None, sems)
    for c in [*early, *late]:
        c.start()
    c = summed((c0, c1, c2, c3), 2)
    cs = stacked(jnp.where(column_mask(meta, 3, 8), c, 0.0))
    finish(early)
    solve_rows(3, meta, ev, yv, cs, late)
    back(meta, 3, 8, ev, jnp.where(row_mask(meta, 3, 8), yv[...], 0.0), [x_out])


def back(meta, level, n, ev, z, x_out):
    zs = stacked(z)
    live = Place(meta).live(level) * B

    def body(j, carry):
        cols = pl.ds(pl.multiple_of(j * 512, 512), 512)
        w = jnp.concatenate([ev[j, i] if level == 0 else ev[i, j] for i in range(4)], 1)
        v = product(zs, w, NND)
        col = lax.broadcasted_iota(jnp.int32, (n, 512), 1) + j * 512
        v = jnp.where(col < live, v, 0.0)
        r = n // len(x_out)
        for s, out in enumerate(x_out):
            out[:, cols] = v[s * r : (s + 1) * r]
        return carry

    lax.fori_loop(0, 4, body, 0)


def x3_kernel(meta, c0, c1, c2, c3, x_out, give, anc):
    x = summed((c0, c1, c2, c3), 2)
    x_out[...] = x
    anc[0] = x
    take_tiles(meta, Place(meta).partner(2), anc, give)


def merged(a, b, h, bit):
    parts = []
    for s in range(4):
        u, v = a[s * h : (s + 1) * h, :], b[s * h : (s + 1) * h, :]
        parts += [jnp.where(bit == 0, u, v), jnp.where(bit == 0, v, u)]
    return jnp.concatenate(parts, 0)


def x2_kernel(meta, c0, c1, c2, c3, x3, x3r, anc_out, give):
    anc_out[0] = summed((c0, c1, c2, c3), 4)
    anc_out[1] = merged(x3[...], x3r[...], 2, Place(meta).x1)
    take_tiles(meta, Place(meta).partner(1), anc_out, give)


def x1_kernel(meta, c0, c1, c2, c3, a_mine, a_other, anc_out, give, own):
    anc_out[0] = (c0[...] + c1[...]) + (c2[...] + c3[...])
    for i in (0, 1):
        u, v = a_mine[i], a_other[i]
        bit = Place(meta).x0
        anc_out[i + 1, 0:4, :] = jnp.where(bit == 0, u, v)
        anc_out[i + 1, 4:8, :] = jnp.where(bit == 0, v, u)
    take_tiles(meta, Place(meta).partner(0), anc_out, give)
    take_tiles(meta, Place(meta).own(0), anc_out, own)


def backward_kernel(level, n, meta, *refs):
    count = WEIGHTS[level]
    if level == 0:
        g_refs, refs = refs[:4], refs[4:]
    else:
        (anc, recv), refs = refs[:2], refs[2:]
    y_ref, refs = refs[0], refs[1:]
    w_refs, refs = refs[:count], refs[count:]
    x_out, (ev, fv, gv, ov, sems) = refs[:-5], refs[-5:]
    early, late, first = copies(level, meta, w_refs, ev, fv, sems)
    for c in [*first, *early, *late]:
        c.start()
    r = n // 4
    if level == 0:
        for s in range(4):
            gv[pl.ds(s * r, r), :] = g_refs[s][...]
        g = gv[...]
    else:
        take_tiles(meta, Place(meta).own(level), anc, ov)
        g = merged(ov[...], recv[...], r // 2, Place(meta).bit(level))
    gs = stacked(g)
    finish(first)
    w = jnp.concatenate([fv[w].reshape(1024, B) for w in range(4)], 1)
    z = y_ref[...] - product(gs, w, NND)
    z = jnp.where(row_mask(meta, level, n), z, 0.0)
    finish(early)
    finish(late)
    back(meta, level, n, ev, z, x_out)


SMEM = pl.BlockSpec(memory_space=pltpu.SMEM)
VMEM = pl.BlockSpec(memory_space=pltpu.VMEM)
ANY = pl.BlockSpec(memory_space=pl.ANY)


def call(kernel, name, shapes, scratch, meta, small, weights=(), flops=0):
    weights = [pltpu.with_memory_space_constraint(w, pltpu.HBM) for w in weights]
    moved = sum(w.size * 4 for w in weights) + sum(v.size * 4 for v in small)
    return pl.pallas_call(
        kernel,
        out_shape=[jax.ShapeDtypeStruct(s, f32) for s in shapes],
        in_specs=[SMEM] + [VMEM] * len(small) + [ANY] * len(weights),
        out_specs=[VMEM] * len(shapes),
        scratch_shapes=scratch,
        compiler_params=pltpu.CompilerParams(vmem_limit_bytes=(14 if flops else 3) * 2**20),
        cost_estimate=pl.CostEstimate(flops=flops, bytes_accessed=moved, transcendentals=0),
        name=name,
    )(meta, *small, *weights)


def local(
    live_tiles, row_tiles, rhs0, rhs1, rhs2, rhs3, dinv0, dinv1, dinv2, dinv3, off0, off1, off2
):
    ci, x0, x1 = lax.axis_index("core"), lax.axis_index("x0"), lax.axis_index("x1")
    zi = lax.axis_index("z")
    leaf = x1 * 4 + x0 * 2 + ci
    here = leaf * 16 + zi * 4 + lax.axis_index("y")
    meta = jnp.concatenate([here.reshape(1), live_tiles, row_tiles.reshape(-1)])
    bits = [("core", ci), ("x0", x0), ("x1", x1)]

    def joined(v, i, dim=0):
        axis, bit = bits[i]
        return ordered(v, flip(v, axis), bit, dim)

    def pick(v, i, dim=0):
        return lax.dynamic_index_in_dim(v, i, dim, keepdims=False)

    def for_z(pair, other, bit):
        blocks = []
        for s in range(4):
            z = (zi + s) % 4
            blocks.append(jnp.where(z // 2 == bit, pick(pair, z % 2), pick(other, z % 2)))
        return blocks

    def over_z(blocks):
        return [blocks[0]] + [shift(blocks[s], "z", s) for s in (1, 2, 3)]

    def gathered(blocks, f):
        parts = [v[None] for v in blocks] + ([] if f is None else [f.reshape(2, 256, B)])
        return lax.all_gather(jnp.concatenate(parts, 0), "y", axis=0, tiled=False)

    gate = lax.optimization_barrier
    e0 = jnp.swapaxes(dinv0.reshape(4, 4, B, B), 0, 1).reshape(4, 512, B)
    e1 = dinv1.reshape(2, 2, 256, B)
    e1_mine, e1_other = pick(e1, ci, 1), flip(pick(e1, 1 - ci, 1), "core")
    e0, e1_mine, e1_other = gate((e0, e1_mine, e1_other))
    e0 = lax.all_to_all(e0, "y", 0, 0, tiled=True)
    e1 = for_z(e1_mine, e1_other, ci)
    e1, off0 = gate((e1, off0.reshape(4, 256, B)))
    e1 = over_z(e1)
    fa, fb = shift(off0, "z", 1), shift(off0, "z", -1)
    e0, fa, fb, e1, dinv2, off2, dinv3, rhs0 = gate((e0, fa, fb, e1, dinv2, off2, dinv3, rhs0))
    m1 = gathered(e1, off1)

    ea, eb = shift(e0, "z", 1), shift(e0, "z", -1)
    e2 = dinv2.reshape(2, 256, B)
    e2 = ordered(pick(e2, ci)[None], flip(pick(e2, 1 - ci)[None], "core"), ci, 0)
    e2 = over_z(for_z(e2, flip(e2, "x0"), x0))
    f2 = joined(off2, 1)
    fc, fd = shift(fa[:2], "z", 1), shift(fb[2:], "z", -1)
    c0 = gather4(rhs0, "y")
    e2[0], ea, eb, fc, fd, c0 = gate((e2[0], ea, eb, fc, fd, c0))
    ec, ed = shift(ea[:2], "z", 1), shift(eb[2:], "z", -1)
    e3 = joined(dinv3[None], 1)
    e3_other = flip(e3, "x1")
    b_mine, b_other = halves(jnp.concatenate([rhs1, rhs2, rhs3], 1), ci)
    b_other = flip(b_other, "core")
    ec, ed, e2, f2, e3, e3_other, b_mine, b_other = gate(
        (ec, ed, e2, f2, e3, e3_other, b_mine, b_other)
    )
    m2 = gathered(e2, f2)
    w0 = [e0, ea, eb, ec, ed, off0, fa, fb, fc, fd]
    e3 = over_z(for_z(e3, e3_other, x1))
    e3, b_mine = gate((e3, b_mine))
    m3 = gathered(e3, None)

    dma = pltpu.SemaphoreType.DMA
    ev, fv = pltpu.VMEM((4, 4, 512, B), f32), pltpu.VMEM((4, 4, 256, B), f32)

    def work(n):
        return [pltpu.VMEM((n, ORDER), f32), pltpu.VMEM((n, 512), f32), pltpu.VMEM((n, 1024), f32)]

    def flops(n):
        return 2 * n * 512 * (2048 + 1024) * 12

    y0, *u = call(
        functools.partial(forward_kernel, 0, 64, "rs"), "f0", [(64, 512)] + [(16, 1024)] * 4,
        [ev, fv, *work(64), dma((10,))], meta, c0, w0, flops(64),
    )
    m1, _ = gate((m1, y0))
    w1 = m1, flip(m1, "core")
    parts = scatter4(u, "y")
    u = (parts[0] + parts[1]) + (parts[2] + parts[3])
    keep, give = halves(u, ci)
    c1, pk, pg = call(
        s01_kernel, "s01", [(8, ORDER), (2, 4, ORDER), (2, 4, ORDER)],
        [pltpu.VMEM((3, 8, ORDER), f32)], meta, [keep, flip(give, "core"), b_mine, b_other],
    )
    pr = flip(pg, "x0")
    y1, keep, give = call(
        functools.partial(forward_kernel, 1, 32, "ar"), "f1", [(32, 512), (16, 1024), (16, 1024)],
        [ev, fv, *work(32), dma((12,))], meta, gather4(c1, "z"), w1, flops(32),
    )
    part, keep3, give3 = call(
        s12_kernel, "s12", [(16, ORDER), (8, ORDER), (8, ORDER)],
        [pltpu.VMEM((2, 16, ORDER), f32)], meta, [keep, flip(give, "x0"), pk, pr],
    )
    m2, _ = gate((m2, part))
    w2 = m2, flip(m2, "core")
    recv3 = flip(give3, "x1")
    y2, keep, give = call(
        functools.partial(forward_kernel, 2, 16, "ar"), "f2", [(16, 512), (8, 1024), (8, 1024)],
        [ev, fv, *work(16), dma((12,))], meta, gather4(part, "z"), w2, flops(16),
    )
    (part,) = call(
        s23_kernel, "s23", [(8, ORDER)],
        [pltpu.VMEM((1, 8, ORDER), f32)], meta, [keep, flip(give, "x1"), keep3, recv3],
    )

    m3, _ = gate((m3, part))
    w3 = m3, flip(m3, "core")
    (part,) = call(
        top_kernel, "top", [(8, ORDER)], [ev, pltpu.VMEM((8, 512), f32), dma((8,))],
        meta, gather4(part, "z"), w3, flops(8),
    )
    x3, give = call(
        x3_kernel, "x3", [(8, ORDER), (8, 1024)], [pltpu.VMEM((1, 8, ORDER), f32)],
        meta, gather4(part, "z"),
    )
    recv = flip(give, "x1")
    x3r = flip(x3, "x1")

    def rest(n, small):
        return [ev, fv, pltpu.VMEM((n, 1024), f32), pltpu.VMEM((n // 2, 1024), f32), dma((12,))]

    (part,) = call(
        functools.partial(backward_kernel, 2, 16), "b2", [(16, ORDER)], rest(16, 0),
        meta, [x3[None], recv, y2], w2, flops(16),
    )
    anc, give = call(
        x2_kernel, "x2", [(2, 16, ORDER), (16, 1024)], [],
        meta, gather4(part, "z") + [x3, x3r],
    )
    recv = flip(give, "x0")
    a_mine = anc[:, :4]
    a_other = flip(a_mine, "x0")
    parts = call(
        functools.partial(backward_kernel, 1, 32), "b1", [(8, ORDER)] * 4, rest(32, 0),
        meta, [anc, recv, y1], w1, flops(32),
    )
    anc, give, own = call(
        x1_kernel, "x1", [(3, 8, ORDER), (8, 1024), (8, 1024)], [],
        meta, scatter4(parts, "z") + [a_mine, a_other],
    )
    g = ordered(own, flip(give, "core"), ci, 0)
    parts = call(
        functools.partial(backward_kernel, 0, 64), "b0", [(16, ORDER)] * 4, rest(64, 0),
        meta, gather4(g, "y") + [y0], w0, flops(64),
    )
    parts = scatter4(parts, "y")
    sol0 = (parts[0] + parts[1]) + (parts[2] + parts[3])

    outs = [sol0]
    for k in (1, 2, 3):
        width = ORDER // 2**k
        place = leaf % 2**k
        mine = lax.dynamic_slice_in_dim(anc[k - 1], place * width, width, 1)
        give = lax.dynamic_slice_in_dim(anc[k - 1], (place ^ 1) * width, width, 1)
        outs.append(ordered(mine, flip(give, "core"), ci, 0))
    return tuple(outs)


def solution(mesh):
    fine = Mesh(mesh.devices.reshape(2, 2, 2, 4, 4), ("x1", "x0", "core", "z", "y"))
    leaf, panel = ("x1", "x0", "core"), ("z", "y")
    return jax.shard_map(
        local,
        mesh=fine,
        in_specs=(P(), P()) + (P(panel, leaf),) * 4 + (P(leaf, panel),) * 7,
        out_specs=(P(panel, leaf),) * 4,
        check_vma=False,
    )
```

```python
import functools
import jax
import jax.numpy as jnp
from jax import lax
from jax.experimental import pallas as pl
from jax.experimental.pallas import tpu as pltpu
from jax.sharding import Mesh, PartitionSpec as P

B = 128
ORDER = 2048
NT = 16
f32 = jnp.float32
bf16 = jnp.bfloat16

FIRST = (0, 8, 12, 14)


class Place:
    def __init__(self, meta):
        self.meta = meta
        self.leaf = meta[0] >> 4
        self.zi, self.yi = (meta[0] >> 2) & 3, meta[0] & 3
        self.ci, self.x0, self.x1 = self.leaf & 1, (self.leaf >> 1) & 1, self.leaf >> 2

    def live(self, level):
        return self.meta[1 + FIRST[level] + (self.leaf >> level)]

    def own(self, level):
        return 16 + 8 * (FIRST[level] + (self.leaf >> level))

    def partner(self, level):
        return 16 + 8 * (FIRST[level] + ((self.leaf >> level) ^ 1))

    def bit(self, level):
        return (self.ci, self.x0, self.x1)[level]


def shift(v, axis, s):
    return lax.ppermute(v, axis, [(i, (i + s) % 4) for i in range(4)])


def flip(v, axis):
    return lax.ppermute(v, axis, [(0, 1), (1, 0)])


def gather4(v, axis):
    far = shift(v, axis, 2)
    return [v, shift(v, axis, 1), far, shift(v, axis, 3)]


def scatter4(parts, axis):
    far = shift(parts[2], axis, 2)
    return [parts[0], shift(parts[1], axis, -1), far, shift(parts[3], axis, 1)]


def ring(v, axis, dim):
    h = v.shape[dim] // 2
    a = shift(v, axis, 1)
    b = shift(v, axis, -1)
    c = shift(lax.slice_in_dim(a, 0, h, axis=dim), axis, 1)
    d = shift(lax.slice_in_dim(b, h, 2 * h, axis=dim), axis, -1)
    return [v, a, b, c, d]


def ordered(mine, other, bit, dim):
    return jnp.where(
        bit == 0, jnp.concatenate([mine, other], dim), jnp.concatenate([other, mine], dim)
    )


def halves(v, bit):
    h = v.shape[0] // 2
    return (
        jnp.where(bit == 0, v[:h], v[h:]),
        jnp.where(bit == 0, v[h:], v[:h]),
    )


def stacked(v):
    hi = v.astype(bf16).astype(f32)
    return jnp.concatenate([hi, v - hi], 0).astype(bf16)


def product(left, w, dims):
    hi = w.astype(bf16)
    lo = (w - hi.astype(f32)).astype(bf16)
    r = lax.dot_general(left, hi, (dims, ((), ())), preferred_element_type=f32)
    r = r + lax.dot_general(left, lo, (dims, ((), ())), preferred_element_type=f32)
    n = left.shape[0] // 2
    return r[:n] + r[n:]


NTD = ((1,), (1,))
NND = ((1,), (0,))


def copies_first(meta, refs, ev, fv, sems):
    e, f = refs[:5], refs[5:]
    zi = Place(meta).zi
    spots = [zi, lax.rem(zi + 3, 4), lax.rem(zi + 1, 4)]
    far = lax.rem(zi + 2, 4)
    pairs_e = [(ref, ev.at[w]) for ref, w in zip(e[:3], spots)]
    pairs_e += [(e[3], ev.at[far, 0:2]), (e[4], ev.at[far, 2:4])]
    pairs_f = [(ref, fv.at[w]) for ref, w in zip(f[:3], spots)]
    pairs_f += [(f[3], fv.at[far, 0:2]), (f[4], fv.at[far, 2:4])]
    made = [
        pltpu.make_async_copy(src, dst, sems.at[k]) for k, (src, dst) in enumerate(pairs_e + pairs_f)
    ]
    return made[:5], [], made[5:]


def copies_upper(level, meta, bufs, ev, fv, sems):
    place = Place(meta)
    groups = ([], [], [])
    k = 0
    for i, q in ((0, place.ci), (1, 1 - place.ci)):
        rows = pl.ds(pl.multiple_of(q * 256, 256), 256)
        pairs = [(bufs[i].at[:, s], ev.at[:, lax.rem(place.zi + 4 - s, 4), rows]) for s in range(4)]
        late = []
        if level == 1:
            late = [(bufs[i].at[:, 4:6], fv.at[:, pl.ds(2 * q, 2)])]
        elif level == 2:
            late = [(bufs[i].at[:, 4 + h], fv.at[:, 2 * h + q]) for h in (0, 1)]
        for group, some in ((groups[i], pairs), (groups[2], late)):
            for src, dst in some:
                group.append(pltpu.make_async_copy(src, dst, sems.at[k]))
                k += 1
    return groups


def copies(level, meta, refs, ev, fv, sems):
    if level == 0:
        return copies_first(meta, refs, ev, fv, sems)
    return copies_upper(level, meta, refs, ev, fv, sems)


def finish(group):
    for c in group:
        c.wait()


def tiles_in_order(level):
    if level == 0:
        return [(t // 4, t % 4) for t in range(NT)]
    return [(t % 4, t // 4) for t in range(NT)]


def column_mask(meta, level, n):
    col = lax.broadcasted_iota(jnp.int32, (n, ORDER), 1)
    return col < Place(meta).live(level) * B


def row_mask(meta, level, n):
    own = lax.broadcasted_iota(jnp.int32, (n, 512), 1) // B
    place = Place(meta)
    tile = 4 * own + place.yi if level == 0 else 4 * place.zi + own
    return tile < Place(meta).live(level)


def solve_rows(level, meta, ev, yv, cs, late):
    first = Place(meta).ci if level else 0

    def body(j, carry):
        @pl.when(j == 1)
        def _():
            finish(late)

        at = pl.multiple_of(jnp.where(j == 0, first, 1 - first) * 256, 256)
        rows = pl.ds(at, 256)
        w = jnp.concatenate([ev[w, s, rows, :] for w, s in tiles_in_order(level)], 1)
        yv[:, rows] = product(cs, w, NTD)
        return carry

    lax.fori_loop(0, 2, body, 0)


WEIGHTS = (10, 2, 2, 2)


def forward_kernel(level, n, mode, meta, *refs):
    count = WEIGHTS[level]
    c_refs, refs = refs[:4], refs[4:]
    w_refs, refs = refs[:count], refs[count:]
    if mode == "rs":
        y_out, u_out = refs[0], refs[1:5]
        refs = refs[5:]
    else:
        y_out, keep_out, give_out = refs[:3]
        refs = refs[3:]
    ev, fv, cv, yv, uv, sems = refs
    early, late, last = copies(level, meta, w_refs, ev, fv, sems)
    for c in [*early, *late, *last]:
        c.start()
    r = n // 4
    if level < 2:
        for s in range(4):
            cv[pl.ds(s * r, r), :] = c_refs[s][...]
        c = cv[...]
    else:
        c = summed(c_refs, r)
    cs = stacked(jnp.where(column_mask(meta, level, n), c, 0.0))
    finish(early)
    solve_rows(level, meta, ev, yv, cs, late)
    y = jnp.where(row_mask(meta, level, n), yv[...], 0.0)
    y_out[...] = y
    ys = stacked(y)
    finish(last)

    def body(j, carry):
        w = jnp.concatenate([fv[w, j] for w in range(4)], 1)
        uv[:, pl.ds(pl.multiple_of(j * 256, 256), 256)] = product(ys, w, NTD)
        return carry

    lax.fori_loop(0, 4, body, 0)
    if mode == "rs":
        for s in range(4):
            u_out[s][...] = uv[pl.ds(s * r, r), :]
    else:
        split_rows(uv, r, Place(meta).bit(level), keep_out, give_out)


def split_rows(v, r, bit, keep_out, give_out):
    h = r // 2
    for s in range(4):
        low = v[pl.ds(s * r, h), :]
        high = v[pl.ds(s * r + h, h), :]
        keep_out[pl.ds(s * h, h), :] = jnp.where(bit == 0, low, high)
        give_out[pl.ds(s * h, h), :] = jnp.where(bit == 0, high, low)


def summed(refs, r):
    parts = []
    for s in range(4):
        total = refs[0][pl.ds(s * r, r), :]
        for d in (1, 2, 3):
            total = total + refs[d][pl.ds((s - d) % 4 * r, r), :]
        parts.append(total)
    return jnp.concatenate(parts, 0)


def add_tiles(meta, at, src, acc):
    for t in range(8):
        v = meta[at + t]
        cols = pl.ds(pl.multiple_of(lax.rem(v, NT) * B, B), B)
        lev = lax.div(v, NT)
        acc[lev, :, cols] = acc[lev, :, cols] + src[:, t * B : (t + 1) * B]


def take_tiles(meta, at, anc, dst):
    for t in range(8):
        v = meta[at + t]
        cols = pl.ds(pl.multiple_of(lax.rem(v, NT) * B, B), B)
        dst[:, t * B : (t + 1) * B] = anc[lax.div(v, NT), :, cols]


def s01_kernel(meta, keep, recv, b_mine, b_other, c1, pk, pg, acc):
    place = Place(meta)
    acc[...] = jnp.zeros_like(acc)
    add_tiles(meta, place.own(0), keep, acc)
    add_tiles(meta, place.partner(0), recv, acc)
    group = (0, place.x0, place.leaf >> 1)
    for ref, c in ((b_mine, place.ci), (b_other, 1 - place.ci)):
        at = 0
        for i in range(3):
            width = 1024 >> i
            cols = pl.ds(pl.multiple_of((2 * group[i] + c) * width, width), width)
            acc[i, :, cols] = acc[i, :, cols] - ref[:, at : at + width]
            at += width
    c1[...] = -acc[0]
    for i in (0, 1):
        low, high = acc[i + 1, 0:4, :], acc[i + 1, 4:8, :]
        pk[i] = jnp.where(place.x0 == 0, low, high)
        pg[i] = jnp.where(place.x0 == 0, high, low)


def s12_kernel(meta, keep, recv, pk, pr, part, keep3, give3, acc):
    place = Place(meta)
    acc[...] = jnp.zeros_like(acc)
    add_tiles(meta, place.own(1), keep, acc)
    add_tiles(meta, place.partner(1), recv, acc)
    for i in (0, 1):
        acc[i, 0:4, :] = acc[i, 0:4, :] + (pk[i] + pr[i])
    part[...] = -acc[0]
    split_rows(acc.at[1], 4, place.x1, keep3, give3)


def s23_kernel(meta, keep, recv, keep3, recv3, part, acc):
    place = Place(meta)
    acc[...] = jnp.zeros_like(acc)
    add_tiles(meta, place.own(2), keep, acc)
    add_tiles(meta, place.partner(2), recv, acc)
    part[...] = -(acc[0] + (keep3[...] + recv3[...]))


def top_kernel(meta, c0, c1, c2, c3, *refs):
    w_refs, (x_out, ev, yv, sems) = refs[:2], refs[2:]
    early, late, _ = copies(3, meta, w_refs, ev, None, sems)
    for c in [*early, *late]:
        c.start()
    c = summed((c0, c1, c2, c3), 2)
    cs = stacked(jnp.where(column_mask(meta, 3, 8), c, 0.0))
    finish(early)
    solve_rows(3, meta, ev, yv, cs, late)
    back(meta, 3, 8, ev, jnp.where(row_mask(meta, 3, 8), yv[...], 0.0), [x_out])


def back(meta, level, n, ev, z, x_out):
    zs = stacked(z)
    live = Place(meta).live(level) * B

    def body(j, carry):
        cols = pl.ds(pl.multiple_of(j * 512, 512), 512)
        w = jnp.concatenate([ev[j, i] if level == 0 else ev[i, j] for i in range(4)], 1)
        v = product(zs, w, NND)
        col = lax.broadcasted_iota(jnp.int32, (n, 512), 1) + j * 512
        v = jnp.where(col < live, v, 0.0)
        r = n // len(x_out)
        for s, out in enumerate(x_out):
            out[:, cols] = v[s * r : (s + 1) * r]
        return carry

    lax.fori_loop(0, 4, body, 0)


def x3_kernel(meta, c0, c1, c2, c3, x_out):
    x_out[...] = summed((c0, c1, c2, c3), 2)


def merged(a, b, h, bit):
    parts = []
    for s in range(4):
        u, v = a[s * h : (s + 1) * h, :], b[s * h : (s + 1) * h, :]
        parts += [jnp.where(bit == 0, u, v), jnp.where(bit == 0, v, u)]
    return jnp.concatenate(parts, 0)


def x2_kernel(meta, c0, c1, c2, c3, x3, x3r, anc_out, give):
    anc_out[0] = summed((c0, c1, c2, c3), 4)
    anc_out[1] = merged(x3[...], x3r[...], 2, Place(meta).x1)
    take_tiles(meta, Place(meta).partner(1), anc_out, give)


def x1_kernel(meta, c0, c1, c2, c3, a_mine, a_other, anc_out, give, own):
    anc_out[0] = (c0[...] + c1[...]) + (c2[...] + c3[...])
    for i in (0, 1):
        u, v = a_mine[i], a_other[i]
        bit = Place(meta).x0
        anc_out[i + 1, 0:4, :] = jnp.where(bit == 0, u, v)
        anc_out[i + 1, 4:8, :] = jnp.where(bit == 0, v, u)
    take_tiles(meta, Place(meta).partner(0), anc_out, give)
    take_tiles(meta, Place(meta).own(0), anc_out, own)


def backward_kernel(level, n, meta, *refs):
    count = WEIGHTS[level]
    if level == 0:
        g_refs, refs = refs[:4], refs[4:]
    else:
        (anc, recv), refs = refs[:2], refs[2:]
    y_ref, refs = refs[0], refs[1:]
    w_refs, refs = refs[:count], refs[count:]
    x_out, (ev, fv, gv, ov, sems) = refs[:-5], refs[-5:]
    early, late, first = copies(level, meta, w_refs, ev, fv, sems)
    for c in [*first, *early, *late]:
        c.start()
    r = n // 4
    if level == 0:
        for s in range(4):
            gv[pl.ds(s * r, r), :] = g_refs[s][...]
        g = gv[...]
    else:
        take_tiles(meta, Place(meta).own(level), anc, ov)
        if level == 2:
            take_tiles(meta, Place(meta).own(level), recv, gv)
            recv = gv
        g = merged(ov[...], recv[...], r // 2, Place(meta).bit(level))
    gs = stacked(g)
    finish(first)
    w = jnp.concatenate([fv[w].reshape(1024, B) for w in range(4)], 1)
    z = y_ref[...] - product(gs, w, NND)
    z = jnp.where(row_mask(meta, level, n), z, 0.0)
    finish(early)
    finish(late)
    back(meta, level, n, ev, z, x_out)


SMEM = pl.BlockSpec(memory_space=pltpu.SMEM)
VMEM = pl.BlockSpec(memory_space=pltpu.VMEM)
ANY = pl.BlockSpec(memory_space=pl.ANY)


def call(kernel, name, shapes, scratch, meta, small, weights=(), flops=0):
    weights = [pltpu.with_memory_space_constraint(w, pltpu.HBM) for w in weights]
    moved = sum(w.size * 4 for w in weights) + sum(v.size * 4 for v in small)
    return pl.pallas_call(
        kernel,
        out_shape=[jax.ShapeDtypeStruct(s, f32) for s in shapes],
        in_specs=[SMEM] + [VMEM] * len(small) + [ANY] * len(weights),
        out_specs=[VMEM] * len(shapes),
        scratch_shapes=scratch,
        compiler_params=pltpu.CompilerParams(vmem_limit_bytes=(14 if flops else 3) * 2**20),
        cost_estimate=pl.CostEstimate(flops=flops, bytes_accessed=moved, transcendentals=0),
        name=name,
    )(meta, *small, *weights)


def local(
    live_tiles, row_tiles, rhs0, rhs1, rhs2, rhs3, dinv0, dinv1, dinv2, dinv3, off0, off1, off2
):
    ci, x0, x1 = lax.axis_index("core"), lax.axis_index("x0"), lax.axis_index("x1")
    zi = lax.axis_index("z")
    leaf = x1 * 4 + x0 * 2 + ci
    here = leaf * 16 + zi * 4 + lax.axis_index("y")
    meta = jnp.concatenate([here.reshape(1), live_tiles, row_tiles.reshape(-1)])
    bits = [("core", ci), ("x0", x0), ("x1", x1)]

    def joined(v, i, dim=0):
        axis, bit = bits[i]
        return ordered(v, flip(v, axis), bit, dim)

    def pick(v, i, dim=0):
        return lax.dynamic_index_in_dim(v, i, dim, keepdims=False)

    def for_z(pair, other, bit):
        blocks = []
        for s in range(4):
            z = (zi + s) % 4
            blocks.append(jnp.where(z // 2 == bit, pick(pair, z % 2), pick(other, z % 2)))
        return blocks

    def over_z(blocks):
        return [blocks[0]] + [shift(blocks[s], "z", s) for s in (1, 2, 3)]

    def gathered(blocks, f):
        parts = [v[None] for v in blocks] + ([] if f is None else [f.reshape(2, 256, B)])
        return lax.all_gather(jnp.concatenate(parts, 0), "y", axis=0, tiled=False)

    gate = lax.optimization_barrier
    e0 = jnp.swapaxes(dinv0.reshape(4, 4, B, B), 0, 1).reshape(4, 512, B)
    e1 = dinv1.reshape(2, 2, 256, B)
    e1_mine, e1_other = pick(e1, ci, 1), flip(pick(e1, 1 - ci, 1), "core")
    e0, e1_mine, e1_other, dinv2, rhs0 = gate((e0, e1_mine, e1_other, dinv2, rhs0))
    e0 = lax.all_to_all(e0, "y", 0, 0, tiled=True)
    e1 = over_z(for_z(e1_mine, e1_other, ci))
    e2 = dinv2.reshape(2, 256, B)
    e2 = ordered(pick(e2, ci)[None], flip(pick(e2, 1 - ci)[None], "core"), ci, 0)
    e2_other = flip(e2, "x0")
    e0, e1, e2, e2_other, off0, off2, dinv3, rhs0 = gate(
        (e0, e1, e2, e2_other, off0.reshape(4, 256, B), off2, dinv3, rhs0)
    )
    m1 = gathered(e1, off1)

    fa, fb = shift(off0, "z", 1), shift(off0, "z", -1)
    ea, eb = shift(e0, "z", 1), shift(e0, "z", -1)
    e2 = over_z(for_z(e2, e2_other, x0))
    f2 = joined(off2, 1)
    fc, fd = shift(fa[:2], "z", 1), shift(fb[2:], "z", -1)
    c0 = gather4(rhs0, "y")
    e2, f2, ea, eb, fc, fd, c0 = gate((e2, f2, ea, eb, fc, fd, c0))

    ec, ed = shift(ea[:2], "z", 1), shift(eb[2:], "z", -1)
    m2 = gathered(e2, f2)
    e3 = joined(dinv3[None], 1)
    e3_other = flip(e3, "x1")
    b_mine, b_other = halves(jnp.concatenate([rhs1, rhs2, rhs3], 1), ci)
    b_other = flip(b_other, "core")
    ec, ed, e3, e3_other, b_mine, b_other = gate((ec, ed, e3, e3_other, b_mine, b_other))
    w0 = [e0, ea, eb, ec, ed, off0, fa, fb, fc, fd]
    e3 = over_z(for_z(e3, e3_other, x1))
    e3, b_mine = gate((e3, b_mine))
    m3 = gathered(e3, None)

    dma = pltpu.SemaphoreType.DMA
    ev, fv = pltpu.VMEM((4, 4, 512, B), f32), pltpu.VMEM((4, 4, 256, B), f32)

    def work(n):
        return [pltpu.VMEM((n, ORDER), f32), pltpu.VMEM((n, 512), f32), pltpu.VMEM((n, 1024), f32)]

    def flops(n):
        return 2 * n * 512 * (2048 + 1024) * 12

    y0, *u = call(
        functools.partial(forward_kernel, 0, 64, "rs"), "f0", [(64, 512)] + [(16, 1024)] * 4,
        [ev, fv, *work(64), dma((10,))], meta, c0, w0, flops(64),
    )
    m1, _ = gate((m1, y0))
    w1 = m1, flip(m1, "core")
    parts = scatter4(u, "y")
    u = (parts[0] + parts[1]) + (parts[2] + parts[3])
    keep, give = halves(u, ci)
    c1, pk, pg = call(
        s01_kernel, "s01", [(8, ORDER), (2, 4, ORDER), (2, 4, ORDER)],
        [pltpu.VMEM((3, 8, ORDER), f32)], meta, [keep, flip(give, "core"), b_mine, b_other],
    )
    pr = flip(pg, "x0")
    y1, keep, give = call(
        functools.partial(forward_kernel, 1, 32, "ar"), "f1", [(32, 512), (16, 1024), (16, 1024)],
        [ev, fv, *work(32), dma((12,))], meta, gather4(c1, "z"), w1, flops(32),
    )
    part, keep3, give3 = call(
        s12_kernel, "s12", [(16, ORDER), (8, ORDER), (8, ORDER)],
        [pltpu.VMEM((2, 16, ORDER), f32)], meta, [keep, flip(give, "x0"), pk, pr],
    )
    m2, _ = gate((m2, part))
    w2 = m2, flip(m2, "core")
    recv3 = flip(give3, "x1")
    y2, keep, give = call(
        functools.partial(forward_kernel, 2, 16, "ar"), "f2", [(16, 512), (8, 1024), (8, 1024)],
        [ev, fv, *work(16), dma((12,))], meta, gather4(part, "z"), w2, flops(16),
    )
    (part,) = call(
        s23_kernel, "s23", [(8, ORDER)],
        [pltpu.VMEM((1, 8, ORDER), f32)], meta, [keep, flip(give, "x1"), keep3, recv3],
    )

    m3, _ = gate((m3, part))
    w3 = m3, flip(m3, "core")
    (part,) = call(
        top_kernel, "top", [(8, ORDER)], [ev, pltpu.VMEM((8, 512), f32), dma((8,))],
        meta, gather4(part, "z"), w3, flops(8),
    )
    (x3,) = call(x3_kernel, "x3", [(8, ORDER)], [], meta, gather4(part, "z"))
    x3r = flip(x3, "x1")

    def rest(n):
        rows = n if n != 16 else 8
        return [ev, fv, pltpu.VMEM((rows, 1024), f32), pltpu.VMEM((n // 2, 1024), f32), dma((12,))]

    (part,) = call(
        functools.partial(backward_kernel, 2, 16), "b2", [(16, ORDER)], rest(16),
        meta, [x3[None], x3r[None], y2], w2, flops(16),
    )
    anc, give = call(
        x2_kernel, "x2", [(2, 16, ORDER), (16, 1024)], [],
        meta, gather4(part, "z") + [x3, x3r],
    )
    recv = flip(give, "x0")
    a_mine = anc[:, :4]
    a_other = flip(a_mine, "x0")
    parts = call(
        functools.partial(backward_kernel, 1, 32), "b1", [(8, ORDER)] * 4, rest(32),
        meta, [anc, recv, y1], w1, flops(32),
    )
    anc, give, own = call(
        x1_kernel, "x1", [(3, 8, ORDER), (8, 1024), (8, 1024)], [],
        meta, scatter4(parts, "z") + [a_mine, a_other],
    )
    g = ordered(own, flip(give, "core"), ci, 0)
    parts = call(
        functools.partial(backward_kernel, 0, 64), "b0", [(16, ORDER)] * 4, rest(64),
        meta, gather4(g, "y") + [y0], w0, flops(64),
    )
    parts = scatter4(parts, "y")
    sol0 = (parts[0] + parts[1]) + (parts[2] + parts[3])

    outs = [sol0]
    for k in (1, 2, 3):
        width = ORDER // 2**k
        place = leaf % 2**k
        mine = lax.dynamic_slice_in_dim(anc[k - 1], place * width, width, 1)
        give = lax.dynamic_slice_in_dim(anc[k - 1], (place ^ 1) * width, width, 1)
        outs.append(ordered(mine, flip(give, "core"), ci, 0))
    return tuple(outs)


def solution(mesh):
    fine = Mesh(mesh.devices.reshape(2, 2, 2, 4, 4), ("x1", "x0", "core", "z", "y"))
    leaf, panel = ("x1", "x0", "core"), ("z", "y")
    return jax.shard_map(
        local,
        mesh=fine,
        in_specs=(P(), P()) + (P(panel, leaf),) * 4 + (P(leaf, panel),) * 7,
        out_specs=(P(panel, leaf),) * 4,
        check_vma=False,
    )
```

```python
import functools
import jax
import jax.numpy as jnp
from jax import lax
from jax.experimental import pallas as pl
from jax.experimental.pallas import tpu as pltpu
from jax.sharding import Mesh, PartitionSpec as P

B = 128
ORDER = 2048
NT = 16
f32 = jnp.float32
bf16 = jnp.bfloat16

FIRST = (0, 8, 12, 14)


class Place:
    def __init__(self, meta):
        self.meta = meta
        self.leaf = meta[0] >> 4
        self.zi, self.yi = (meta[0] >> 2) & 3, meta[0] & 3
        self.ci, self.x0, self.x1 = self.leaf & 1, (self.leaf >> 1) & 1, self.leaf >> 2

    def live(self, level):
        return self.meta[1 + FIRST[level] + (self.leaf >> level)]

    def own(self, level):
        return 16 + 8 * (FIRST[level] + (self.leaf >> level))

    def partner(self, level):
        return 16 + 8 * (FIRST[level] + ((self.leaf >> level) ^ 1))

    def bit(self, level):
        return (self.ci, self.x0, self.x1)[level]


def shift(v, axis, s):
    return lax.ppermute(v, axis, [(i, (i + s) % 4) for i in range(4)])


def flip(v, axis):
    return lax.ppermute(v, axis, [(0, 1), (1, 0)])


def gather4(v, axis):
    far = shift(v, axis, 2)
    return [v, shift(v, axis, 1), far, shift(v, axis, 3)]


def scatter4(parts, axis):
    far = shift(parts[2], axis, 2)
    return [parts[0], shift(parts[1], axis, -1), far, shift(parts[3], axis, 1)]


def ring(v, axis, dim):
    h = v.shape[dim] // 2
    a = shift(v, axis, 1)
    b = shift(v, axis, -1)
    c = shift(lax.slice_in_dim(a, 0, h, axis=dim), axis, 1)
    d = shift(lax.slice_in_dim(b, h, 2 * h, axis=dim), axis, -1)
    return [v, a, b, c, d]


def ordered(mine, other, bit, dim):
    return jnp.where(
        bit == 0, jnp.concatenate([mine, other], dim), jnp.concatenate([other, mine], dim)
    )


def halves(v, bit):
    h = v.shape[0] // 2
    return (
        jnp.where(bit == 0, v[:h], v[h:]),
        jnp.where(bit == 0, v[h:], v[:h]),
    )


def stacked(v):
    hi = v.astype(bf16).astype(f32)
    return jnp.concatenate([hi, v - hi], 0).astype(bf16)


def product(left, w, dims):
    hi = w.astype(bf16)
    lo = (w - hi.astype(f32)).astype(bf16)
    r = lax.dot_general(left, hi, (dims, ((), ())), preferred_element_type=f32)
    r = r + lax.dot_general(left, lo, (dims, ((), ())), preferred_element_type=f32)
    n = left.shape[0] // 2
    return r[:n] + r[n:]


NTD = ((1,), (1,))
NND = ((1,), (0,))


def copies_first(meta, refs, ev, fv, sems):
    e, f = refs[:5], refs[5:]
    zi = Place(meta).zi
    spots = [zi, lax.rem(zi + 3, 4), lax.rem(zi + 1, 4)]
    far = lax.rem(zi + 2, 4)
    pairs_e = [(ref, ev.at[w]) for ref, w in zip(e[:3], spots)]
    pairs_e += [(e[3], ev.at[far, 0:2]), (e[4], ev.at[far, 2:4])]
    pairs_f = [(ref, fv.at[w]) for ref, w in zip(f[:3], spots)]
    pairs_f += [(f[3], fv.at[far, 0:2]), (f[4], fv.at[far, 2:4])]
    made = [
        pltpu.make_async_copy(src, dst, sems.at[k]) for k, (src, dst) in enumerate(pairs_e + pairs_f)
    ]
    return made[:5], [], made[5:]


def copies_upper(level, meta, bufs, ev, fv, sems):
    place = Place(meta)
    groups = ([], [], [])
    k = 0
    for i, q in ((0, place.ci), (1, 1 - place.ci)):
        rows = pl.ds(pl.multiple_of(q * 256, 256), 256)
        pairs = [(bufs[i].at[:, s], ev.at[:, lax.rem(place.zi + 4 - s, 4), rows]) for s in range(4)]
        late = []
        if level == 1:
            late = [(bufs[i].at[:, 4:6], fv.at[:, pl.ds(2 * q, 2)])]
        elif level == 2:
            late = [(bufs[i].at[:, 4 + h], fv.at[:, 2 * h + q]) for h in (0, 1)]
        for group, some in ((groups[i], pairs), (groups[2], late)):
            for src, dst in some:
                group.append(pltpu.make_async_copy(src, dst, sems.at[k]))
                k += 1
    return groups


def copies(level, meta, refs, ev, fv, sems):
    if level == 0:
        return copies_first(meta, refs, ev, fv, sems)
    return copies_upper(level, meta, refs, ev, fv, sems)


def finish(group):
    for c in group:
        c.wait()


def tiles_in_order(level):
    if level == 0:
        return [(t // 4, t % 4) for t in range(NT)]
    return [(t % 4, t // 4) for t in range(NT)]


def column_mask(meta, level, n):
    col = lax.broadcasted_iota(jnp.int32, (n, ORDER), 1)
    return col < Place(meta).live(level) * B


def row_mask(meta, level, n):
    own = lax.broadcasted_iota(jnp.int32, (n, 512), 1) // B
    place = Place(meta)
    tile = 4 * own + place.yi if level == 0 else 4 * place.zi + own
    return tile < Place(meta).live(level)


def solve_rows(level, meta, ev, yv, cs, late):
    first = Place(meta).ci if level else 0

    def body(j, carry):
        @pl.when(j == 1)
        def _():
            finish(late)

        at = pl.multiple_of(jnp.where(j == 0, first, 1 - first) * 256, 256)
        rows = pl.ds(at, 256)
        w = jnp.concatenate([ev[w, s, rows, :] for w, s in tiles_in_order(level)], 1)
        yv[:, rows] = product(cs, w, NTD)
        return carry

    lax.fori_loop(0, 2, body, 0)


WEIGHTS = (10, 2, 2, 2)


def forward_kernel(level, n, mode, meta, *refs):
    count = WEIGHTS[level]
    c_refs, refs = refs[:4], refs[4:]
    w_refs, refs = refs[:count], refs[count:]
    if mode == "rs":
        y_out, u_out = refs[0], refs[1:5]
        refs = refs[5:]
    else:
        y_out, keep_out, give_out = refs[:3]
        refs = refs[3:]
    ev, fv, cv, yv, uv, sems = refs
    early, late, last = copies(level, meta, w_refs, ev, fv, sems)
    for c in [*early, *late, *last]:
        c.start()
    r = n // 4
    if level < 2:
        for s in range(4):
            cv[pl.ds(s * r, r), :] = c_refs[s][...]
        c = cv[...]
    else:
        c = summed(c_refs, r)
    cs = stacked(jnp.where(column_mask(meta, level, n), c, 0.0))
    finish(early)
    solve_rows(level, meta, ev, yv, cs, late)
    y = jnp.where(row_mask(meta, level, n), yv[...], 0.0)
    y_out[...] = y
    ys = stacked(y)
    finish(last)

    def body(j, carry):
        w = jnp.concatenate([fv[w, j] for w in range(4)], 1)
        uv[:, pl.ds(pl.multiple_of(j * 256, 256), 256)] = product(ys, w, NTD)
        return carry

    lax.fori_loop(0, 4, body, 0)
    if mode == "rs":
        for s in range(4):
            u_out[s][...] = uv[pl.ds(s * r, r), :]
    else:
        split_rows(uv, r, Place(meta).bit(level), keep_out, give_out)


def split_rows(v, r, bit, keep_out, give_out):
    h = r // 2
    for s in range(4):
        low = v[pl.ds(s * r, h), :]
        high = v[pl.ds(s * r + h, h), :]
        keep_out[pl.ds(s * h, h), :] = jnp.where(bit == 0, low, high)
        give_out[pl.ds(s * h, h), :] = jnp.where(bit == 0, high, low)


def summed(refs, r):
    parts = []
    for s in range(4):
        total = refs[0][pl.ds(s * r, r), :]
        for d in (1, 2, 3):
            total = total + refs[d][pl.ds((s - d) % 4 * r, r), :]
        parts.append(total)
    return jnp.concatenate(parts, 0)


def add_tiles(meta, at, src, acc):
    for t in range(8):
        v = meta[at + t]
        cols = pl.ds(pl.multiple_of(lax.rem(v, NT) * B, B), B)
        lev = lax.div(v, NT)
        acc[lev, :, cols] = acc[lev, :, cols] + src[:, t * B : (t + 1) * B]


def take_tiles(meta, at, anc, dst):
    for t in range(8):
        v = meta[at + t]
        cols = pl.ds(pl.multiple_of(lax.rem(v, NT) * B, B), B)
        dst[:, t * B : (t + 1) * B] = anc[lax.div(v, NT), :, cols]


def s01_kernel(meta, keep, recv, b_mine, b_other, c1, pk, pg, acc):
    place = Place(meta)
    acc[...] = jnp.zeros_like(acc)
    add_tiles(meta, place.own(0), keep, acc)
    add_tiles(meta, place.partner(0), recv, acc)
    group = (0, place.x0, place.leaf >> 1)
    for ref, c in ((b_mine, place.ci), (b_other, 1 - place.ci)):
        at = 0
        for i in range(3):
            width = 1024 >> i
            cols = pl.ds(pl.multiple_of((2 * group[i] + c) * width, width), width)
            acc[i, :, cols] = acc[i, :, cols] - ref[:, at : at + width]
            at += width
    c1[...] = -acc[0]
    for i in (0, 1):
        low, high = acc[i + 1, 0:4, :], acc[i + 1, 4:8, :]
        pk[i] = jnp.where(place.x0 == 0, low, high)
        pg[i] = jnp.where(place.x0 == 0, high, low)


def s12_kernel(meta, keep, recv, pk, pr, part, keep3, give3, acc):
    place = Place(meta)
    acc[...] = jnp.zeros_like(acc)
    add_tiles(meta, place.own(1), keep, acc)
    add_tiles(meta, place.partner(1), recv, acc)
    for i in (0, 1):
        acc[i, 0:4, :] = acc[i, 0:4, :] + (pk[i] + pr[i])
    part[...] = -acc[0]
    split_rows(acc.at[1], 4, place.x1, keep3, give3)


def s23_kernel(meta, keep, recv, keep3, recv3, part, acc):
    place = Place(meta)
    acc[...] = jnp.zeros_like(acc)
    add_tiles(meta, place.own(2), keep, acc)
    add_tiles(meta, place.partner(2), recv, acc)
    part[...] = -(acc[0] + (keep3[...] + recv3[...]))


def top_kernel(meta, c0, c1, c2, c3, *refs):
    w_refs, (x_out, ev, yv, sems) = refs[:2], refs[2:]
    early, late, _ = copies(3, meta, w_refs, ev, None, sems)
    for c in [*early, *late]:
        c.start()
    c = summed((c0, c1, c2, c3), 2)
    cs = stacked(jnp.where(column_mask(meta, 3, 8), c, 0.0))
    finish(early)
    solve_rows(3, meta, ev, yv, cs, late)
    back(meta, 3, 8, ev, jnp.where(row_mask(meta, 3, 8), yv[...], 0.0), [x_out])


def back(meta, level, n, ev, z, x_out):
    zs = stacked(z)
    live = Place(meta).live(level) * B

    def body(j, carry):
        cols = pl.ds(pl.multiple_of(j * 512, 512), 512)
        w = jnp.concatenate([ev[j, i] if level == 0 else ev[i, j] for i in range(4)], 1)
        v = product(zs, w, NND)
        col = lax.broadcasted_iota(jnp.int32, (n, 512), 1) + j * 512
        v = jnp.where(col < live, v, 0.0)
        r = n // len(x_out)
        for s, out in enumerate(x_out):
            out[:, cols] = v[s * r : (s + 1) * r]
        return carry

    lax.fori_loop(0, 4, body, 0)


def x3_kernel(meta, c0, c1, c2, c3, x_out):
    x_out[...] = summed((c0, c1, c2, c3), 2)


def merged(a, b, h, bit):
    parts = []
    for s in range(4):
        u, v = a[s * h : (s + 1) * h, :], b[s * h : (s + 1) * h, :]
        parts += [jnp.where(bit == 0, u, v), jnp.where(bit == 0, v, u)]
    return jnp.concatenate(parts, 0)


def x2_kernel(meta, c0, c1, c2, c3, x3, x3r, anc_out, give):
    anc_out[0] = summed((c0, c1, c2, c3), 4)
    anc_out[1] = merged(x3[...], x3r[...], 2, Place(meta).x1)
    take_tiles(meta, Place(meta).partner(1), anc_out, give)


def x1_kernel(meta, c0, c1, c2, c3, a_mine, a_other, anc_out, give, own):
    anc_out[0] = (c0[...] + c1[...]) + (c2[...] + c3[...])
    for i in (0, 1):
        u, v = a_mine[i], a_other[i]
        bit = Place(meta).x0
        anc_out[i + 1, 0:4, :] = jnp.where(bit == 0, u, v)
        anc_out[i + 1, 4:8, :] = jnp.where(bit == 0, v, u)
    take_tiles(meta, Place(meta).partner(0), anc_out, give)
    take_tiles(meta, Place(meta).own(0), anc_out, own)


def backward_kernel(level, n, meta, *refs):
    count = WEIGHTS[level]
    if level == 0:
        g_refs, refs = refs[:4], refs[4:]
    else:
        (anc, recv), refs = refs[:2], refs[2:]
    y_ref, refs = refs[0], refs[1:]
    w_refs, refs = refs[:count], refs[count:]
    x_out, (ev, fv, gv, ov, sems) = refs[:-5], refs[-5:]
    early, late, first = copies(level, meta, w_refs, ev, fv, sems)
    for c in [*first, *early, *late]:
        c.start()
    r = n // 4
    if level == 0:
        for s in range(4):
            gv[pl.ds(s * r, r), :] = g_refs[s][...]
        g = gv[...]
    else:
        take_tiles(meta, Place(meta).own(level), anc, ov)
        if level == 2:
            take_tiles(meta, Place(meta).own(level), recv, gv)
            recv = gv
        g = merged(ov[...], recv[...], r // 2, Place(meta).bit(level))
    gs = stacked(g)
    finish(first)
    w = jnp.concatenate([fv[w].reshape(1024, B) for w in range(4)], 1)
    z = y_ref[...] - product(gs, w, NND)
    z = jnp.where(row_mask(meta, level, n), z, 0.0)
    finish(early)
    finish(late)
    back(meta, level, n, ev, z, x_out)


SMEM = pl.BlockSpec(memory_space=pltpu.SMEM)
VMEM = pl.BlockSpec(memory_space=pltpu.VMEM)
ANY = pl.BlockSpec(memory_space=pl.ANY)


def call(kernel, name, shapes, scratch, meta, small, weights=(), flops=0):
    weights = [pltpu.with_memory_space_constraint(w, pltpu.HBM) for w in weights]
    moved = sum(w.size * 4 for w in weights) + sum(v.size * 4 for v in small)
    return pl.pallas_call(
        kernel,
        out_shape=[jax.ShapeDtypeStruct(s, f32) for s in shapes],
        in_specs=[SMEM] + [VMEM] * len(small) + [ANY] * len(weights),
        out_specs=[VMEM] * len(shapes),
        scratch_shapes=scratch,
        compiler_params=pltpu.CompilerParams(vmem_limit_bytes=(14 if flops else 3) * 2**20),
        cost_estimate=pl.CostEstimate(flops=flops, bytes_accessed=moved, transcendentals=0),
        name=name,
    )(meta, *small, *weights)


def local(
    live_tiles, row_tiles, rhs0, rhs1, rhs2, rhs3, dinv0, dinv1, dinv2, dinv3, off0, off1, off2
):
    ci, x0, x1 = lax.axis_index("core"), lax.axis_index("x0"), lax.axis_index("x1")
    zi = lax.axis_index("z")
    leaf = x1 * 4 + x0 * 2 + ci
    here = leaf * 16 + zi * 4 + lax.axis_index("y")
    meta = jnp.concatenate([here.reshape(1), live_tiles, row_tiles.reshape(-1)])
    bits = [("core", ci), ("x0", x0), ("x1", x1)]

    def joined(v, i, dim=0):
        axis, bit = bits[i]
        return ordered(v, flip(v, axis), bit, dim)

    def pick(v, i, dim=0):
        return lax.dynamic_index_in_dim(v, i, dim, keepdims=False)

    def for_z(pair, other, bit):
        blocks = []
        for s in range(4):
            z = (zi + s) % 4
            blocks.append(jnp.where(z // 2 == bit, pick(pair, z % 2), pick(other, z % 2)))
        return blocks

    def over_z(blocks):
        return [blocks[0]] + [shift(blocks[s], "z", s) for s in (1, 2, 3)]

    def gathered(blocks, f):
        parts = [v[None] for v in blocks] + ([] if f is None else [f.reshape(2, 256, B)])
        return lax.all_gather(jnp.concatenate(parts, 0), "y", axis=0, tiled=False)

    gate = lax.optimization_barrier
    off0 = off0.reshape(4, 256, B)
    fa, fb = shift(off0, "z", 1), shift(off0, "z", -1)
    fc, fd = shift(fa[:2], "z", 1), shift(fb[2:], "z", -1)
    e0 = jnp.swapaxes(dinv0.reshape(4, 4, B, B), 0, 1).reshape(4, 512, B)
    e0 = lax.all_to_all(e0, "y", 0, 0, tiled=True)
    e1 = dinv1.reshape(2, 2, 256, B)
    e1 = over_z(for_z(pick(e1, ci, 1), flip(pick(e1, 1 - ci, 1), "core"), ci))
    e0, e1, fa, fb, fc, fd, dinv2, off2, dinv3, rhs0, rhs1 = gate(
        (e0, e1, fa, fb, fc, fd, dinv2, off2, dinv3, rhs0, rhs1)
    )
    m1 = gathered(e1, off1)

    ea, eb = shift(e0, "z", 1), shift(e0, "z", -1)
    e2 = dinv2.reshape(2, 256, B)
    e2 = ordered(pick(e2, ci)[None], flip(pick(e2, 1 - ci)[None], "core"), ci, 0)
    e2_other = flip(e2, "x0")
    f2 = joined(off2, 1)
    e3 = joined(dinv3[None], 1)
    e3_other = flip(e3, "x1")
    c0 = gather4(rhs0, "y")
    b_mine, b_other = halves(jnp.concatenate([rhs1, rhs2, rhs3], 1), ci)
    b_other = flip(b_other, "core")
    ea, eb, e2, e2_other, f2, e3, e3_other, c0, b_mine, b_other = gate(
        (ea, eb, e2, e2_other, f2, e3, e3_other, c0, b_mine, b_other)
    )

    ec, ed = shift(ea[:2], "z", 1), shift(eb[2:], "z", -1)
    e2 = over_z(for_z(e2, e2_other, x0))
    e2[0], ec, ed = gate((e2[0], ec, ed))
    w0 = [e0, ea, eb, ec, ed, off0, fa, fb, fc, fd]
    e3 = over_z(for_z(e3, e3_other, x1))
    e3, b_mine = gate((e3, b_mine))
    m3 = gathered(e3, None)

    dma = pltpu.SemaphoreType.DMA
    ev, fv = pltpu.VMEM((4, 4, 512, B), f32), pltpu.VMEM((4, 4, 256, B), f32)

    def work(n):
        return [pltpu.VMEM((n, ORDER), f32), pltpu.VMEM((n, 512), f32), pltpu.VMEM((n, 1024), f32)]

    def flops(n):
        return 2 * n * 512 * (2048 + 1024) * 12

    y0, *u = call(
        functools.partial(forward_kernel, 0, 64, "rs"), "f0", [(64, 512)] + [(16, 1024)] * 4,
        [ev, fv, *work(64), dma((10,))], meta, c0, w0, flops(64),
    )
    e2, _ = gate((e2, y0))
    m2 = gathered(e2, f2)
    parts = scatter4(u, "y")
    m1, _ = gate((m1, parts[1]))
    w1 = m1, flip(m1, "core")
    u = (parts[0] + parts[1]) + (parts[2] + parts[3])
    keep, give = halves(u, ci)
    c1, pk, pg = call(
        s01_kernel, "s01", [(8, ORDER), (2, 4, ORDER), (2, 4, ORDER)],
        [pltpu.VMEM((3, 8, ORDER), f32)], meta, [keep, flip(give, "core"), b_mine, b_other],
    )
    pr = flip(pg, "x0")
    y1, keep, give = call(
        functools.partial(forward_kernel, 1, 32, "ar"), "f1", [(32, 512), (16, 1024), (16, 1024)],
        [ev, fv, *work(32), dma((12,))], meta, gather4(c1, "z"), w1, flops(32),
    )
    part, keep3, give3 = call(
        s12_kernel, "s12", [(16, ORDER), (8, ORDER), (8, ORDER)],
        [pltpu.VMEM((2, 16, ORDER), f32)], meta, [keep, flip(give, "x0"), pk, pr],
    )
    m2, _ = gate((m2, part))
    w2 = m2, flip(m2, "core")
    recv3 = flip(give3, "x1")
    y2, keep, give = call(
        functools.partial(forward_kernel, 2, 16, "ar"), "f2", [(16, 512), (8, 1024), (8, 1024)],
        [ev, fv, *work(16), dma((12,))], meta, gather4(part, "z"), w2, flops(16),
    )
    (part,) = call(
        s23_kernel, "s23", [(8, ORDER)],
        [pltpu.VMEM((1, 8, ORDER), f32)], meta, [keep, flip(give, "x1"), keep3, recv3],
    )

    m3, _ = gate((m3, part))
    w3 = m3, flip(m3, "core")
    (part,) = call(
        top_kernel, "top", [(8, ORDER)], [ev, pltpu.VMEM((8, 512), f32), dma((8,))],
        meta, gather4(part, "z"), w3, flops(8),
    )
    (x3,) = call(x3_kernel, "x3", [(8, ORDER)], [], meta, gather4(part, "z"))
    x3r = flip(x3, "x1")

    def rest(n):
        rows = n if n != 16 else 8
        return [ev, fv, pltpu.VMEM((rows, 1024), f32), pltpu.VMEM((n // 2, 1024), f32), dma((12,))]

    (part,) = call(
        functools.partial(backward_kernel, 2, 16), "b2", [(16, ORDER)], rest(16),
        meta, [x3[None], x3r[None], y2], w2, flops(16),
    )
    anc, give = call(
        x2_kernel, "x2", [(2, 16, ORDER), (16, 1024)], [],
        meta, gather4(part, "z") + [x3, x3r],
    )
    recv = flip(give, "x0")
    a_mine = anc[:, :4]
    a_other = flip(a_mine, "x0")
    parts = call(
        functools.partial(backward_kernel, 1, 32), "b1", [(8, ORDER)] * 4, rest(32),
        meta, [anc, recv, y1], w1, flops(32),
    )
    anc, give, own = call(
        x1_kernel, "x1", [(3, 8, ORDER), (8, 1024), (8, 1024)], [],
        meta, scatter4(parts, "z") + [a_mine, a_other],
    )
    g = ordered(own, flip(give, "core"), ci, 0)
    parts = call(
        functools.partial(backward_kernel, 0, 64), "b0", [(16, ORDER)] * 4, rest(64),
        meta, gather4(g, "y") + [y0], w0, flops(64),
    )
    parts = scatter4(parts, "y")
    sol0 = (parts[0] + parts[1]) + (parts[2] + parts[3])

    outs = [sol0]
    for k in (1, 2, 3):
        width = ORDER // 2**k
        place = leaf % 2**k
        mine = lax.dynamic_slice_in_dim(anc[k - 1], place * width, width, 1)
        give = lax.dynamic_slice_in_dim(anc[k - 1], (place ^ 1) * width, width, 1)
        outs.append(ordered(mine, flip(give, "core"), ci, 0))
    return tuple(outs)


def solution(mesh):
    fine = Mesh(mesh.devices.reshape(2, 2, 2, 4, 4), ("x1", "x0", "core", "z", "y"))
    leaf, panel = ("x1", "x0", "core"), ("z", "y")
    return jax.shard_map(
        local,
        mesh=fine,
        in_specs=(P(), P()) + (P(panel, leaf),) * 4 + (P(leaf, panel),) * 7,
        out_specs=(P(panel, leaf),) * 4,
        check_vma=False,
    )
```

```python
import functools
import jax
import jax.numpy as jnp
from jax import lax
from jax.experimental import pallas as pl
from jax.experimental.pallas import tpu as pltpu
from jax.sharding import Mesh, PartitionSpec as P

B = 128
ORDER = 2048
NT = 16
f32 = jnp.float32
bf16 = jnp.bfloat16

FIRST = (0, 8, 12, 14)


class Place:
    def __init__(self, meta):
        self.meta = meta
        self.leaf = meta[0] >> 4
        self.zi, self.yi = (meta[0] >> 2) & 3, meta[0] & 3
        self.ci, self.x0, self.x1 = self.leaf & 1, (self.leaf >> 1) & 1, self.leaf >> 2

    def live(self, level):
        return self.meta[1 + FIRST[level] + (self.leaf >> level)]

    def own(self, level):
        return 16 + 8 * (FIRST[level] + (self.leaf >> level))

    def partner(self, level):
        return 16 + 8 * (FIRST[level] + ((self.leaf >> level) ^ 1))

    def bit(self, level):
        return (self.ci, self.x0, self.x1)[level]


def shift(v, axis, s):
    return lax.ppermute(v, axis, [(i, (i + s) % 4) for i in range(4)])


def flip(v, axis):
    return lax.ppermute(v, axis, [(0, 1), (1, 0)])


def gather4(v, axis):
    far = shift(v, axis, 2)
    return [v, shift(v, axis, 1), far, shift(v, axis, 3)]


def scatter4(parts, axis):
    far = shift(parts[2], axis, 2)
    return [parts[0], shift(parts[1], axis, -1), far, shift(parts[3], axis, 1)]


def ring(v, axis, dim):
    h = v.shape[dim] // 2
    a = shift(v, axis, 1)
    b = shift(v, axis, -1)
    c = shift(lax.slice_in_dim(a, 0, h, axis=dim), axis, 1)
    d = shift(lax.slice_in_dim(b, h, 2 * h, axis=dim), axis, -1)
    return [v, a, b, c, d]


def ordered(mine, other, bit, dim):
    return jnp.where(
        bit == 0, jnp.concatenate([mine, other], dim), jnp.concatenate([other, mine], dim)
    )


def halves(v, bit):
    h = v.shape[0] // 2
    return (
        jnp.where(bit == 0, v[:h], v[h:]),
        jnp.where(bit == 0, v[h:], v[:h]),
    )


def stacked(v):
    hi = v.astype(bf16).astype(f32)
    return jnp.concatenate([hi, v - hi], 0).astype(bf16)


def product(left, w, dims):
    hi = w.astype(bf16)
    lo = (w - hi.astype(f32)).astype(bf16)
    r = lax.dot_general(left, hi, (dims, ((), ())), preferred_element_type=f32)
    r = r + lax.dot_general(left, lo, (dims, ((), ())), preferred_element_type=f32)
    n = left.shape[0] // 2
    return r[:n] + r[n:]


NTD = ((1,), (1,))
NND = ((1,), (0,))


def copies_first(meta, refs, ev, fv, sems):
    e, f = refs[:5], refs[5:]
    zi = Place(meta).zi
    spots = [zi, lax.rem(zi + 3, 4), lax.rem(zi + 1, 4)]
    far = lax.rem(zi + 2, 4)
    pairs_e = [(ref, ev.at[w]) for ref, w in zip(e[:3], spots)]
    pairs_e += [(e[3], ev.at[far, 0:2]), (e[4], ev.at[far, 2:4])]
    pairs_f = [(ref, fv.at[w]) for ref, w in zip(f[:3], spots)]
    pairs_f += [(f[3], fv.at[far, 0:2]), (f[4], fv.at[far, 2:4])]
    made = [
        pltpu.make_async_copy(src, dst, sems.at[k]) for k, (src, dst) in enumerate(pairs_e + pairs_f)
    ]
    return made[:5], [], made[5:]


def copies_upper(level, meta, bufs, ev, fv, sems):
    place = Place(meta)
    groups = ([], [], [])
    k = 0
    for i, q in ((0, place.ci), (1, 1 - place.ci)):
        rows = pl.ds(pl.multiple_of(q * 256, 256), 256)
        pairs = [(bufs[i].at[:, s], ev.at[:, lax.rem(place.zi + 4 - s, 4), rows]) for s in range(4)]
        late = []
        if level == 1:
            late = [(bufs[i].at[:, 4:6], fv.at[:, pl.ds(2 * q, 2)])]
        elif level == 2:
            late = [(bufs[i].at[:, 4 + h], fv.at[:, 2 * h + q]) for h in (0, 1)]
        for group, some in ((groups[i], pairs), (groups[2], late)):
            for src, dst in some:
                group.append(pltpu.make_async_copy(src, dst, sems.at[k]))
                k += 1
    return groups


def copies(level, meta, refs, ev, fv, sems):
    if level == 0:
        return copies_first(meta, refs, ev, fv, sems)
    return copies_upper(level, meta, refs, ev, fv, sems)


def finish(group):
    for c in group:
        c.wait()


def tiles_in_order(level):
    if level == 0:
        return [(t // 4, t % 4) for t in range(NT)]
    return [(t % 4, t // 4) for t in range(NT)]


def column_mask(meta, level, n):
    col = lax.broadcasted_iota(jnp.int32, (n, ORDER), 1)
    return col < Place(meta).live(level) * B


def row_mask(meta, level, n):
    own = lax.broadcasted_iota(jnp.int32, (n, 512), 1) // B
    place = Place(meta)
    tile = 4 * own + place.yi if level == 0 else 4 * place.zi + own
    return tile < Place(meta).live(level)


def solve_rows(level, meta, ev, yv, cs, late):
    first = Place(meta).ci if level else 0

    def body(j, carry):
        @pl.when(j == 1)
        def _():
            finish(late)

        at = pl.multiple_of(jnp.where(j == 0, first, 1 - first) * 256, 256)
        rows = pl.ds(at, 256)
        w = jnp.concatenate([ev[w, s, rows, :] for w, s in tiles_in_order(level)], 1)
        yv[:, rows] = product(cs, w, NTD)
        return carry

    lax.fori_loop(0, 2, body, 0)


WEIGHTS = (10, 2, 2, 2)


def forward_kernel(level, n, mode, meta, *refs):
    count = WEIGHTS[level]
    c_refs, refs = refs[:4], refs[4:]
    w_refs, refs = refs[:count], refs[count:]
    if mode == "rs":
        y_out, u_out = refs[0], refs[1:5]
        refs = refs[5:]
    else:
        y_out, keep_out, give_out = refs[:3]
        refs = refs[3:]
    ev, fv, cv, yv, uv, sems = refs
    early, late, last = copies(level, meta, w_refs, ev, fv, sems)
    for c in [*early, *late, *last]:
        c.start()
    r = n // 4
    if level < 2:
        for s in range(4):
            cv[pl.ds(s * r, r), :] = c_refs[s][...]
        c = cv[...]
    else:
        c = summed(c_refs, r)
    cs = stacked(jnp.where(column_mask(meta, level, n), c, 0.0))
    finish(early)
    solve_rows(level, meta, ev, yv, cs, late)
    y = jnp.where(row_mask(meta, level, n), yv[...], 0.0)
    y_out[...] = y
    ys = stacked(y)
    finish(last)

    def body(j, carry):
        w = jnp.concatenate([fv[w, j] for w in range(4)], 1)
        uv[:, pl.ds(pl.multiple_of(j * 256, 256), 256)] = product(ys, w, NTD)
        return carry

    lax.fori_loop(0, 4, body, 0)
    if mode == "rs":
        for s in range(4):
            u_out[s][...] = uv[pl.ds(s * r, r), :]
    else:
        split_rows(uv, r, Place(meta).bit(level), keep_out, give_out)


def split_rows(v, r, bit, keep_out, give_out):
    h = r // 2
    for s in range(4):
        low = v[pl.ds(s * r, h), :]
        high = v[pl.ds(s * r + h, h), :]
        keep_out[pl.ds(s * h, h), :] = jnp.where(bit == 0, low, high)
        give_out[pl.ds(s * h, h), :] = jnp.where(bit == 0, high, low)


def summed(refs, r):
    parts = []
    for s in range(4):
        total = refs[0][pl.ds(s * r, r), :]
        for d in (1, 2, 3):
            total = total + refs[d][pl.ds((s - d) % 4 * r, r), :]
        parts.append(total)
    return jnp.concatenate(parts, 0)


def add_tiles(meta, at, src, acc):
    for t in range(8):
        v = meta[at + t]
        cols = pl.ds(pl.multiple_of(lax.rem(v, NT) * B, B), B)
        lev = lax.div(v, NT)
        acc[lev, :, cols] = acc[lev, :, cols] + src[:, t * B : (t + 1) * B]


def take_tiles(meta, at, anc, dst):
    for t in range(8):
        v = meta[at + t]
        cols = pl.ds(pl.multiple_of(lax.rem(v, NT) * B, B), B)
        dst[:, t * B : (t + 1) * B] = anc[lax.div(v, NT), :, cols]


def s01_kernel(meta, keep, recv, b_mine, b_other, c1, pk, pg, acc):
    place = Place(meta)
    acc[...] = jnp.zeros_like(acc)
    add_tiles(meta, place.own(0), keep, acc)
    add_tiles(meta, place.partner(0), recv, acc)
    group = (0, place.x0, place.leaf >> 1)
    for ref, c in ((b_mine, place.ci), (b_other, 1 - place.ci)):
        at = 0
        for i in range(3):
            width = 1024 >> i
            cols = pl.ds(pl.multiple_of((2 * group[i] + c) * width, width), width)
            acc[i, :, cols] = acc[i, :, cols] - ref[:, at : at + width]
            at += width
    c1[...] = -acc[0]
    for i in (0, 1):
        low, high = acc[i + 1, 0:4, :], acc[i + 1, 4:8, :]
        pk[i] = jnp.where(place.x0 == 0, low, high)
        pg[i] = jnp.where(place.x0 == 0, high, low)


def s12_kernel(meta, keep, recv, pk, pr, part, keep3, give3, acc):
    place = Place(meta)
    acc[...] = jnp.zeros_like(acc)
    add_tiles(meta, place.own(1), keep, acc)
    add_tiles(meta, place.partner(1), recv, acc)
    for i in (0, 1):
        acc[i, 0:4, :] = acc[i, 0:4, :] + (pk[i] + pr[i])
    part[...] = -acc[0]
    split_rows(acc.at[1], 4, place.x1, keep3, give3)


def s23_kernel(meta, keep, recv, keep3, recv3, part, acc):
    place = Place(meta)
    acc[...] = jnp.zeros_like(acc)
    add_tiles(meta, place.own(2), keep, acc)
    add_tiles(meta, place.partner(2), recv, acc)
    part[...] = -(acc[0] + (keep3[...] + recv3[...]))


def top_kernel(meta, c0, c1, c2, c3, *refs):
    w_refs, (x_out, ev, yv, sems) = refs[:2], refs[2:]
    early, late, _ = copies(3, meta, w_refs, ev, None, sems)
    for c in [*early, *late]:
        c.start()
    c = summed((c0, c1, c2, c3), 2)
    cs = stacked(jnp.where(column_mask(meta, 3, 8), c, 0.0))
    finish(early)
    solve_rows(3, meta, ev, yv, cs, late)
    back(meta, 3, 8, ev, jnp.where(row_mask(meta, 3, 8), yv[...], 0.0), [x_out])


def back(meta, level, n, ev, z, x_out):
    zs = stacked(z)
    live = Place(meta).live(level) * B

    def body(j, carry):
        cols = pl.ds(pl.multiple_of(j * 512, 512), 512)
        w = jnp.concatenate([ev[j, i] if level == 0 else ev[i, j] for i in range(4)], 1)
        v = product(zs, w, NND)
        col = lax.broadcasted_iota(jnp.int32, (n, 512), 1) + j * 512
        v = jnp.where(col < live, v, 0.0)
        r = n // len(x_out)
        for s, out in enumerate(x_out):
            out[:, cols] = v[s * r : (s + 1) * r]
        return carry

    lax.fori_loop(0, 4, body, 0)


def x3_kernel(meta, c0, c1, c2, c3, x_out):
    x_out[...] = summed((c0, c1, c2, c3), 2)


def merged(a, b, h, bit):
    parts = []
    for s in range(4):
        u, v = a[s * h : (s + 1) * h, :], b[s * h : (s + 1) * h, :]
        parts += [jnp.where(bit == 0, u, v), jnp.where(bit == 0, v, u)]
    return jnp.concatenate(parts, 0)


def x2_kernel(meta, c0, c1, c2, c3, x3, x3r, anc_out, give):
    anc_out[0] = summed((c0, c1, c2, c3), 4)
    anc_out[1] = merged(x3[...], x3r[...], 2, Place(meta).x1)
    take_tiles(meta, Place(meta).partner(1), anc_out, give)


def x1_kernel(meta, c0, c1, c2, c3, a_mine, a_other, anc_out, give, own):
    anc_out[0] = (c0[...] + c1[...]) + (c2[...] + c3[...])
    for i in (0, 1):
        u, v = a_mine[i], a_other[i]
        bit = Place(meta).x0
        anc_out[i + 1, 0:4, :] = jnp.where(bit == 0, u, v)
        anc_out[i + 1, 4:8, :] = jnp.where(bit == 0, v, u)
    take_tiles(meta, Place(meta).partner(0), anc_out, give)
    take_tiles(meta, Place(meta).own(0), anc_out, own)


def backward_kernel(level, n, meta, *refs):
    count = WEIGHTS[level]
    if level == 0:
        g_refs, refs = refs[:4], refs[4:]
    else:
        (anc, recv), refs = refs[:2], refs[2:]
    y_ref, refs = refs[0], refs[1:]
    w_refs, refs = refs[:count], refs[count:]
    x_out, (ev, fv, gv, ov, sems) = refs[:-5], refs[-5:]
    early, late, first = copies(level, meta, w_refs, ev, fv, sems)
    for c in [*first, *early, *late]:
        c.start()
    r = n // 4
    if level == 0:
        for s in range(4):
            gv[pl.ds(s * r, r), :] = g_refs[s][...]
        g = gv[...]
    else:
        take_tiles(meta, Place(meta).own(level), anc, ov)
        if level == 2:
            take_tiles(meta, Place(meta).own(level), recv, gv)
            recv = gv
        g = merged(ov[...], recv[...], r // 2, Place(meta).bit(level))
    gs = stacked(g)
    finish(first)
    w = jnp.concatenate([fv[w].reshape(1024, B) for w in range(4)], 1)
    z = y_ref[...] - product(gs, w, NND)
    z = jnp.where(row_mask(meta, level, n), z, 0.0)
    finish(early)
    finish(late)
    back(meta, level, n, ev, z, x_out)


SMEM = pl.BlockSpec(memory_space=pltpu.SMEM)
VMEM = pl.BlockSpec(memory_space=pltpu.VMEM)
ANY = pl.BlockSpec(memory_space=pl.ANY)


def call(kernel, name, shapes, scratch, meta, small, weights=(), flops=0):
    weights = [pltpu.with_memory_space_constraint(w, pltpu.HBM) for w in weights]
    moved = sum(w.size * 4 for w in weights) + sum(v.size * 4 for v in small)
    return pl.pallas_call(
        kernel,
        out_shape=[jax.ShapeDtypeStruct(s, f32) for s in shapes],
        in_specs=[SMEM] + [VMEM] * len(small) + [ANY] * len(weights),
        out_specs=[VMEM] * len(shapes),
        scratch_shapes=scratch,
        compiler_params=pltpu.CompilerParams(vmem_limit_bytes=(14 if flops else 3) * 2**20),
        cost_estimate=pl.CostEstimate(flops=flops, bytes_accessed=moved, transcendentals=0),
        name=name,
    )(meta, *small, *weights)


def local(
    live_tiles, row_tiles, rhs0, rhs1, rhs2, rhs3, dinv0, dinv1, dinv2, dinv3, off0, off1, off2
):
    ci, x0, x1 = lax.axis_index("core"), lax.axis_index("x0"), lax.axis_index("x1")
    zi = lax.axis_index("z")
    leaf = x1 * 4 + x0 * 2 + ci
    here = leaf * 16 + zi * 4 + lax.axis_index("y")
    meta = jnp.concatenate([here.reshape(1), live_tiles, row_tiles.reshape(-1)])
    bits = [("core", ci), ("x0", x0), ("x1", x1)]

    def joined(v, i, dim=0):
        axis, bit = bits[i]
        return ordered(v, flip(v, axis), bit, dim)

    def pick(v, i, dim=0):
        return lax.dynamic_index_in_dim(v, i, dim, keepdims=False)

    def for_z(pair, other, bit):
        blocks = []
        for s in range(4):
            z = (zi + s) % 4
            blocks.append(jnp.where(z // 2 == bit, pick(pair, z % 2), pick(other, z % 2)))
        return blocks

    def over_z(blocks):
        return [blocks[0]] + [shift(blocks[s], "z", s) for s in (1, 2, 3)]

    def gathered(blocks, f):
        parts = [v[None] for v in blocks] + ([] if f is None else [f.reshape(2, 256, B)])
        return lax.all_gather(jnp.concatenate(parts, 0), "y", axis=0, tiled=False)

    gate = lax.optimization_barrier
    off0 = off0.reshape(4, 256, B)
    fa, fb = shift(off0, "z", 1), shift(off0, "z", -1)
    fc, fd = shift(fa[:2], "z", 1), shift(fb[2:], "z", -1)
    e0 = jnp.swapaxes(dinv0.reshape(4, 4, B, B), 0, 1).reshape(4, 512, B)
    e0 = lax.all_to_all(e0, "y", 0, 0, tiled=True)
    e1 = dinv1.reshape(2, 2, 256, B)
    e1 = over_z(for_z(pick(e1, ci, 1), flip(pick(e1, 1 - ci, 1), "core"), ci))
    e0, e1, fa, fb, fc, fd, dinv2, off2, dinv3, rhs0, rhs1 = gate(
        (e0, e1, fa, fb, fc, fd, dinv2, off2, dinv3, rhs0, rhs1)
    )
    m1 = gathered(e1, off1)

    ea, eb = shift(e0, "z", 1), shift(e0, "z", -1)
    e2 = dinv2.reshape(2, 256, B)
    e2 = ordered(pick(e2, ci)[None], flip(pick(e2, 1 - ci)[None], "core"), ci, 0)
    e2_other = flip(e2, "x0")
    f2 = joined(off2, 1)
    e3 = joined(dinv3[None], 1)
    e3_other = flip(e3, "x1")
    e2 = over_z(for_z(e2, e2_other, x0))
    b_mine, b_other = halves(jnp.concatenate([rhs1, rhs2, rhs3], 1), ci)
    b_other = flip(b_other, "core")
    ea, eb, e2, f2, e3, e3_other, b_mine, b_other = gate(
        (ea, eb, e2, f2, e3, e3_other, b_mine, b_other)
    )

    ec, ed = shift(ea[:2], "z", 1), shift(eb[2:], "z", -1)
    m2 = gathered(e2, f2)
    e3 = over_z(for_z(e3, e3_other, x1))
    c0 = gather4(rhs0, "y")
    e3[0], ec, ed, c0 = gate((e3[0], ec, ed, c0))
    w0 = [e0, ea, eb, ec, ed, off0, fa, fb, fc, fd]

    dma = pltpu.SemaphoreType.DMA
    ev, fv = pltpu.VMEM((4, 4, 512, B), f32), pltpu.VMEM((4, 4, 256, B), f32)

    def work(n):
        return [pltpu.VMEM((n, ORDER), f32), pltpu.VMEM((n, 512), f32), pltpu.VMEM((n, 1024), f32)]

    def flops(n):
        return 2 * n * 512 * (2048 + 1024) * 12

    y0, *u = call(
        functools.partial(forward_kernel, 0, 64, "rs"), "f0", [(64, 512)] + [(16, 1024)] * 4,
        [ev, fv, *work(64), dma((10,))], meta, c0, w0, flops(64),
    )
    parts = scatter4(u, "y")
    e3, _ = gate((e3, y0))
    m3 = gathered(e3, None)
    u = (parts[0] + parts[1]) + (parts[2] + parts[3])
    m1, _ = gate((m1, u))
    w1 = m1, flip(m1, "core")
    keep, give = halves(u, ci)
    c1, pk, pg = call(
        s01_kernel, "s01", [(8, ORDER), (2, 4, ORDER), (2, 4, ORDER)],
        [pltpu.VMEM((3, 8, ORDER), f32)], meta, [keep, flip(give, "core"), b_mine, b_other],
    )
    pr = flip(pg, "x0")
    y1, keep, give = call(
        functools.partial(forward_kernel, 1, 32, "ar"), "f1", [(32, 512), (16, 1024), (16, 1024)],
        [ev, fv, *work(32), dma((12,))], meta, gather4(c1, "z"), w1, flops(32),
    )
    part, keep3, give3 = call(
        s12_kernel, "s12", [(16, ORDER), (8, ORDER), (8, ORDER)],
        [pltpu.VMEM((2, 16, ORDER), f32)], meta, [keep, flip(give, "x0"), pk, pr],
    )
    m2, _ = gate((m2, part))
    w2 = m2, flip(m2, "core")
    recv3 = flip(give3, "x1")
    y2, keep, give = call(
        functools.partial(forward_kernel, 2, 16, "ar"), "f2", [(16, 512), (8, 1024), (8, 1024)],
        [ev, fv, *work(16), dma((12,))], meta, gather4(part, "z"), w2, flops(16),
    )
    (part,) = call(
        s23_kernel, "s23", [(8, ORDER)],
        [pltpu.VMEM((1, 8, ORDER), f32)], meta, [keep, flip(give, "x1"), keep3, recv3],
    )

    m3, _ = gate((m3, part))
    w3 = m3, flip(m3, "core")
    (part,) = call(
        top_kernel, "top", [(8, ORDER)], [ev, pltpu.VMEM((8, 512), f32), dma((8,))],
        meta, gather4(part, "z"), w3, flops(8),
    )
    (x3,) = call(x3_kernel, "x3", [(8, ORDER)], [], meta, gather4(part, "z"))
    x3r = flip(x3, "x1")

    def rest(n):
        rows = n if n != 16 else 8
        return [ev, fv, pltpu.VMEM((rows, 1024), f32), pltpu.VMEM((n // 2, 1024), f32), dma((12,))]

    (part,) = call(
        functools.partial(backward_kernel, 2, 16), "b2", [(16, ORDER)], rest(16),
        meta, [x3[None], x3r[None], y2], w2, flops(16),
    )
    anc, give = call(
        x2_kernel, "x2", [(2, 16, ORDER), (16, 1024)], [],
        meta, gather4(part, "z") + [x3, x3r],
    )
    recv = flip(give, "x0")
    a_mine = anc[:, :4]
    a_other = flip(a_mine, "x0")
    parts = call(
        functools.partial(backward_kernel, 1, 32), "b1", [(8, ORDER)] * 4, rest(32),
        meta, [anc, recv, y1], w1, flops(32),
    )
    anc, give, own = call(
        x1_kernel, "x1", [(3, 8, ORDER), (8, 1024), (8, 1024)], [],
        meta, scatter4(parts, "z") + [a_mine, a_other],
    )
    g = ordered(own, flip(give, "core"), ci, 0)
    parts = call(
        functools.partial(backward_kernel, 0, 64), "b0", [(16, ORDER)] * 4, rest(64),
        meta, gather4(g, "y") + [y0], w0, flops(64),
    )
    parts = scatter4(parts, "y")
    sol0 = (parts[0] + parts[1]) + (parts[2] + parts[3])

    outs = [sol0]
    for k in (1, 2, 3):
        width = ORDER // 2**k
        place = leaf % 2**k
        mine = lax.dynamic_slice_in_dim(anc[k - 1], place * width, width, 1)
        give = lax.dynamic_slice_in_dim(anc[k - 1], (place ^ 1) * width, width, 1)
        outs.append(ordered(mine, flip(give, "core"), ci, 0))
    return tuple(outs)


def solution(mesh):
    fine = Mesh(mesh.devices.reshape(2, 2, 2, 4, 4), ("x1", "x0", "core", "z", "y"))
    leaf, panel = ("x1", "x0", "core"), ("z", "y")
    return jax.shard_map(
        local,
        mesh=fine,
        in_specs=(P(), P()) + (P(panel, leaf),) * 4 + (P(leaf, panel),) * 7,
        out_specs=(P(panel, leaf),) * 4,
        check_vma=False,
    )
```

```python
import functools
import jax
import jax.numpy as jnp
from jax import lax
from jax.experimental import pallas as pl
from jax.experimental.pallas import tpu as pltpu
from jax.sharding import Mesh, PartitionSpec as P

B = 128
ORDER = 2048
NT = 16
f32 = jnp.float32
bf16 = jnp.bfloat16

FIRST = (0, 8, 12, 14)


class Place:
    def __init__(self, meta):
        self.meta = meta
        self.leaf = meta[0] >> 4
        self.zi, self.yi = (meta[0] >> 2) & 3, meta[0] & 3
        self.ci, self.x0, self.x1 = self.leaf & 1, (self.leaf >> 1) & 1, self.leaf >> 2

    def live(self, level):
        return self.meta[1 + FIRST[level] + (self.leaf >> level)]

    def own(self, level):
        return 16 + 8 * (FIRST[level] + (self.leaf >> level))

    def partner(self, level):
        return 16 + 8 * (FIRST[level] + ((self.leaf >> level) ^ 1))

    def bit(self, level):
        return (self.ci, self.x0, self.x1)[level]


def shift(v, axis, s):
    return lax.ppermute(v, axis, [(i, (i + s) % 4) for i in range(4)])


def flip(v, axis):
    return lax.ppermute(v, axis, [(0, 1), (1, 0)])


def gather4(v, axis):
    far = shift(v, axis, 2)
    return [v, shift(v, axis, 1), far, shift(v, axis, 3)]


def scatter4(parts, axis):
    far = shift(parts[2], axis, 2)
    return [parts[0], shift(parts[1], axis, -1), far, shift(parts[3], axis, 1)]


def ring(v, axis, dim):
    h = v.shape[dim] // 2
    a = shift(v, axis, 1)
    b = shift(v, axis, -1)
    c = shift(lax.slice_in_dim(a, 0, h, axis=dim), axis, 1)
    d = shift(lax.slice_in_dim(b, h, 2 * h, axis=dim), axis, -1)
    return [v, a, b, c, d]


def ordered(mine, other, bit, dim):
    return jnp.where(
        bit == 0, jnp.concatenate([mine, other], dim), jnp.concatenate([other, mine], dim)
    )


def halves(v, bit):
    h = v.shape[0] // 2
    return (
        jnp.where(bit == 0, v[:h], v[h:]),
        jnp.where(bit == 0, v[h:], v[:h]),
    )


def stacked(v):
    hi = v.astype(bf16).astype(f32)
    return jnp.concatenate([hi, v - hi], 0).astype(bf16)


def product(left, w, dims):
    hi = w.astype(bf16)
    lo = (w - hi.astype(f32)).astype(bf16)
    r = lax.dot_general(left, hi, (dims, ((), ())), preferred_element_type=f32)
    r = r + lax.dot_general(left, lo, (dims, ((), ())), preferred_element_type=f32)
    n = left.shape[0] // 2
    return r[:n] + r[n:]


NTD = ((1,), (1,))
NND = ((1,), (0,))


def copies_first(meta, refs, ev, fv, sems):
    e, f = refs[:5], refs[5:]
    zi = Place(meta).zi
    spots = [zi, lax.rem(zi + 3, 4), lax.rem(zi + 1, 4)]
    far = lax.rem(zi + 2, 4)
    pairs_e = [(ref, ev.at[w]) for ref, w in zip(e[:3], spots)]
    pairs_e += [(e[3], ev.at[far, 0:2]), (e[4], ev.at[far, 2:4])]
    pairs_f = [(ref, fv.at[w]) for ref, w in zip(f[:3], spots)]
    pairs_f += [(f[3], fv.at[far, 0:2]), (f[4], fv.at[far, 2:4])]
    made = [
        pltpu.make_async_copy(src, dst, sems.at[k]) for k, (src, dst) in enumerate(pairs_e + pairs_f)
    ]
    return made[:5], [], made[5:]


def copies_upper(level, meta, bufs, ev, fv, sems):
    place = Place(meta)
    groups = ([], [], [])
    k = 0
    for i, q in ((0, place.ci), (1, 1 - place.ci)):
        rows = pl.ds(pl.multiple_of(q * 256, 256), 256)
        pairs = [(bufs[i].at[:, s], ev.at[:, lax.rem(place.zi + 4 - s, 4), rows]) for s in range(4)]
        late = []
        if level == 1:
            late = [(bufs[i].at[:, 4:6], fv.at[:, pl.ds(2 * q, 2)])]
        elif level == 2:
            late = [(bufs[i].at[:, 4 + h], fv.at[:, 2 * h + q]) for h in (0, 1)]
        for group, some in ((groups[i], pairs), (groups[2], late)):
            for src, dst in some:
                group.append(pltpu.make_async_copy(src, dst, sems.at[k]))
                k += 1
    return groups


def copies(level, meta, refs, ev, fv, sems):
    if level == 0:
        return copies_first(meta, refs, ev, fv, sems)
    return copies_upper(level, meta, refs, ev, fv, sems)


def finish(group):
    for c in group:
        c.wait()


def tiles_in_order(level):
    if level == 0:
        return [(t // 4, t % 4) for t in range(NT)]
    return [(t % 4, t // 4) for t in range(NT)]


def column_mask(meta, level, n):
    col = lax.broadcasted_iota(jnp.int32, (n, ORDER), 1)
    return col < Place(meta).live(level) * B


def row_mask(meta, level, n):
    own = lax.broadcasted_iota(jnp.int32, (n, 512), 1) // B
    place = Place(meta)
    tile = 4 * own + place.yi if level == 0 else 4 * place.zi + own
    return tile < Place(meta).live(level)


def solve_rows(level, meta, ev, yv, cs, late):
    first = Place(meta).ci if level else 0

    def body(j, carry):
        @pl.when(j == 1)
        def _():
            finish(late)

        at = pl.multiple_of(jnp.where(j == 0, first, 1 - first) * 256, 256)
        rows = pl.ds(at, 256)
        w = jnp.concatenate([ev[w, s, rows, :] for w, s in tiles_in_order(level)], 1)
        yv[:, rows] = product(cs, w, NTD)
        return carry

    lax.fori_loop(0, 2, body, 0)


WEIGHTS = (10, 2, 2, 2)


def forward_kernel(level, n, mode, meta, *refs):
    count = WEIGHTS[level]
    c_refs, refs = refs[:4], refs[4:]
    w_refs, refs = refs[:count], refs[count:]
    if mode == "rs":
        y_out, u_out = refs[0], refs[1:5]
        refs = refs[5:]
    else:
        y_out, keep_out, give_out = refs[:3]
        refs = refs[3:]
    ev, fv, cv, yv, uv, sems = refs
    early, late, last = copies(level, meta, w_refs, ev, fv, sems)
    for c in [*early, *late, *last]:
        c.start()
    r = n // 4
    if level < 2:
        for s in range(4):
            cv[pl.ds(s * r, r), :] = c_refs[s][...]
        c = cv[...]
    else:
        c = summed(c_refs, r)
    cs = stacked(jnp.where(column_mask(meta, level, n), c, 0.0))
    finish(early)
    solve_rows(level, meta, ev, yv, cs, late)
    y = jnp.where(row_mask(meta, level, n), yv[...], 0.0)
    y_out[...] = y
    ys = stacked(y)
    finish(last)

    def body(j, carry):
        w = jnp.concatenate([fv[w, j] for w in range(4)], 1)
        uv[:, pl.ds(pl.multiple_of(j * 256, 256), 256)] = product(ys, w, NTD)
        return carry

    lax.fori_loop(0, 4, body, 0)
    if mode == "rs":
        for s in range(4):
            u_out[s][...] = uv[pl.ds(s * r, r), :]
    else:
        split_rows(uv, r, Place(meta).bit(level), keep_out, give_out)


def split_rows(v, r, bit, keep_out, give_out):
    h = r // 2
    for s in range(4):
        low = v[pl.ds(s * r, h), :]
        high = v[pl.ds(s * r + h, h), :]
        keep_out[pl.ds(s * h, h), :] = jnp.where(bit == 0, low, high)
        give_out[pl.ds(s * h, h), :] = jnp.where(bit == 0, high, low)


def summed(refs, r):
    parts = []
    for s in range(4):
        total = refs[0][pl.ds(s * r, r), :]
        for d in (1, 2, 3):
            total = total + refs[d][pl.ds((s - d) % 4 * r, r), :]
        parts.append(total)
    return jnp.concatenate(parts, 0)


def add_tiles(meta, at, src, acc):
    for t in range(8):
        v = meta[at + t]
        cols = pl.ds(pl.multiple_of(lax.rem(v, NT) * B, B), B)
        lev = lax.div(v, NT)
        acc[lev, :, cols] = acc[lev, :, cols] + src[:, t * B : (t + 1) * B]


def take_tiles(meta, at, anc, dst):
    for t in range(8):
        v = meta[at + t]
        cols = pl.ds(pl.multiple_of(lax.rem(v, NT) * B, B), B)
        dst[:, t * B : (t + 1) * B] = anc[lax.div(v, NT), :, cols]


def s01_kernel(meta, keep, recv, b_mine, b_other, c1, pk, pg, acc):
    place = Place(meta)
    acc[...] = jnp.zeros_like(acc)
    add_tiles(meta, place.own(0), keep, acc)
    add_tiles(meta, place.partner(0), recv, acc)
    group = (0, place.x0, place.leaf >> 1)
    for ref, c in ((b_mine, place.ci), (b_other, 1 - place.ci)):
        at = 0
        for i in range(3):
            width = 1024 >> i
            cols = pl.ds(pl.multiple_of((2 * group[i] + c) * width, width), width)
            acc[i, :, cols] = acc[i, :, cols] - ref[:, at : at + width]
            at += width
    c1[...] = -acc[0]
    for i in (0, 1):
        low, high = acc[i + 1, 0:4, :], acc[i + 1, 4:8, :]
        pk[i] = jnp.where(place.x0 == 0, low, high)
        pg[i] = jnp.where(place.x0 == 0, high, low)


def s12_kernel(meta, keep, recv, pk, pr, part, keep3, give3, acc):
    place = Place(meta)
    acc[...] = jnp.zeros_like(acc)
    add_tiles(meta, place.own(1), keep, acc)
    add_tiles(meta, place.partner(1), recv, acc)
    for i in (0, 1):
        acc[i, 0:4, :] = acc[i, 0:4, :] + (pk[i] + pr[i])
    part[...] = -acc[0]
    split_rows(acc.at[1], 4, place.x1, keep3, give3)


def s23_kernel(meta, keep, recv, keep3, recv3, part, acc):
    place = Place(meta)
    acc[...] = jnp.zeros_like(acc)
    add_tiles(meta, place.own(2), keep, acc)
    add_tiles(meta, place.partner(2), recv, acc)
    part[...] = -(acc[0] + (keep3[...] + recv3[...]))


def top_kernel(meta, c0, c1, c2, c3, *refs):
    w_refs, (x_out, ev, yv, sems) = refs[:2], refs[2:]
    early, late, _ = copies(3, meta, w_refs, ev, None, sems)
    for c in [*early, *late]:
        c.start()
    c = summed((c0, c1, c2, c3), 2)
    cs = stacked(jnp.where(column_mask(meta, 3, 8), c, 0.0))
    finish(early)
    solve_rows(3, meta, ev, yv, cs, late)
    back(meta, 3, 8, ev, jnp.where(row_mask(meta, 3, 8), yv[...], 0.0), [x_out])


def back(meta, level, n, ev, z, x_out):
    zs = stacked(z)
    live = Place(meta).live(level) * B

    def body(j, carry):
        cols = pl.ds(pl.multiple_of(j * 512, 512), 512)
        w = jnp.concatenate([ev[j, i] if level == 0 else ev[i, j] for i in range(4)], 1)
        v = product(zs, w, NND)
        col = lax.broadcasted_iota(jnp.int32, (n, 512), 1) + j * 512
        v = jnp.where(col < live, v, 0.0)
        r = n // len(x_out)
        for s, out in enumerate(x_out):
            out[:, cols] = v[s * r : (s + 1) * r]
        return carry

    lax.fori_loop(0, 4, body, 0)


def x3_kernel(meta, c0, c1, c2, c3, x_out):
    x_out[...] = summed((c0, c1, c2, c3), 2)


def merged(a, b, h, bit):
    parts = []
    for s in range(4):
        u, v = a[s * h : (s + 1) * h, :], b[s * h : (s + 1) * h, :]
        parts += [jnp.where(bit == 0, u, v), jnp.where(bit == 0, v, u)]
    return jnp.concatenate(parts, 0)


def x2_kernel(meta, c0, c1, c2, c3, x3, x3r, anc_out, give):
    anc_out[0] = summed((c0, c1, c2, c3), 4)
    anc_out[1] = merged(x3[...], x3r[...], 2, Place(meta).x1)
    take_tiles(meta, Place(meta).partner(1), anc_out, give)


def x1_kernel(meta, c0, c1, c2, c3, a_mine, a_other, anc_out, give, own):
    anc_out[0] = (c0[...] + c1[...]) + (c2[...] + c3[...])
    for i in (0, 1):
        u, v = a_mine[i], a_other[i]
        bit = Place(meta).x0
        anc_out[i + 1, 0:4, :] = jnp.where(bit == 0, u, v)
        anc_out[i + 1, 4:8, :] = jnp.where(bit == 0, v, u)
    take_tiles(meta, Place(meta).partner(0), anc_out, give)
    take_tiles(meta, Place(meta).own(0), anc_out, own)


def backward_kernel(level, n, meta, *refs):
    count = WEIGHTS[level]
    if level == 0:
        g_refs, refs = refs[:4], refs[4:]
    else:
        (anc, recv), refs = refs[:2], refs[2:]
    y_ref, refs = refs[0], refs[1:]
    w_refs, refs = refs[:count], refs[count:]
    x_out, (ev, fv, gv, ov, sems) = refs[:-5], refs[-5:]
    early, late, first = copies(level, meta, w_refs, ev, fv, sems)
    for c in [*first, *early, *late]:
        c.start()
    r = n // 4
    if level == 0:
        for s in range(4):
            gv[pl.ds(s * r, r), :] = g_refs[s][...]
        g = gv[...]
    else:
        take_tiles(meta, Place(meta).own(level), anc, ov)
        if level == 2:
            take_tiles(meta, Place(meta).own(level), recv, gv)
            recv = gv
        g = merged(ov[...], recv[...], r // 2, Place(meta).bit(level))
    gs = stacked(g)
    finish(first)
    w = jnp.concatenate([fv[w].reshape(1024, B) for w in range(4)], 1)
    z = y_ref[...] - product(gs, w, NND)
    z = jnp.where(row_mask(meta, level, n), z, 0.0)
    finish(early)
    finish(late)
    back(meta, level, n, ev, z, x_out)


SMEM = pl.BlockSpec(memory_space=pltpu.SMEM)
VMEM = pl.BlockSpec(memory_space=pltpu.VMEM)
ANY = pl.BlockSpec(memory_space=pl.ANY)


def call(kernel, name, shapes, scratch, meta, small, weights=(), flops=0):
    weights = [pltpu.with_memory_space_constraint(w, pltpu.HBM) for w in weights]
    moved = sum(w.size * 4 for w in weights) + sum(v.size * 4 for v in small)
    return pl.pallas_call(
        kernel,
        out_shape=[jax.ShapeDtypeStruct(s, f32) for s in shapes],
        in_specs=[SMEM] + [VMEM] * len(small) + [ANY] * len(weights),
        out_specs=[VMEM] * len(shapes),
        scratch_shapes=scratch,
        compiler_params=pltpu.CompilerParams(vmem_limit_bytes=(14 if flops else 3) * 2**20),
        cost_estimate=pl.CostEstimate(flops=flops, bytes_accessed=moved, transcendentals=0),
        name=name,
    )(meta, *small, *weights)


def local(
    live_tiles, row_tiles, rhs0, rhs1, rhs2, rhs3, dinv0, dinv1, dinv2, dinv3, off0, off1, off2
):
    ci, x0, x1 = lax.axis_index("core"), lax.axis_index("x0"), lax.axis_index("x1")
    zi = lax.axis_index("z")
    leaf = x1 * 4 + x0 * 2 + ci
    here = leaf * 16 + zi * 4 + lax.axis_index("y")
    meta = jnp.concatenate([here.reshape(1), live_tiles, row_tiles.reshape(-1)])
    bits = [("core", ci), ("x0", x0), ("x1", x1)]

    def joined(v, i, dim=0):
        axis, bit = bits[i]
        return ordered(v, flip(v, axis), bit, dim)

    def pick(v, i, dim=0):
        return lax.dynamic_index_in_dim(v, i, dim, keepdims=False)

    def for_z(pair, other, bit):
        blocks = []
        for s in range(4):
            z = (zi + s) % 4
            blocks.append(jnp.where(z // 2 == bit, pick(pair, z % 2), pick(other, z % 2)))
        return blocks

    def over_z(blocks):
        return [blocks[0]] + [shift(blocks[s], "z", s) for s in (1, 2, 3)]

    def gathered(blocks, f):
        parts = [v[None] for v in blocks] + ([] if f is None else [f.reshape(2, 256, B)])
        return lax.all_gather(jnp.concatenate(parts, 0), "y", axis=0, tiled=False)

    gate = lax.optimization_barrier
    off0 = off0.reshape(4, 256, B)
    fa, fb = shift(off0, "z", 1), shift(off0, "z", -1)
    fc, fd = shift(fa[:2], "z", 1), shift(fb[2:], "z", -1)
    e0 = jnp.swapaxes(dinv0.reshape(4, 4, B, B), 0, 1).reshape(4, 512, B)
    e0 = lax.all_to_all(e0, "y", 0, 0, tiled=True)
    e1 = dinv1.reshape(2, 2, 256, B)
    e1 = over_z(for_z(pick(e1, ci, 1), flip(pick(e1, 1 - ci, 1), "core"), ci))
    e2 = dinv2.reshape(2, 256, B)
    e2 = ordered(pick(e2, ci)[None], flip(pick(e2, 1 - ci)[None], "core"), ci, 0)
    e2_other = flip(e2, "x0")
    e3 = joined(dinv3[None], 1)
    e3_other = flip(e3, "x1")
    e0, e1, e2, e2_other, e3, e3_other, fa, fb, fc, fd, off2, rhs0, rhs1 = gate(
        (e0, e1, e2, e2_other, e3, e3_other, fa, fb, fc, fd, off2, rhs0, rhs1)
    )
    m1 = gathered(e1, off1)

    ea, eb = shift(e0, "z", 1), shift(e0, "z", -1)
    f2 = joined(off2, 1)
    e23 = zip(for_z(e2, e2_other, x0), for_z(e3, e3_other, x1))
    e23 = over_z([jnp.stack(pair) for pair in e23])
    b_mine, b_other = halves(jnp.concatenate([rhs1, rhs2, rhs3], 1), ci)
    b_other = flip(b_other, "core")
    ea, eb, e23, f2, b_mine, b_other = gate((ea, eb, e23, f2, b_mine, b_other))

    ec, ed = shift(ea[:2], "z", 1), shift(eb[2:], "z", -1)
    m2 = gathered([v[0] for v in e23], f2)
    c0 = gather4(rhs0, "y")
    ec, ed, c0 = gate((ec, ed, c0))
    w0 = [e0, ea, eb, ec, ed, off0, fa, fb, fc, fd]

    dma = pltpu.SemaphoreType.DMA
    ev, fv = pltpu.VMEM((4, 4, 512, B), f32), pltpu.VMEM((4, 4, 256, B), f32)

    def work(n):
        return [pltpu.VMEM((n, ORDER), f32), pltpu.VMEM((n, 512), f32), pltpu.VMEM((n, 1024), f32)]

    def flops(n):
        return 2 * n * 512 * (2048 + 1024) * 12

    y0, *u = call(
        functools.partial(forward_kernel, 0, 64, "rs"), "f0", [(64, 512)] + [(16, 1024)] * 4,
        [ev, fv, *work(64), dma((10,))], meta, c0, w0, flops(64),
    )
    parts = scatter4(u, "y")
    u = (parts[0] + parts[1]) + (parts[2] + parts[3])
    e23, _ = gate((e23, u))
    m3 = gathered([v[1] for v in e23], None)
    keep, give = halves(u, ci)
    c1, pk, pg = call(
        s01_kernel, "s01", [(8, ORDER), (2, 4, ORDER), (2, 4, ORDER)],
        [pltpu.VMEM((3, 8, ORDER), f32)], meta, [keep, flip(give, "core"), b_mine, b_other],
    )
    m1, _ = gate((m1, c1))
    w1 = m1, flip(m1, "core")
    pr = flip(pg, "x0")
    y1, keep, give = call(
        functools.partial(forward_kernel, 1, 32, "ar"), "f1", [(32, 512), (16, 1024), (16, 1024)],
        [ev, fv, *work(32), dma((12,))], meta, gather4(c1, "z"), w1, flops(32),
    )
    part, keep3, give3 = call(
        s12_kernel, "s12", [(16, ORDER), (8, ORDER), (8, ORDER)],
        [pltpu.VMEM((2, 16, ORDER), f32)], meta, [keep, flip(give, "x0"), pk, pr],
    )
    m2, _ = gate((m2, part))
    w2 = m2, flip(m2, "core")
    recv3 = flip(give3, "x1")
    y2, keep, give = call(
        functools.partial(forward_kernel, 2, 16, "ar"), "f2", [(16, 512), (8, 1024), (8, 1024)],
        [ev, fv, *work(16), dma((12,))], meta, gather4(part, "z"), w2, flops(16),
    )
    (part,) = call(
        s23_kernel, "s23", [(8, ORDER)],
        [pltpu.VMEM((1, 8, ORDER), f32)], meta, [keep, flip(give, "x1"), keep3, recv3],
    )

    m3, _ = gate((m3, part))
    w3 = m3, flip(m3, "core")
    (part,) = call(
        top_kernel, "top", [(8, ORDER)], [ev, pltpu.VMEM((8, 512), f32), dma((8,))],
        meta, gather4(part, "z"), w3, flops(8),
    )
    (x3,) = call(x3_kernel, "x3", [(8, ORDER)], [], meta, gather4(part, "z"))
    x3r = flip(x3, "x1")

    def rest(n):
        rows = n if n != 16 else 8
        return [ev, fv, pltpu.VMEM((rows, 1024), f32), pltpu.VMEM((n // 2, 1024), f32), dma((12,))]

    (part,) = call(
        functools.partial(backward_kernel, 2, 16), "b2", [(16, ORDER)], rest(16),
        meta, [x3[None], x3r[None], y2], w2, flops(16),
    )
    anc, give = call(
        x2_kernel, "x2", [(2, 16, ORDER), (16, 1024)], [],
        meta, gather4(part, "z") + [x3, x3r],
    )
    recv = flip(give, "x0")
    a_mine = anc[:, :4]
    a_other = flip(a_mine, "x0")
    parts = call(
        functools.partial(backward_kernel, 1, 32), "b1", [(8, ORDER)] * 4, rest(32),
        meta, [anc, recv, y1], w1, flops(32),
    )
    anc, give, own = call(
        x1_kernel, "x1", [(3, 8, ORDER), (8, 1024), (8, 1024)], [],
        meta, scatter4(parts, "z") + [a_mine, a_other],
    )
    g = ordered(own, flip(give, "core"), ci, 0)
    parts = call(
        functools.partial(backward_kernel, 0, 64), "b0", [(16, ORDER)] * 4, rest(64),
        meta, gather4(g, "y") + [y0], w0, flops(64),
    )
    parts = scatter4(parts, "y")
    sol0 = (parts[0] + parts[1]) + (parts[2] + parts[3])

    outs = [sol0]
    for k in (1, 2, 3):
        width = ORDER // 2**k
        place = leaf % 2**k
        mine = lax.dynamic_slice_in_dim(anc[k - 1], place * width, width, 1)
        give = lax.dynamic_slice_in_dim(anc[k - 1], (place ^ 1) * width, width, 1)
        outs.append(ordered(mine, flip(give, "core"), ci, 0))
    return tuple(outs)


def solution(mesh):
    fine = Mesh(mesh.devices.reshape(2, 2, 2, 4, 4), ("x1", "x0", "core", "z", "y"))
    leaf, panel = ("x1", "x0", "core"), ("z", "y")
    return jax.shard_map(
        local,
        mesh=fine,
        in_specs=(P(), P()) + (P(panel, leaf),) * 4 + (P(leaf, panel),) * 7,
        out_specs=(P(panel, leaf),) * 4,
        check_vma=False,
    )
```

```python
import functools
import jax
import jax.numpy as jnp
from jax import lax
from jax.experimental import pallas as pl
from jax.experimental.pallas import tpu as pltpu
from jax.sharding import Mesh, PartitionSpec as P

B = 128
ORDER = 2048
NT = 16
f32 = jnp.float32
bf16 = jnp.bfloat16

FIRST = (0, 8, 12, 14)


class Place:
    def __init__(self, meta):
        self.meta = meta
        self.leaf = meta[0] >> 4
        self.zi, self.yi = (meta[0] >> 2) & 3, meta[0] & 3
        self.ci, self.x0, self.x1 = self.leaf & 1, (self.leaf >> 1) & 1, self.leaf >> 2

    def live(self, level):
        return self.meta[1 + FIRST[level] + (self.leaf >> level)]

    def own(self, level):
        return 16 + 8 * (FIRST[level] + (self.leaf >> level))

    def partner(self, level):
        return 16 + 8 * (FIRST[level] + ((self.leaf >> level) ^ 1))

    def bit(self, level):
        return (self.ci, self.x0, self.x1)[level]


def shift(v, axis, s):
    return lax.ppermute(v, axis, [(i, (i + s) % 4) for i in range(4)])


def flip(v, axis):
    return lax.ppermute(v, axis, [(0, 1), (1, 0)])


def gather4(v, axis):
    far = shift(v, axis, 2)
    return [v, shift(v, axis, 1), far, shift(v, axis, 3)]


def scatter4(parts, axis):
    far = shift(parts[2], axis, 2)
    return [parts[0], shift(parts[1], axis, -1), far, shift(parts[3], axis, 1)]


def ring(v, axis, dim):
    h = v.shape[dim] // 2
    a = shift(v, axis, 1)
    b = shift(v, axis, -1)
    c = shift(lax.slice_in_dim(a, 0, h, axis=dim), axis, 1)
    d = shift(lax.slice_in_dim(b, h, 2 * h, axis=dim), axis, -1)
    return [v, a, b, c, d]


def ordered(mine, other, bit, dim):
    return jnp.where(
        bit == 0, jnp.concatenate([mine, other], dim), jnp.concatenate([other, mine], dim)
    )


def halves(v, bit):
    h = v.shape[0] // 2
    return (
        jnp.where(bit == 0, v[:h], v[h:]),
        jnp.where(bit == 0, v[h:], v[:h]),
    )


def stacked(v):
    hi = v.astype(bf16).astype(f32)
    return jnp.concatenate([hi, v - hi], 0).astype(bf16)


def product(left, w, dims):
    hi = w.astype(bf16)
    lo = (w - hi.astype(f32)).astype(bf16)
    r = lax.dot_general(left, hi, (dims, ((), ())), preferred_element_type=f32)
    r = r + lax.dot_general(left, lo, (dims, ((), ())), preferred_element_type=f32)
    n = left.shape[0] // 2
    return r[:n] + r[n:]


NTD = ((1,), (1,))
NND = ((1,), (0,))


def copies_first(meta, refs, ev, fv, sems):
    e, f = refs[:5], refs[5:]
    zi = Place(meta).zi
    spots = [zi, lax.rem(zi + 3, 4), lax.rem(zi + 1, 4)]
    far = lax.rem(zi + 2, 4)
    pairs_e = [(ref, ev.at[w]) for ref, w in zip(e[:3], spots)]
    pairs_e += [(e[3], ev.at[far, 0:2]), (e[4], ev.at[far, 2:4])]
    pairs_f = [(ref, fv.at[w]) for ref, w in zip(f[:3], spots)]
    pairs_f += [(f[3], fv.at[far, 0:2]), (f[4], fv.at[far, 2:4])]
    made = [
        pltpu.make_async_copy(src, dst, sems.at[k]) for k, (src, dst) in enumerate(pairs_e + pairs_f)
    ]
    return made[:5], [], made[5:]


def copies_upper(level, meta, bufs, ev, fv, sems):
    place = Place(meta)
    groups = ([], [], [])
    k = 0
    for i, q in ((0, place.ci), (1, 1 - place.ci)):
        rows = pl.ds(pl.multiple_of(q * 256, 256), 256)
        pairs = [(bufs[i].at[:, s], ev.at[:, lax.rem(place.zi + 4 - s, 4), rows]) for s in range(4)]
        late = []
        if level == 1:
            late = [(bufs[i].at[:, 4:6], fv.at[:, pl.ds(2 * q, 2)])]
        elif level == 2:
            late = [(bufs[i].at[:, 4 + h], fv.at[:, 2 * h + q]) for h in (0, 1)]
        for group, some in ((groups[i], pairs), (groups[2], late)):
            for src, dst in some:
                group.append(pltpu.make_async_copy(src, dst, sems.at[k]))
                k += 1
    return groups


def copies(level, meta, refs, ev, fv, sems):
    if level == 0:
        return copies_first(meta, refs, ev, fv, sems)
    return copies_upper(level, meta, refs, ev, fv, sems)


def finish(group):
    for c in group:
        c.wait()


def tiles_in_order(level):
    if level == 0:
        return [(t // 4, t % 4) for t in range(NT)]
    return [(t % 4, t // 4) for t in range(NT)]


def column_mask(meta, level, n):
    col = lax.broadcasted_iota(jnp.int32, (n, ORDER), 1)
    return col < Place(meta).live(level) * B


def row_mask(meta, level, n):
    own = lax.broadcasted_iota(jnp.int32, (n, 512), 1) // B
    place = Place(meta)
    tile = 4 * own + place.yi if level == 0 else 4 * place.zi + own
    return tile < Place(meta).live(level)


def solve_rows(level, meta, ev, yv, cs, late):
    first = Place(meta).ci if level else 0

    def body(j, carry):
        @pl.when(j == 1)
        def _():
            finish(late)

        at = pl.multiple_of(jnp.where(j == 0, first, 1 - first) * 256, 256)
        rows = pl.ds(at, 256)
        w = jnp.concatenate([ev[w, s, rows, :] for w, s in tiles_in_order(level)], 1)
        yv[:, rows] = product(cs, w, NTD)
        return carry

    lax.fori_loop(0, 2, body, 0)


WEIGHTS = (10, 2, 2, 2)


def forward_kernel(level, n, mode, meta, *refs):
    count = WEIGHTS[level]
    c_refs, refs = refs[:4], refs[4:]
    w_refs, refs = refs[:count], refs[count:]
    if mode == "rs":
        y_out, u_out = refs[0], refs[1:5]
        refs = refs[5:]
    else:
        y_out, keep_out, give_out = refs[:3]
        refs = refs[3:]
    ev, fv, cv, yv, uv, sems = refs
    early, late, last = copies(level, meta, w_refs, ev, fv, sems)
    for c in [*early, *late, *last]:
        c.start()
    r = n // 4
    if level < 2:
        for s in range(4):
            cv[pl.ds(s * r, r), :] = c_refs[s][...]
        c = cv[...]
    else:
        c = summed(c_refs, r)
    cs = stacked(jnp.where(column_mask(meta, level, n), c, 0.0))
    finish(early)
    solve_rows(level, meta, ev, yv, cs, late)
    y = jnp.where(row_mask(meta, level, n), yv[...], 0.0)
    y_out[...] = y
    ys = stacked(y)
    finish(last)

    def body(j, carry):
        w = jnp.concatenate([fv[w, j] for w in range(4)], 1)
        uv[:, pl.ds(pl.multiple_of(j * 256, 256), 256)] = product(ys, w, NTD)
        return carry

    lax.fori_loop(0, 4, body, 0)
    if mode == "rs":
        for s in range(4):
            u_out[s][...] = uv[pl.ds(s * r, r), :]
    else:
        split_rows(uv, r, Place(meta).bit(level), keep_out, give_out)


def split_rows(v, r, bit, keep_out, give_out):
    h = r // 2
    for s in range(4):
        low = v[pl.ds(s * r, h), :]
        high = v[pl.ds(s * r + h, h), :]
        keep_out[pl.ds(s * h, h), :] = jnp.where(bit == 0, low, high)
        give_out[pl.ds(s * h, h), :] = jnp.where(bit == 0, high, low)


def summed(refs, r):
    parts = []
    for s in range(4):
        total = refs[0][pl.ds(s * r, r), :]
        for d in (1, 2, 3):
            total = total + refs[d][pl.ds((s - d) % 4 * r, r), :]
        parts.append(total)
    return jnp.concatenate(parts, 0)


def add_tiles(meta, at, src, acc):
    for t in range(8):
        v = meta[at + t]
        cols = pl.ds(pl.multiple_of(lax.rem(v, NT) * B, B), B)
        lev = lax.div(v, NT)
        acc[lev, :, cols] = acc[lev, :, cols] + src[:, t * B : (t + 1) * B]


def take_tiles(meta, at, anc, dst):
    for t in range(8):
        v = meta[at + t]
        cols = pl.ds(pl.multiple_of(lax.rem(v, NT) * B, B), B)
        dst[:, t * B : (t + 1) * B] = anc[lax.div(v, NT), :, cols]


def s01_kernel(meta, keep, recv, b_mine, b_other, c1, pk, pg, acc):
    place = Place(meta)
    acc[...] = jnp.zeros_like(acc)
    add_tiles(meta, place.own(0), keep, acc)
    add_tiles(meta, place.partner(0), recv, acc)
    group = (0, place.x0, place.leaf >> 1)
    for ref, c in ((b_mine, place.ci), (b_other, 1 - place.ci)):
        at = 0
        for i in range(3):
            width = 1024 >> i
            cols = pl.ds(pl.multiple_of((2 * group[i] + c) * width, width), width)
            acc[i, :, cols] = acc[i, :, cols] - ref[:, at : at + width]
            at += width
    c1[...] = -acc[0]
    for i in (0, 1):
        low, high = acc[i + 1, 0:4, :], acc[i + 1, 4:8, :]
        pk[i] = jnp.where(place.x0 == 0, low, high)
        pg[i] = jnp.where(place.x0 == 0, high, low)


def s12_kernel(meta, keep, recv, pk, pr, part, keep3, give3, acc):
    place = Place(meta)
    acc[...] = jnp.zeros_like(acc)
    add_tiles(meta, place.own(1), keep, acc)
    add_tiles(meta, place.partner(1), recv, acc)
    for i in (0, 1):
        acc[i, 0:4, :] = acc[i, 0:4, :] + (pk[i] + pr[i])
    part[...] = -acc[0]
    split_rows(acc.at[1], 4, place.x1, keep3, give3)


def s23_kernel(meta, keep, recv, keep3, recv3, part, acc):
    place = Place(meta)
    acc[...] = jnp.zeros_like(acc)
    add_tiles(meta, place.own(2), keep, acc)
    add_tiles(meta, place.partner(2), recv, acc)
    part[...] = -(acc[0] + (keep3[...] + recv3[...]))


def top_kernel(meta, c0, c1, c2, c3, *refs):
    w_refs, (x_out, ev, yv, sems) = refs[:2], refs[2:]
    early, late, _ = copies(3, meta, w_refs, ev, None, sems)
    for c in [*early, *late]:
        c.start()
    c = summed((c0, c1, c2, c3), 2)
    cs = stacked(jnp.where(column_mask(meta, 3, 8), c, 0.0))
    finish(early)
    solve_rows(3, meta, ev, yv, cs, late)
    back(meta, 3, 8, ev, jnp.where(row_mask(meta, 3, 8), yv[...], 0.0), [x_out])


def back(meta, level, n, ev, z, x_out):
    zs = stacked(z)
    live = Place(meta).live(level) * B

    def body(j, carry):
        cols = pl.ds(pl.multiple_of(j * 512, 512), 512)
        w = jnp.concatenate([ev[j, i] if level == 0 else ev[i, j] for i in range(4)], 1)
        v = product(zs, w, NND)
        col = lax.broadcasted_iota(jnp.int32, (n, 512), 1) + j * 512
        v = jnp.where(col < live, v, 0.0)
        r = n // len(x_out)
        for s, out in enumerate(x_out):
            out[:, cols] = v[s * r : (s + 1) * r]
        return carry

    lax.fori_loop(0, 4, body, 0)


def x3_kernel(meta, c0, c1, c2, c3, x_out):
    x_out[...] = summed((c0, c1, c2, c3), 2)


def merged(a, b, h, bit):
    parts = []
    for s in range(4):
        u, v = a[s * h : (s + 1) * h, :], b[s * h : (s + 1) * h, :]
        parts += [jnp.where(bit == 0, u, v), jnp.where(bit == 0, v, u)]
    return jnp.concatenate(parts, 0)


def x2_kernel(meta, c0, c1, c2, c3, x3, x3r, anc_out, give):
    anc_out[0] = summed((c0, c1, c2, c3), 4)
    anc_out[1] = merged(x3[...], x3r[...], 2, Place(meta).x1)
    take_tiles(meta, Place(meta).partner(1), anc_out, give)


def x1_kernel(meta, c0, c1, c2, c3, a_mine, a_other, anc_out, give, own):
    anc_out[0] = (c0[...] + c1[...]) + (c2[...] + c3[...])
    for i in (0, 1):
        u, v = a_mine[i], a_other[i]
        bit = Place(meta).x0
        anc_out[i + 1, 0:4, :] = jnp.where(bit == 0, u, v)
        anc_out[i + 1, 4:8, :] = jnp.where(bit == 0, v, u)
    take_tiles(meta, Place(meta).partner(0), anc_out, give)
    take_tiles(meta, Place(meta).own(0), anc_out, own)


def backward_kernel(level, n, meta, *refs):
    count = WEIGHTS[level]
    if level == 0:
        g_refs, refs = refs[:4], refs[4:]
    else:
        (anc, recv), refs = refs[:2], refs[2:]
    y_ref, refs = refs[0], refs[1:]
    w_refs, refs = refs[:count], refs[count:]
    x_out, (ev, fv, gv, ov, sems) = refs[:-5], refs[-5:]
    early, late, first = copies(level, meta, w_refs, ev, fv, sems)
    for c in [*first, *early, *late]:
        c.start()
    r = n // 4
    if level == 0:
        for s in range(4):
            gv[pl.ds(s * r, r), :] = g_refs[s][...]
        g = gv[...]
    else:
        take_tiles(meta, Place(meta).own(level), anc, ov)
        if level == 2:
            take_tiles(meta, Place(meta).own(level), recv, gv)
            recv = gv
        g = merged(ov[...], recv[...], r // 2, Place(meta).bit(level))
    gs = stacked(g)
    finish(first)
    w = jnp.concatenate([fv[w].reshape(1024, B) for w in range(4)], 1)
    z = y_ref[...] - product(gs, w, NND)
    z = jnp.where(row_mask(meta, level, n), z, 0.0)
    finish(early)
    finish(late)
    back(meta, level, n, ev, z, x_out)


SMEM = pl.BlockSpec(memory_space=pltpu.SMEM)
VMEM = pl.BlockSpec(memory_space=pltpu.VMEM)
ANY = pl.BlockSpec(memory_space=pl.ANY)


def call(kernel, name, shapes, scratch, meta, small, weights=(), flops=0):
    weights = [pltpu.with_memory_space_constraint(w, pltpu.HBM) for w in weights]
    moved = sum(w.size * 4 for w in weights) + sum(v.size * 4 for v in small)
    return pl.pallas_call(
        kernel,
        out_shape=[jax.ShapeDtypeStruct(s, f32) for s in shapes],
        in_specs=[SMEM] + [VMEM] * len(small) + [ANY] * len(weights),
        out_specs=[VMEM] * len(shapes),
        scratch_shapes=scratch,
        compiler_params=pltpu.CompilerParams(vmem_limit_bytes=(14 if flops else 3) * 2**20),
        cost_estimate=pl.CostEstimate(flops=flops, bytes_accessed=moved, transcendentals=0),
        name=name,
    )(meta, *small, *weights)


def local(
    live_tiles, row_tiles, rhs0, rhs1, rhs2, rhs3, dinv0, dinv1, dinv2, dinv3, off0, off1, off2
):
    ci, x0, x1 = lax.axis_index("core"), lax.axis_index("x0"), lax.axis_index("x1")
    zi = lax.axis_index("z")
    leaf = x1 * 4 + x0 * 2 + ci
    here = leaf * 16 + zi * 4 + lax.axis_index("y")
    meta = jnp.concatenate([here.reshape(1), live_tiles, row_tiles.reshape(-1)])
    bits = [("core", ci), ("x0", x0), ("x1", x1)]

    def joined(v, i, dim=0):
        axis, bit = bits[i]
        return ordered(v, flip(v, axis), bit, dim)

    def pick(v, i, dim=0):
        return lax.dynamic_index_in_dim(v, i, dim, keepdims=False)

    def for_z(pair, other, bit):
        blocks = []
        for s in range(4):
            z = (zi + s) % 4
            blocks.append(jnp.where(z // 2 == bit, pick(pair, z % 2), pick(other, z % 2)))
        return blocks

    def over_z(blocks):
        return [blocks[0]] + [shift(blocks[s], "z", s) for s in (1, 2, 3)]

    def packed(blocks, f=None):
        parts = [v[None] for v in blocks] + ([] if f is None else [f.reshape(2, 256, B)])
        return jnp.concatenate(parts, 0)

    def gathered(block):
        return lax.all_gather(block, "y", axis=0, tiled=False)

    gate = lax.optimization_barrier
    off0 = off0.reshape(4, 256, B)
    fa, fb = shift(off0, "z", 1), shift(off0, "z", -1)
    fc, fd = shift(fa[:2], "z", 1), shift(fb[2:], "z", -1)
    e0 = jnp.swapaxes(dinv0.reshape(4, 4, B, B), 0, 1).reshape(4, 512, B)
    e0 = lax.all_to_all(e0, "y", 0, 0, tiled=True)
    e1 = dinv1.reshape(2, 2, 256, B)
    e1 = over_z(for_z(pick(e1, ci, 1), flip(pick(e1, 1 - ci, 1), "core"), ci))
    e2 = dinv2.reshape(2, 256, B)
    e2 = ordered(pick(e2, ci)[None], flip(pick(e2, 1 - ci)[None], "core"), ci, 0)
    e2_other = flip(e2, "x0")
    e0, e1, e2, e2_other, fa, fb, fc, fd, off2, dinv3, rhs0, rhs1 = gate(
        (e0, e1, e2, e2_other, fa, fb, fc, fd, off2, dinv3, rhs0, rhs1)
    )
    m1 = gathered(packed(e1, off1))

    ea, eb = shift(e0, "z", 1), shift(e0, "z", -1)
    f2 = joined(off2, 1)
    e3 = joined(dinv3[None], 1)
    e3_other = flip(e3, "x1")
    e23 = zip(for_z(e2, e2_other, x0), for_z(e3, e3_other, x1))
    e23 = over_z([jnp.stack(pair) for pair in e23])
    b_mine, b_other = halves(jnp.concatenate([rhs1, rhs2, rhs3], 1), ci)
    b_other = flip(b_other, "core")
    ea, eb, e23, f2, b_mine, b_other = gate((ea, eb, e23, f2, b_mine, b_other))

    ec, ed = shift(ea[:2], "z", 1), shift(eb[2:], "z", -1)
    m2 = gathered(packed([v[0] for v in e23], f2))
    c0 = gather4(rhs0, "y")
    ec, ed, c0 = gate((ec, ed, c0))
    w0 = [e0, ea, eb, ec, ed, off0, fa, fb, fc, fd]

    dma = pltpu.SemaphoreType.DMA
    ev, fv = pltpu.VMEM((4, 4, 512, B), f32), pltpu.VMEM((4, 4, 256, B), f32)

    def work(n):
        return [pltpu.VMEM((n, ORDER), f32), pltpu.VMEM((n, 512), f32), pltpu.VMEM((n, 1024), f32)]

    def flops(n):
        return 2 * n * 512 * (2048 + 1024) * 12

    y0, *u = call(
        functools.partial(forward_kernel, 0, 64, "rs"), "f0", [(64, 512)] + [(16, 1024)] * 4,
        [ev, fv, *work(64), dma((10,))], meta, c0, w0, flops(64),
    )
    parts = scatter4(u, "y")
    u = (parts[0] + parts[1]) + (parts[2] + parts[3])
    e3, u = gate((packed([v[1] for v in e23]), u))
    m3 = gathered(e3)
    keep, give = halves(u, ci)
    c1, pk, pg = call(
        s01_kernel, "s01", [(8, ORDER), (2, 4, ORDER), (2, 4, ORDER)],
        [pltpu.VMEM((3, 8, ORDER), f32)], meta, [keep, flip(give, "core"), b_mine, b_other],
    )
    m1, _ = gate((m1, c1))
    w1 = m1, flip(m1, "core")
    pr = flip(pg, "x0")
    y1, keep, give = call(
        functools.partial(forward_kernel, 1, 32, "ar"), "f1", [(32, 512), (16, 1024), (16, 1024)],
        [ev, fv, *work(32), dma((12,))], meta, gather4(c1, "z"), w1, flops(32),
    )
    part, keep3, give3 = call(
        s12_kernel, "s12", [(16, ORDER), (8, ORDER), (8, ORDER)],
        [pltpu.VMEM((2, 16, ORDER), f32)], meta, [keep, flip(give, "x0"), pk, pr],
    )
    m2, _ = gate((m2, part))
    w2 = m2, flip(m2, "core")
    recv3 = flip(give3, "x1")
    y2, keep, give = call(
        functools.partial(forward_kernel, 2, 16, "ar"), "f2", [(16, 512), (8, 1024), (8, 1024)],
        [ev, fv, *work(16), dma((12,))], meta, gather4(part, "z"), w2, flops(16),
    )
    (part,) = call(
        s23_kernel, "s23", [(8, ORDER)],
        [pltpu.VMEM((1, 8, ORDER), f32)], meta, [keep, flip(give, "x1"), keep3, recv3],
    )

    m3, _ = gate((m3, part))
    w3 = m3, flip(m3, "core")
    (part,) = call(
        top_kernel, "top", [(8, ORDER)], [ev, pltpu.VMEM((8, 512), f32), dma((8,))],
        meta, gather4(part, "z"), w3, flops(8),
    )
    (x3,) = call(x3_kernel, "x3", [(8, ORDER)], [], meta, gather4(part, "z"))
    x3r = flip(x3, "x1")

    def rest(n):
        rows = n if n != 16 else 8
        return [ev, fv, pltpu.VMEM((rows, 1024), f32), pltpu.VMEM((n // 2, 1024), f32), dma((12,))]

    (part,) = call(
        functools.partial(backward_kernel, 2, 16), "b2", [(16, ORDER)], rest(16),
        meta, [x3[None], x3r[None], y2], w2, flops(16),
    )
    anc, give = call(
        x2_kernel, "x2", [(2, 16, ORDER), (16, 1024)], [],
        meta, gather4(part, "z") + [x3, x3r],
    )
    recv = flip(give, "x0")
    a_mine = anc[:, :4]
    a_other = flip(a_mine, "x0")
    parts = call(
        functools.partial(backward_kernel, 1, 32), "b1", [(8, ORDER)] * 4, rest(32),
        meta, [anc, recv, y1], w1, flops(32),
    )
    anc, give, own = call(
        x1_kernel, "x1", [(3, 8, ORDER), (8, 1024), (8, 1024)], [],
        meta, scatter4(parts, "z") + [a_mine, a_other],
    )
    g = ordered(own, flip(give, "core"), ci, 0)
    parts = call(
        functools.partial(backward_kernel, 0, 64), "b0", [(16, ORDER)] * 4, rest(64),
        meta, gather4(g, "y") + [y0], w0, flops(64),
    )
    parts = scatter4(parts, "y")
    sol0 = (parts[0] + parts[1]) + (parts[2] + parts[3])

    outs = [sol0]
    for k in (1, 2, 3):
        width = ORDER // 2**k
        place = leaf % 2**k
        mine = lax.dynamic_slice_in_dim(anc[k - 1], place * width, width, 1)
        give = lax.dynamic_slice_in_dim(anc[k - 1], (place ^ 1) * width, width, 1)
        outs.append(ordered(mine, flip(give, "core"), ci, 0))
    return tuple(outs)


def solution(mesh):
    fine = Mesh(mesh.devices.reshape(2, 2, 2, 4, 4), ("x1", "x0", "core", "z", "y"))
    leaf, panel = ("x1", "x0", "core"), ("z", "y")
    return jax.shard_map(
        local,
        mesh=fine,
        in_specs=(P(), P()) + (P(panel, leaf),) * 4 + (P(leaf, panel),) * 7,
        out_specs=(P(panel, leaf),) * 4,
        check_vma=False,
    )
```

```python
import functools
import jax
import jax.numpy as jnp
from jax import lax
from jax.experimental import pallas as pl
from jax.experimental.pallas import tpu as pltpu
from jax.sharding import Mesh, PartitionSpec as P

B = 128
ORDER = 2048
NT = 16
f32 = jnp.float32
bf16 = jnp.bfloat16

FIRST = (0, 8, 12, 14)


class Place:
    def __init__(self, meta):
        self.meta = meta
        self.leaf = meta[0] >> 4
        self.zi, self.yi = (meta[0] >> 2) & 3, meta[0] & 3
        self.ci, self.x0, self.x1 = self.leaf & 1, (self.leaf >> 1) & 1, self.leaf >> 2

    def live(self, level):
        return self.meta[1 + FIRST[level] + (self.leaf >> level)]

    def own(self, level):
        return 16 + 8 * (FIRST[level] + (self.leaf >> level))

    def partner(self, level):
        return 16 + 8 * (FIRST[level] + ((self.leaf >> level) ^ 1))

    def bit(self, level):
        return (self.ci, self.x0, self.x1)[level]


def shift(v, axis, s):
    return lax.ppermute(v, axis, [(i, (i + s) % 4) for i in range(4)])


def flip(v, axis):
    return lax.ppermute(v, axis, [(0, 1), (1, 0)])


def gather4(v, axis):
    far = shift(v, axis, 2)
    return [v, shift(v, axis, 1), far, shift(v, axis, 3)]


def scatter4(parts, axis):
    far = shift(parts[2], axis, 2)
    return [parts[0], shift(parts[1], axis, -1), far, shift(parts[3], axis, 1)]


def ring(v, axis, dim):
    h = v.shape[dim] // 2
    a = shift(v, axis, 1)
    b = shift(v, axis, -1)
    c = shift(lax.slice_in_dim(a, 0, h, axis=dim), axis, 1)
    d = shift(lax.slice_in_dim(b, h, 2 * h, axis=dim), axis, -1)
    return [v, a, b, c, d]


def ordered(mine, other, bit, dim):
    return jnp.where(
        bit == 0, jnp.concatenate([mine, other], dim), jnp.concatenate([other, mine], dim)
    )


def halves(v, bit):
    h = v.shape[0] // 2
    return (
        jnp.where(bit == 0, v[:h], v[h:]),
        jnp.where(bit == 0, v[h:], v[:h]),
    )


def stacked(v):
    hi = v.astype(bf16).astype(f32)
    return jnp.concatenate([hi, v - hi], 0).astype(bf16)


def product(left, w, dims):
    hi = w.astype(bf16)
    lo = (w - hi.astype(f32)).astype(bf16)
    r = lax.dot_general(left, hi, (dims, ((), ())), preferred_element_type=f32)
    r = r + lax.dot_general(left, lo, (dims, ((), ())), preferred_element_type=f32)
    n = left.shape[0] // 2
    return r[:n] + r[n:]


NTD = ((1,), (1,))
NND = ((1,), (0,))


def copies_first(meta, refs, ev, fv, sems):
    e, f = refs[:5], refs[5:]
    zi = Place(meta).zi
    spots = [zi, lax.rem(zi + 3, 4), lax.rem(zi + 1, 4)]
    far = lax.rem(zi + 2, 4)
    pairs_e = [(ref, ev.at[w]) for ref, w in zip(e[:3], spots)]
    pairs_e += [(e[3], ev.at[far, 0:2]), (e[4], ev.at[far, 2:4])]
    pairs_f = [(ref, fv.at[w]) for ref, w in zip(f[:3], spots)]
    pairs_f += [(f[3], fv.at[far, 0:2]), (f[4], fv.at[far, 2:4])]
    made = [
        pltpu.make_async_copy(src, dst, sems.at[k]) for k, (src, dst) in enumerate(pairs_e + pairs_f)
    ]
    return made[:5], [], made[5:]


def copies_upper(level, meta, bufs, ev, fv, sems):
    place = Place(meta)
    groups = ([], [], [])
    k = 0
    for i, q in ((0, place.ci), (1, 1 - place.ci)):
        rows = pl.ds(pl.multiple_of(q * 256, 256), 256)
        pairs = [(bufs[i].at[:, s], ev.at[:, lax.rem(place.zi + 4 - s, 4), rows]) for s in range(4)]
        late = []
        if level == 1:
            late = [(bufs[i].at[:, 4:6], fv.at[:, pl.ds(2 * q, 2)])]
        elif level == 2:
            late = [(bufs[i].at[:, 4 + h], fv.at[:, 2 * h + q]) for h in (0, 1)]
        for group, some in ((groups[i], pairs), (groups[2], late)):
            for src, dst in some:
                group.append(pltpu.make_async_copy(src, dst, sems.at[k]))
                k += 1
    return groups


def copies(level, meta, refs, ev, fv, sems):
    if level == 0:
        return copies_first(meta, refs, ev, fv, sems)
    return copies_upper(level, meta, refs, ev, fv, sems)


def finish(group):
    for c in group:
        c.wait()


def tiles_in_order(level):
    if level == 0:
        return [(t // 4, t % 4) for t in range(NT)]
    return [(t % 4, t // 4) for t in range(NT)]


def column_mask(meta, level, n):
    col = lax.broadcasted_iota(jnp.int32, (n, ORDER), 1)
    return col < Place(meta).live(level) * B


def row_mask(meta, level, n):
    own = lax.broadcasted_iota(jnp.int32, (n, 512), 1) // B
    place = Place(meta)
    tile = 4 * own + place.yi if level == 0 else 4 * place.zi + own
    return tile < Place(meta).live(level)


def solve_rows(level, meta, ev, yv, cs, late):
    first = Place(meta).ci if level else 0

    def body(j, carry):
        @pl.when(j == 1)
        def _():
            finish(late)

        at = pl.multiple_of(jnp.where(j == 0, first, 1 - first) * 256, 256)
        rows = pl.ds(at, 256)
        w = jnp.concatenate([ev[w, s, rows, :] for w, s in tiles_in_order(level)], 1)
        yv[:, rows] = product(cs, w, NTD)
        return carry

    lax.fori_loop(0, 2, body, 0)


WEIGHTS = (10, 2, 2, 2)


def forward_kernel(level, n, mode, meta, *refs):
    count = WEIGHTS[level]
    c_refs, refs = refs[:4], refs[4:]
    w_refs, refs = refs[:count], refs[count:]
    if mode == "rs":
        y_out, u_out = refs[0], refs[1:5]
        refs = refs[5:]
    else:
        y_out, keep_out, give_out = refs[:3]
        refs = refs[3:]
    ev, fv, cv, yv, uv, sems = refs
    early, late, last = copies(level, meta, w_refs, ev, fv, sems)
    for c in [*early, *late, *last]:
        c.start()
    r = n // 4
    if level < 2:
        for s in range(4):
            cv[pl.ds(s * r, r), :] = c_refs[s][...]
        c = cv[...]
    else:
        c = summed(c_refs, r)
    cs = stacked(jnp.where(column_mask(meta, level, n), c, 0.0))
    finish(early)
    solve_rows(level, meta, ev, yv, cs, late)
    y = jnp.where(row_mask(meta, level, n), yv[...], 0.0)
    y_out[...] = y
    ys = stacked(y)
    finish(last)

    def body(j, carry):
        w = jnp.concatenate([fv[w, j] for w in range(4)], 1)
        uv[:, pl.ds(pl.multiple_of(j * 256, 256), 256)] = product(ys, w, NTD)
        return carry

    lax.fori_loop(0, 4, body, 0)
    if mode == "rs":
        for s in range(4):
            u_out[s][...] = uv[pl.ds(s * r, r), :]
    else:
        split_rows(uv, r, Place(meta).bit(level), keep_out, give_out)


def split_rows(v, r, bit, keep_out, give_out):
    h = r // 2
    for s in range(4):
        low = v[pl.ds(s * r, h), :]
        high = v[pl.ds(s * r + h, h), :]
        keep_out[pl.ds(s * h, h), :] = jnp.where(bit == 0, low, high)
        give_out[pl.ds(s * h, h), :] = jnp.where(bit == 0, high, low)


def summed(refs, r):
    parts = []
    for s in range(4):
        total = refs[0][pl.ds(s * r, r), :]
        for d in (1, 2, 3):
            total = total + refs[d][pl.ds((s - d) % 4 * r, r), :]
        parts.append(total)
    return jnp.concatenate(parts, 0)


def add_tiles(meta, at, src, acc):
    for t in range(8):
        v = meta[at + t]
        cols = pl.ds(pl.multiple_of(lax.rem(v, NT) * B, B), B)
        lev = lax.div(v, NT)
        acc[lev, :, cols] = acc[lev, :, cols] + src[:, t * B : (t + 1) * B]


def take_tiles(meta, at, anc, dst):
    for t in range(8):
        v = meta[at + t]
        cols = pl.ds(pl.multiple_of(lax.rem(v, NT) * B, B), B)
        dst[:, t * B : (t + 1) * B] = anc[lax.div(v, NT), :, cols]


def s01_kernel(meta, keep, recv, b_mine, b_other, c1, pk, pg, acc):
    place = Place(meta)
    acc[...] = jnp.zeros_like(acc)
    add_tiles(meta, place.own(0), keep, acc)
    add_tiles(meta, place.partner(0), recv, acc)
    group = (0, place.x0, place.leaf >> 1)
    for ref, c in ((b_mine, place.ci), (b_other, 1 - place.ci)):
        at = 0
        for i in range(3):
            width = 1024 >> i
            cols = pl.ds(pl.multiple_of((2 * group[i] + c) * width, width), width)
            acc[i, :, cols] = acc[i, :, cols] - ref[:, at : at + width]
            at += width
    c1[...] = -acc[0]
    for i in (0, 1):
        low, high = acc[i + 1, 0:4, :], acc[i + 1, 4:8, :]
        pk[i] = jnp.where(place.x0 == 0, low, high)
        pg[i] = jnp.where(place.x0 == 0, high, low)


def s12_kernel(meta, keep, recv, pk, pr, part, keep3, give3, acc):
    place = Place(meta)
    acc[...] = jnp.zeros_like(acc)
    add_tiles(meta, place.own(1), keep, acc)
    add_tiles(meta, place.partner(1), recv, acc)
    for i in (0, 1):
        acc[i, 0:4, :] = acc[i, 0:4, :] + (pk[i] + pr[i])
    part[...] = -acc[0]
    split_rows(acc.at[1], 4, place.x1, keep3, give3)


def s23_kernel(meta, keep, recv, keep3, recv3, part, acc):
    place = Place(meta)
    acc[...] = jnp.zeros_like(acc)
    add_tiles(meta, place.own(2), keep, acc)
    add_tiles(meta, place.partner(2), recv, acc)
    part[...] = -(acc[0] + (keep3[...] + recv3[...]))


def top_kernel(meta, c0, c1, c2, c3, *refs):
    w_refs, (x_out, ev, yv, sems) = refs[:2], refs[2:]
    early, late, _ = copies(3, meta, w_refs, ev, None, sems)
    for c in [*early, *late]:
        c.start()
    c = summed((c0, c1, c2, c3), 2)
    cs = stacked(jnp.where(column_mask(meta, 3, 8), c, 0.0))
    finish(early)
    solve_rows(3, meta, ev, yv, cs, late)
    back(meta, 3, 8, ev, jnp.where(row_mask(meta, 3, 8), yv[...], 0.0), [x_out])


def back(meta, level, n, ev, z, x_out):
    zs = stacked(z)
    live = Place(meta).live(level) * B

    def body(j, carry):
        cols = pl.ds(pl.multiple_of(j * 512, 512), 512)
        w = jnp.concatenate([ev[j, i] if level == 0 else ev[i, j] for i in range(4)], 1)
        v = product(zs, w, NND)
        col = lax.broadcasted_iota(jnp.int32, (n, 512), 1) + j * 512
        v = jnp.where(col < live, v, 0.0)
        r = n // len(x_out)
        for s, out in enumerate(x_out):
            out[:, cols] = v[s * r : (s + 1) * r]
        return carry

    lax.fori_loop(0, 4, body, 0)


def x3_kernel(meta, c0, c1, c2, c3, x_out):
    x_out[...] = summed((c0, c1, c2, c3), 2)


def merged(a, b, h, bit):
    parts = []
    for s in range(4):
        u, v = a[s * h : (s + 1) * h, :], b[s * h : (s + 1) * h, :]
        parts += [jnp.where(bit == 0, u, v), jnp.where(bit == 0, v, u)]
    return jnp.concatenate(parts, 0)


def x2_kernel(meta, c0, c1, c2, c3, x3, x3r, anc_out, give):
    anc_out[0] = summed((c0, c1, c2, c3), 4)
    anc_out[1] = merged(x3[...], x3r[...], 2, Place(meta).x1)
    take_tiles(meta, Place(meta).partner(1), anc_out, give)


def x1_kernel(meta, c0, c1, c2, c3, a_mine, a_other, anc_out, give, own):
    anc_out[0] = (c0[...] + c1[...]) + (c2[...] + c3[...])
    for i in (0, 1):
        u, v = a_mine[i], a_other[i]
        bit = Place(meta).x0
        anc_out[i + 1, 0:4, :] = jnp.where(bit == 0, u, v)
        anc_out[i + 1, 4:8, :] = jnp.where(bit == 0, v, u)
    take_tiles(meta, Place(meta).partner(0), anc_out, give)
    take_tiles(meta, Place(meta).own(0), anc_out, own)


def backward_kernel(level, n, meta, *refs):
    count = WEIGHTS[level]
    if level == 0:
        g_refs, refs = refs[:4], refs[4:]
    else:
        (anc, recv), refs = refs[:2], refs[2:]
    y_ref, refs = refs[0], refs[1:]
    w_refs, refs = refs[:count], refs[count:]
    x_out, (ev, fv, gv, ov, sems) = refs[:-5], refs[-5:]
    early, late, first = copies(level, meta, w_refs, ev, fv, sems)
    for c in [*first, *early, *late]:
        c.start()
    r = n // 4
    if level == 0:
        for s in range(4):
            gv[pl.ds(s * r, r), :] = g_refs[s][...]
        g = gv[...]
    else:
        take_tiles(meta, Place(meta).own(level), anc, ov)
        if level == 2:
            take_tiles(meta, Place(meta).own(level), recv, gv)
            recv = gv
        g = merged(ov[...], recv[...], r // 2, Place(meta).bit(level))
    gs = stacked(g)
    finish(first)
    w = jnp.concatenate([fv[w].reshape(1024, B) for w in range(4)], 1)
    z = y_ref[...] - product(gs, w, NND)
    z = jnp.where(row_mask(meta, level, n), z, 0.0)
    finish(early)
    finish(late)
    back(meta, level, n, ev, z, x_out)


SMEM = pl.BlockSpec(memory_space=pltpu.SMEM)
VMEM = pl.BlockSpec(memory_space=pltpu.VMEM)
ANY = pl.BlockSpec(memory_space=pl.ANY)


def call(kernel, name, shapes, scratch, meta, small, weights=(), flops=0):
    weights = [pltpu.with_memory_space_constraint(w, pltpu.HBM) for w in weights]
    moved = sum(w.size * 4 for w in weights) + sum(v.size * 4 for v in small)
    return pl.pallas_call(
        kernel,
        out_shape=[jax.ShapeDtypeStruct(s, f32) for s in shapes],
        in_specs=[SMEM] + [VMEM] * len(small) + [ANY] * len(weights),
        out_specs=[VMEM] * len(shapes),
        scratch_shapes=scratch,
        compiler_params=pltpu.CompilerParams(vmem_limit_bytes=(14 if flops else 3) * 2**20),
        cost_estimate=pl.CostEstimate(flops=flops, bytes_accessed=moved, transcendentals=0),
        name=name,
    )(meta, *small, *weights)


def local(
    live_tiles, row_tiles, rhs0, rhs1, rhs2, rhs3, dinv0, dinv1, dinv2, dinv3, off0, off1, off2
):
    ci, x0, x1 = lax.axis_index("core"), lax.axis_index("x0"), lax.axis_index("x1")
    zi = lax.axis_index("z")
    leaf = x1 * 4 + x0 * 2 + ci
    here = leaf * 16 + zi * 4 + lax.axis_index("y")
    meta = jnp.concatenate([here.reshape(1), live_tiles, row_tiles.reshape(-1)])
    bits = [("core", ci), ("x0", x0), ("x1", x1)]

    def joined(v, i, dim=0):
        axis, bit = bits[i]
        return ordered(v, flip(v, axis), bit, dim)

    def pick(v, i, dim=0):
        return lax.dynamic_index_in_dim(v, i, dim, keepdims=False)

    def for_z(pair, other, bit):
        blocks = []
        for s in range(4):
            z = (zi + s) % 4
            blocks.append(jnp.where(z // 2 == bit, pick(pair, z % 2), pick(other, z % 2)))
        return blocks

    def over_z(blocks):
        return [blocks[0]] + [shift(blocks[s], "z", s) for s in (1, 2, 3)]

    def packed(blocks, f=None):
        parts = [v[None] for v in blocks] + ([] if f is None else [f.reshape(2, 256, B)])
        return jnp.concatenate(parts, 0)

    def gathered(block):
        return lax.all_gather(block, "y", axis=0, tiled=False)

    gate = lax.optimization_barrier
    off0 = off0.reshape(4, 256, B)
    fa, fb = shift(off0, "z", 1), shift(off0, "z", -1)
    fc, fd = shift(fa[:2], "z", 1), shift(fb[2:], "z", -1)
    e0 = jnp.swapaxes(dinv0.reshape(4, 4, B, B), 0, 1).reshape(4, 512, B)
    e0 = lax.all_to_all(e0, "y", 0, 0, tiled=True)
    e1 = dinv1.reshape(2, 2, 256, B)
    e1 = over_z(for_z(pick(e1, ci, 1), flip(pick(e1, 1 - ci, 1), "core"), ci))
    e2 = dinv2.reshape(2, 256, B)
    e2 = ordered(pick(e2, ci)[None], flip(pick(e2, 1 - ci)[None], "core"), ci, 0)
    e2_other = flip(e2, "x0")
    e0, e1, e2, e2_other, fa, fb, fc, fd, off2, dinv3, rhs0, rhs1 = gate(
        (e0, e1, e2, e2_other, fa, fb, fc, fd, off2, dinv3, rhs0, rhs1)
    )
    m1 = gathered(packed(e1, off1))

    ea, eb = shift(e0, "z", 1), shift(e0, "z", -1)
    f2 = joined(off2, 1)
    e3 = joined(dinv3[None], 1)
    e3_other = flip(e3, "x1")
    e23 = zip(for_z(e2, e2_other, x0), for_z(e3, e3_other, x1))
    e23 = over_z([jnp.stack(pair) for pair in e23])
    b_mine, b_other = halves(jnp.concatenate([rhs1, rhs2, rhs3], 1), ci)
    b_other = flip(b_other, "core")
    ea, eb, e23[0], f2, b_mine, b_other = gate((ea, eb, e23[0], f2, b_mine, b_other))

    ec, ed = shift(ea[:2], "z", 1), shift(eb[2:], "z", -1)
    e2, rhs0 = gate((packed([v[0] for v in e23], f2), rhs0))
    m2 = gathered(e2)
    c0 = gather4(rhs0, "y")
    ec, ed, c0 = gate((ec, ed, c0))
    w0 = [e0, ea, eb, ec, ed, off0, fa, fb, fc, fd]

    dma = pltpu.SemaphoreType.DMA
    ev, fv = pltpu.VMEM((4, 4, 512, B), f32), pltpu.VMEM((4, 4, 256, B), f32)

    def work(n):
        return [pltpu.VMEM((n, ORDER), f32), pltpu.VMEM((n, 512), f32), pltpu.VMEM((n, 1024), f32)]

    def flops(n):
        return 2 * n * 512 * (2048 + 1024) * 12

    y0, *u = call(
        functools.partial(forward_kernel, 0, 64, "rs"), "f0", [(64, 512)] + [(16, 1024)] * 4,
        [ev, fv, *work(64), dma((10,))], meta, c0, w0, flops(64),
    )
    parts = scatter4(u, "y")
    u = (parts[0] + parts[1]) + (parts[2] + parts[3])
    e3, u = gate((packed([v[1] for v in e23]), u))
    m3 = gathered(e3)
    keep, give = halves(u, ci)
    c1, pk, pg = call(
        s01_kernel, "s01", [(8, ORDER), (2, 4, ORDER), (2, 4, ORDER)],
        [pltpu.VMEM((3, 8, ORDER), f32)], meta, [keep, flip(give, "core"), b_mine, b_other],
    )
    m1, _ = gate((m1, c1))
    w1 = m1, flip(m1, "core")
    pr = flip(pg, "x0")
    y1, keep, give = call(
        functools.partial(forward_kernel, 1, 32, "ar"), "f1", [(32, 512), (16, 1024), (16, 1024)],
        [ev, fv, *work(32), dma((12,))], meta, gather4(c1, "z"), w1, flops(32),
    )
    recv = flip(give, "x0")
    part, keep3, give3 = call(
        s12_kernel, "s12", [(16, ORDER), (8, ORDER), (8, ORDER)],
        [pltpu.VMEM((2, 16, ORDER), f32)], meta, [keep, recv, pk, pr],
    )
    m2, _ = gate((m2, recv))
    w2 = m2, flip(m2, "core")
    recv3 = flip(give3, "x1")
    y2, keep, give = call(
        functools.partial(forward_kernel, 2, 16, "ar"), "f2", [(16, 512), (8, 1024), (8, 1024)],
        [ev, fv, *work(16), dma((12,))], meta, gather4(part, "z"), w2, flops(16),
    )
    (part,) = call(
        s23_kernel, "s23", [(8, ORDER)],
        [pltpu.VMEM((1, 8, ORDER), f32)], meta, [keep, flip(give, "x1"), keep3, recv3],
    )

    m3, _ = gate((m3, part))
    w3 = m3, flip(m3, "core")
    (part,) = call(
        top_kernel, "top", [(8, ORDER)], [ev, pltpu.VMEM((8, 512), f32), dma((8,))],
        meta, gather4(part, "z"), w3, flops(8),
    )
    (x3,) = call(x3_kernel, "x3", [(8, ORDER)], [], meta, gather4(part, "z"))
    x3r = flip(x3, "x1")

    def rest(n):
        rows = n if n != 16 else 8
        return [ev, fv, pltpu.VMEM((rows, 1024), f32), pltpu.VMEM((n // 2, 1024), f32), dma((12,))]

    (part,) = call(
        functools.partial(backward_kernel, 2, 16), "b2", [(16, ORDER)], rest(16),
        meta, [x3[None], x3r[None], y2], w2, flops(16),
    )
    anc, give = call(
        x2_kernel, "x2", [(2, 16, ORDER), (16, 1024)], [],
        meta, gather4(part, "z") + [x3, x3r],
    )
    recv = flip(give, "x0")
    a_mine = anc[:, :4]
    a_other = flip(a_mine, "x0")
    parts = call(
        functools.partial(backward_kernel, 1, 32), "b1", [(8, ORDER)] * 4, rest(32),
        meta, [anc, recv, y1], w1, flops(32),
    )
    anc, give, own = call(
        x1_kernel, "x1", [(3, 8, ORDER), (8, 1024), (8, 1024)], [],
        meta, scatter4(parts, "z") + [a_mine, a_other],
    )
    g = ordered(own, flip(give, "core"), ci, 0)
    parts = call(
        functools.partial(backward_kernel, 0, 64), "b0", [(16, ORDER)] * 4, rest(64),
        meta, gather4(g, "y") + [y0], w0, flops(64),
    )
    parts = scatter4(parts, "y")
    sol0 = (parts[0] + parts[1]) + (parts[2] + parts[3])

    outs = [sol0]
    for k in (1, 2, 3):
        width = ORDER // 2**k
        place = leaf % 2**k
        mine = lax.dynamic_slice_in_dim(anc[k - 1], place * width, width, 1)
        give = lax.dynamic_slice_in_dim(anc[k - 1], (place ^ 1) * width, width, 1)
        outs.append(ordered(mine, flip(give, "core"), ci, 0))
    return tuple(outs)


def solution(mesh):
    fine = Mesh(mesh.devices.reshape(2, 2, 2, 4, 4), ("x1", "x0", "core", "z", "y"))
    leaf, panel = ("x1", "x0", "core"), ("z", "y")
    return jax.shard_map(
        local,
        mesh=fine,
        in_specs=(P(), P()) + (P(panel, leaf),) * 4 + (P(leaf, panel),) * 7,
        out_specs=(P(panel, leaf),) * 4,
        check_vma=False,
    )
```

```python
import functools
import jax
import jax.numpy as jnp
from jax import lax
from jax.experimental import pallas as pl
from jax.experimental.pallas import tpu as pltpu
from jax.sharding import Mesh, PartitionSpec as P

B = 128
ORDER = 2048
NT = 16
f32 = jnp.float32
bf16 = jnp.bfloat16

FIRST = (0, 8, 12, 14)


class Place:
    def __init__(self, meta):
        self.meta = meta
        self.leaf = meta[0] >> 4
        self.zi, self.yi = (meta[0] >> 2) & 3, meta[0] & 3
        self.ci, self.x0, self.x1 = self.leaf & 1, (self.leaf >> 1) & 1, self.leaf >> 2

    def live(self, level):
        return self.meta[1 + FIRST[level] + (self.leaf >> level)]

    def own(self, level):
        return 16 + 8 * (FIRST[level] + (self.leaf >> level))

    def partner(self, level):
        return 16 + 8 * (FIRST[level] + ((self.leaf >> level) ^ 1))

    def bit(self, level):
        return (self.ci, self.x0, self.x1)[level]


def shift(v, axis, s):
    return lax.ppermute(v, axis, [(i, (i + s) % 4) for i in range(4)])


def flip(v, axis):
    return lax.ppermute(v, axis, [(0, 1), (1, 0)])


def gather4(v, axis):
    far = shift(v, axis, 2)
    return [v, shift(v, axis, 1), far, shift(v, axis, 3)]


def scatter4(parts, axis):
    far = shift(parts[2], axis, 2)
    return [parts[0], shift(parts[1], axis, -1), far, shift(parts[3], axis, 1)]


def ring(v, axis, dim):
    h = v.shape[dim] // 2
    a = shift(v, axis, 1)
    b = shift(v, axis, -1)
    c = shift(lax.slice_in_dim(a, 0, h, axis=dim), axis, 1)
    d = shift(lax.slice_in_dim(b, h, 2 * h, axis=dim), axis, -1)
    return [v, a, b, c, d]


def ordered(mine, other, bit, dim):
    return jnp.where(
        bit == 0, jnp.concatenate([mine, other], dim), jnp.concatenate([other, mine], dim)
    )


def halves(v, bit):
    h = v.shape[0] // 2
    return (
        jnp.where(bit == 0, v[:h], v[h:]),
        jnp.where(bit == 0, v[h:], v[:h]),
    )


def stacked(v):
    hi = v.astype(bf16).astype(f32)
    return jnp.concatenate([hi, v - hi], 0).astype(bf16)


def product(left, w, dims):
    hi = w.astype(bf16)
    lo = (w - hi.astype(f32)).astype(bf16)
    r = lax.dot_general(left, hi, (dims, ((), ())), preferred_element_type=f32)
    r = r + lax.dot_general(left, lo, (dims, ((), ())), preferred_element_type=f32)
    n = left.shape[0] // 2
    return r[:n] + r[n:]


NTD = ((1,), (1,))
NND = ((1,), (0,))


def copies_first(meta, refs, ev, fv, sems):
    e, f = refs[:5], refs[5:]
    zi = Place(meta).zi
    spots = [zi, lax.rem(zi + 3, 4), lax.rem(zi + 1, 4)]
    far = lax.rem(zi + 2, 4)
    pairs_e = [(ref, ev.at[w]) for ref, w in zip(e[:3], spots)]
    pairs_e += [(e[3], ev.at[far, 0:2]), (e[4], ev.at[far, 2:4])]
    pairs_f = [(ref, fv.at[w]) for ref, w in zip(f[:3], spots)]
    pairs_f += [(f[3], fv.at[far, 0:2]), (f[4], fv.at[far, 2:4])]
    made = [
        pltpu.make_async_copy(src, dst, sems.at[k]) for k, (src, dst) in enumerate(pairs_e + pairs_f)
    ]
    return made[:5], [], made[5:]


def copies_upper(level, meta, bufs, ev, fv, sems):
    place = Place(meta)
    groups = ([], [], [])
    k = 0
    for i, q in ((0, place.ci), (1, 1 - place.ci)):
        rows = pl.ds(pl.multiple_of(q * 256, 256), 256)
        pairs = [(bufs[i].at[:, s], ev.at[:, lax.rem(place.zi + 4 - s, 4), rows]) for s in range(4)]
        late = []
        if level == 1:
            late = [(bufs[i].at[:, 4:6], fv.at[:, pl.ds(2 * q, 2)])]
        elif level == 2:
            late = [(bufs[i].at[:, 4 + h], fv.at[:, 2 * h + q]) for h in (0, 1)]
        for group, some in ((groups[i], pairs), (groups[2], late)):
            for src, dst in some:
                group.append(pltpu.make_async_copy(src, dst, sems.at[k]))
                k += 1
    return groups


def copies(level, meta, refs, ev, fv, sems):
    if level == 0:
        return copies_first(meta, refs, ev, fv, sems)
    return copies_upper(level, meta, refs, ev, fv, sems)


def finish(group):
    for c in group:
        c.wait()


def tiles_in_order(level):
    if level == 0:
        return [(t // 4, t % 4) for t in range(NT)]
    return [(t % 4, t // 4) for t in range(NT)]


def column_mask(meta, level, n):
    col = lax.broadcasted_iota(jnp.int32, (n, ORDER), 1)
    return col < Place(meta).live(level) * B


def row_mask(meta, level, n):
    own = lax.broadcasted_iota(jnp.int32, (n, 512), 1) // B
    place = Place(meta)
    tile = 4 * own + place.yi if level == 0 else 4 * place.zi + own
    return tile < Place(meta).live(level)


def solve_rows(level, meta, ev, yv, cs, late):
    first = Place(meta).ci if level else 0

    def body(j, carry):
        @pl.when(j == 1)
        def _():
            finish(late)

        at = pl.multiple_of(jnp.where(j == 0, first, 1 - first) * 256, 256)
        rows = pl.ds(at, 256)
        w = jnp.concatenate([ev[w, s, rows, :] for w, s in tiles_in_order(level)], 1)
        yv[:, rows] = product(cs, w, NTD)
        return carry

    lax.fori_loop(0, 2, body, 0)


WEIGHTS = (10, 2, 2, 2)


def forward_kernel(level, n, mode, meta, *refs):
    count = WEIGHTS[level]
    c_refs, refs = refs[:4], refs[4:]
    w_refs, refs = refs[:count], refs[count:]
    if mode == "rs":
        y_out, u_out = refs[0], refs[1:5]
        refs = refs[5:]
    else:
        y_out, keep_out, give_out = refs[:3]
        refs = refs[3:]
    ev, fv, cv, yv, uv, sems = refs
    early, late, last = copies(level, meta, w_refs, ev, fv, sems)
    for c in [*early, *late, *last]:
        c.start()
    r = n // 4
    if level < 2:
        for s in range(4):
            cv[pl.ds(s * r, r), :] = c_refs[s][...]
        c = cv[...]
    else:
        c = summed(c_refs, r)
    cs = stacked(jnp.where(column_mask(meta, level, n), c, 0.0))
    finish(early)
    solve_rows(level, meta, ev, yv, cs, late)
    y = jnp.where(row_mask(meta, level, n), yv[...], 0.0)
    y_out[...] = y
    ys = stacked(y)
    finish(last)

    def body(j, carry):
        w = jnp.concatenate([fv[w, j] for w in range(4)], 1)
        uv[:, pl.ds(pl.multiple_of(j * 256, 256), 256)] = product(ys, w, NTD)
        return carry

    lax.fori_loop(0, 4, body, 0)
    if mode == "rs":
        for s in range(4):
            u_out[s][...] = uv[pl.ds(s * r, r), :]
    else:
        split_rows(uv, r, Place(meta).bit(level), keep_out, give_out)


def split_rows(v, r, bit, keep_out, give_out):
    h = r // 2
    for s in range(4):
        low = v[pl.ds(s * r, h), :]
        high = v[pl.ds(s * r + h, h), :]
        keep_out[pl.ds(s * h, h), :] = jnp.where(bit == 0, low, high)
        give_out[pl.ds(s * h, h), :] = jnp.where(bit == 0, high, low)


def summed(refs, r):
    parts = []
    for s in range(4):
        total = refs[0][pl.ds(s * r, r), :]
        for d in (1, 2, 3):
            total = total + refs[d][pl.ds((s - d) % 4 * r, r), :]
        parts.append(total)
    return jnp.concatenate(parts, 0)


def add_tiles(meta, at, src, acc):
    for t in range(8):
        v = meta[at + t]
        cols = pl.ds(pl.multiple_of(lax.rem(v, NT) * B, B), B)
        lev = lax.div(v, NT)
        acc[lev, :, cols] = acc[lev, :, cols] + src[:, t * B : (t + 1) * B]


def take_tiles(meta, at, anc, dst):
    for t in range(8):
        v = meta[at + t]
        cols = pl.ds(pl.multiple_of(lax.rem(v, NT) * B, B), B)
        dst[:, t * B : (t + 1) * B] = anc[lax.div(v, NT), :, cols]


def s01_kernel(meta, keep, recv, b_mine, b_other, c1, pk, pg, acc):
    place = Place(meta)
    acc[...] = jnp.zeros_like(acc)
    add_tiles(meta, place.own(0), keep, acc)
    add_tiles(meta, place.partner(0), recv, acc)
    group = (0, place.x0, place.leaf >> 1)
    for ref, c in ((b_mine, place.ci), (b_other, 1 - place.ci)):
        at = 0
        for i in range(3):
            width = 1024 >> i
            cols = pl.ds(pl.multiple_of((2 * group[i] + c) * width, width), width)
            acc[i, :, cols] = acc[i, :, cols] - ref[:, at : at + width]
            at += width
    c1[...] = -acc[0]
    for i in (0, 1):
        low, high = acc[i + 1, 0:4, :], acc[i + 1, 4:8, :]
        pk[i] = jnp.where(place.x0 == 0, low, high)
        pg[i] = jnp.where(place.x0 == 0, high, low)


def s12_kernel(meta, keep, recv, pk, pr, part, keep3, give3, acc):
    place = Place(meta)
    acc[...] = jnp.zeros_like(acc)
    add_tiles(meta, place.own(1), keep, acc)
    add_tiles(meta, place.partner(1), recv, acc)
    for i in (0, 1):
        acc[i, 0:4, :] = acc[i, 0:4, :] + (pk[i] + pr[i])
    part[...] = -acc[0]
    split_rows(acc.at[1], 4, place.x1, keep3, give3)


def s23_kernel(meta, keep, recv, keep3, recv3, part, acc):
    place = Place(meta)
    acc[...] = jnp.zeros_like(acc)
    add_tiles(meta, place.own(2), keep, acc)
    add_tiles(meta, place.partner(2), recv, acc)
    part[...] = -(acc[0] + (keep3[...] + recv3[...]))


def top_kernel(meta, c0, c1, c2, c3, *refs):
    w_refs, (x_out, ev, yv, sems) = refs[:2], refs[2:]
    early, late, _ = copies(3, meta, w_refs, ev, None, sems)
    for c in [*early, *late]:
        c.start()
    c = summed((c0, c1, c2, c3), 2)
    cs = stacked(jnp.where(column_mask(meta, 3, 8), c, 0.0))
    finish(early)
    solve_rows(3, meta, ev, yv, cs, late)
    back(meta, 3, 8, ev, jnp.where(row_mask(meta, 3, 8), yv[...], 0.0), [x_out])


def back(meta, level, n, ev, z, x_out):
    zs = stacked(z)
    live = Place(meta).live(level) * B

    def body(j, carry):
        cols = pl.ds(pl.multiple_of(j * 512, 512), 512)
        w = jnp.concatenate([ev[j, i] if level == 0 else ev[i, j] for i in range(4)], 1)
        v = product(zs, w, NND)
        col = lax.broadcasted_iota(jnp.int32, (n, 512), 1) + j * 512
        v = jnp.where(col < live, v, 0.0)
        r = n // len(x_out)
        for s, out in enumerate(x_out):
            out[:, cols] = v[s * r : (s + 1) * r]
        return carry

    lax.fori_loop(0, 4, body, 0)


def x3_kernel(meta, c0, c1, c2, c3, x_out):
    x_out[...] = summed((c0, c1, c2, c3), 2)


def merged(a, b, h, bit):
    parts = []
    for s in range(4):
        u, v = a[s * h : (s + 1) * h, :], b[s * h : (s + 1) * h, :]
        parts += [jnp.where(bit == 0, u, v), jnp.where(bit == 0, v, u)]
    return jnp.concatenate(parts, 0)


def x2_kernel(meta, c0, c1, c2, c3, x3, x3r, anc_out, give):
    anc_out[0] = summed((c0, c1, c2, c3), 4)
    anc_out[1] = merged(x3[...], x3r[...], 2, Place(meta).x1)
    take_tiles(meta, Place(meta).partner(1), anc_out, give)


def x1_kernel(meta, c0, c1, c2, c3, a_mine, a_other, anc_out, give, own):
    anc_out[0] = (c0[...] + c1[...]) + (c2[...] + c3[...])
    for i in (0, 1):
        u, v = a_mine[i], a_other[i]
        bit = Place(meta).x0
        anc_out[i + 1, 0:4, :] = jnp.where(bit == 0, u, v)
        anc_out[i + 1, 4:8, :] = jnp.where(bit == 0, v, u)
    take_tiles(meta, Place(meta).partner(0), anc_out, give)
    take_tiles(meta, Place(meta).own(0), anc_out, own)


def backward_kernel(level, n, meta, *refs):
    count = WEIGHTS[level]
    if level == 0:
        g_refs, refs = refs[:4], refs[4:]
    else:
        (anc, recv), refs = refs[:2], refs[2:]
    y_ref, refs = refs[0], refs[1:]
    w_refs, refs = refs[:count], refs[count:]
    x_out, (ev, fv, gv, ov, sems) = refs[:-5], refs[-5:]
    early, late, first = copies(level, meta, w_refs, ev, fv, sems)
    for c in [*first, *early, *late]:
        c.start()
    r = n // 4
    if level == 0:
        for s in range(4):
            gv[pl.ds(s * r, r), :] = g_refs[s][...]
        g = gv[...]
    else:
        take_tiles(meta, Place(meta).own(level), anc, ov)
        if level == 2:
            take_tiles(meta, Place(meta).own(level), recv, gv)
            recv = gv
        g = merged(ov[...], recv[...], r // 2, Place(meta).bit(level))
    gs = stacked(g)
    finish(first)
    w = jnp.concatenate([fv[w].reshape(1024, B) for w in range(4)], 1)
    z = y_ref[...] - product(gs, w, NND)
    z = jnp.where(row_mask(meta, level, n), z, 0.0)
    finish(early)
    finish(late)
    back(meta, level, n, ev, z, x_out)


SMEM = pl.BlockSpec(memory_space=pltpu.SMEM)
VMEM = pl.BlockSpec(memory_space=pltpu.VMEM)
ANY = pl.BlockSpec(memory_space=pl.ANY)


def call(kernel, name, shapes, scratch, meta, small, weights=(), flops=0):
    weights = [pltpu.with_memory_space_constraint(w, pltpu.HBM) for w in weights]
    moved = sum(w.size * 4 for w in weights) + sum(v.size * 4 for v in small)
    return pl.pallas_call(
        kernel,
        out_shape=[jax.ShapeDtypeStruct(s, f32) for s in shapes],
        in_specs=[SMEM] + [VMEM] * len(small) + [ANY] * len(weights),
        out_specs=[VMEM] * len(shapes),
        scratch_shapes=scratch,
        compiler_params=pltpu.CompilerParams(vmem_limit_bytes=(14 if flops else 3) * 2**20),
        cost_estimate=pl.CostEstimate(flops=flops, bytes_accessed=moved, transcendentals=0),
        name=name,
    )(meta, *small, *weights)


def local(
    live_tiles, row_tiles, rhs0, rhs1, rhs2, rhs3, dinv0, dinv1, dinv2, dinv3, off0, off1, off2
):
    ci, x0, x1 = lax.axis_index("core"), lax.axis_index("x0"), lax.axis_index("x1")
    zi = lax.axis_index("z")
    leaf = x1 * 4 + x0 * 2 + ci
    here = leaf * 16 + zi * 4 + lax.axis_index("y")
    meta = jnp.concatenate([here.reshape(1), live_tiles, row_tiles.reshape(-1)])
    bits = [("core", ci), ("x0", x0), ("x1", x1)]

    def joined(v, i, dim=0):
        axis, bit = bits[i]
        return ordered(v, flip(v, axis), bit, dim)

    def pick(v, i, dim=0):
        return lax.dynamic_index_in_dim(v, i, dim, keepdims=False)

    def for_z(pair, other, bit):
        blocks = []
        for s in range(4):
            z = (zi + s) % 4
            blocks.append(jnp.where(z // 2 == bit, pick(pair, z % 2), pick(other, z % 2)))
        return blocks

    def over_z(blocks):
        return [blocks[0]] + [shift(blocks[s], "z", s) for s in (1, 2, 3)]

    def packed(blocks, f=None):
        parts = [v[None] for v in blocks] + ([] if f is None else [f.reshape(2, 256, B)])
        return jnp.concatenate(parts, 0)

    def gathered(block):
        return lax.all_gather(block, "y", axis=0, tiled=False)

    gate = lax.optimization_barrier
    off0 = off0.reshape(4, 256, B)
    fa, fb = shift(off0, "z", 1), shift(off0, "z", -1)
    fc, fd = shift(fa[:2], "z", 1), shift(fb[2:], "z", -1)
    e0 = jnp.swapaxes(dinv0.reshape(4, 4, B, B), 0, 1).reshape(4, 512, B)
    e0 = lax.all_to_all(e0, "y", 0, 0, tiled=True)
    e1 = dinv1.reshape(2, 2, 256, B)
    e1 = over_z(for_z(pick(e1, ci, 1), flip(pick(e1, 1 - ci, 1), "core"), ci))
    e2 = dinv2.reshape(2, 256, B)
    e2 = ordered(pick(e2, ci)[None], flip(pick(e2, 1 - ci)[None], "core"), ci, 0)
    e2_other = flip(e2, "x0")
    e0, e1, e2, e2_other, fa, fb, fc, fd, off2, dinv3, rhs0, rhs1 = gate(
        (e0, e1, e2, e2_other, fa, fb, fc, fd, off2, dinv3, rhs0, rhs1)
    )
    m1 = gathered(packed(e1, off1))

    ea, eb = shift(e0, "z", 1), shift(e0, "z", -1)
    f2 = joined(off2, 1)
    e3 = joined(dinv3[None], 1)
    e3_other = flip(e3, "x1")
    e23 = zip(for_z(e2, e2_other, x0), for_z(e3, e3_other, x1))
    e23 = over_z([jnp.stack(pair) for pair in e23])
    b_mine, b_other = halves(jnp.concatenate([rhs1, rhs2, rhs3], 1), ci)
    b_other = flip(b_other, "core")
    ea, eb, e23[0], f2, b_mine, b_other = gate((ea, eb, e23[0], f2, b_mine, b_other))

    ec, ed = shift(ea[:2], "z", 1), shift(eb[2:], "z", -1)
    e2, rhs0 = gate((packed([v[0] for v in e23], f2), rhs0))
    m2 = gathered(e2)
    c0 = gather4(rhs0, "y")
    ec, ed, c0 = gate((ec, ed, c0))
    w0 = [e0, ea, eb, ec, ed, off0, fa, fb, fc, fd]

    dma = pltpu.SemaphoreType.DMA
    ev, fv = pltpu.VMEM((4, 4, 512, B), f32), pltpu.VMEM((4, 4, 256, B), f32)

    def work(n):
        return [pltpu.VMEM((n, ORDER), f32), pltpu.VMEM((n, 512), f32), pltpu.VMEM((n, 1024), f32)]

    def flops(n):
        return 2 * n * 512 * (2048 + 1024) * 12

    y0, *u = call(
        functools.partial(forward_kernel, 0, 64, "rs"), "f0", [(64, 512)] + [(16, 1024)] * 4,
        [ev, fv, *work(64), dma((10,))], meta, c0, w0, flops(64),
    )
    parts = scatter4(u, "y")
    u = (parts[0] + parts[1]) + (parts[2] + parts[3])
    e3, u = gate((packed([v[1] for v in e23]), u))
    m3 = gathered(e3)
    keep, give = halves(u, ci)
    c1, pk, pg = call(
        s01_kernel, "s01", [(8, ORDER), (2, 4, ORDER), (2, 4, ORDER)],
        [pltpu.VMEM((3, 8, ORDER), f32)], meta, [keep, flip(give, "core"), b_mine, b_other],
    )
    m1, _ = gate((m1, c1))
    w1 = m1, flip(m1, "core")
    pr = flip(pg, "x0")
    m2, pr, c1 = gate((m2, pr, gather4(c1, "z")))
    w2 = m2, flip(m2, "core")
    y1, keep, give = call(
        functools.partial(forward_kernel, 1, 32, "ar"), "f1", [(32, 512), (16, 1024), (16, 1024)],
        [ev, fv, *work(32), dma((12,))], meta, c1, w1, flops(32),
    )
    recv = flip(give, "x0")
    part, keep3, give3 = call(
        s12_kernel, "s12", [(16, ORDER), (8, ORDER), (8, ORDER)],
        [pltpu.VMEM((2, 16, ORDER), f32)], meta, [keep, recv, pk, pr],
    )
    recv3 = flip(give3, "x1")
    y2, keep, give = call(
        functools.partial(forward_kernel, 2, 16, "ar"), "f2", [(16, 512), (8, 1024), (8, 1024)],
        [ev, fv, *work(16), dma((12,))], meta, gather4(part, "z"), w2, flops(16),
    )
    (part,) = call(
        s23_kernel, "s23", [(8, ORDER)],
        [pltpu.VMEM((1, 8, ORDER), f32)], meta, [keep, flip(give, "x1"), keep3, recv3],
    )

    m3, _ = gate((m3, part))
    w3 = m3, flip(m3, "core")
    (part,) = call(
        top_kernel, "top", [(8, ORDER)], [ev, pltpu.VMEM((8, 512), f32), dma((8,))],
        meta, gather4(part, "z"), w3, flops(8),
    )
    (x3,) = call(x3_kernel, "x3", [(8, ORDER)], [], meta, gather4(part, "z"))
    x3r = flip(x3, "x1")

    def rest(n):
        rows = n if n != 16 else 8
        return [ev, fv, pltpu.VMEM((rows, 1024), f32), pltpu.VMEM((n // 2, 1024), f32), dma((12,))]

    (part,) = call(
        functools.partial(backward_kernel, 2, 16), "b2", [(16, ORDER)], rest(16),
        meta, [x3[None], x3r[None], y2], w2, flops(16),
    )
    anc, give = call(
        x2_kernel, "x2", [(2, 16, ORDER), (16, 1024)], [],
        meta, gather4(part, "z") + [x3, x3r],
    )
    recv = flip(give, "x0")
    a_mine = anc[:, :4]
    a_other = flip(a_mine, "x0")
    parts = call(
        functools.partial(backward_kernel, 1, 32), "b1", [(8, ORDER)] * 4, rest(32),
        meta, [anc, recv, y1], w1, flops(32),
    )
    anc, give, own = call(
        x1_kernel, "x1", [(3, 8, ORDER), (8, 1024), (8, 1024)], [],
        meta, scatter4(parts, "z") + [a_mine, a_other],
    )
    g = ordered(own, flip(give, "core"), ci, 0)
    parts = call(
        functools.partial(backward_kernel, 0, 64), "b0", [(16, ORDER)] * 4, rest(64),
        meta, gather4(g, "y") + [y0], w0, flops(64),
    )
    parts = scatter4(parts, "y")
    sol0 = (parts[0] + parts[1]) + (parts[2] + parts[3])

    outs = [sol0]
    for k in (1, 2, 3):
        width = ORDER // 2**k
        place = leaf % 2**k
        mine = lax.dynamic_slice_in_dim(anc[k - 1], place * width, width, 1)
        give = lax.dynamic_slice_in_dim(anc[k - 1], (place ^ 1) * width, width, 1)
        outs.append(ordered(mine, flip(give, "core"), ci, 0))
    return tuple(outs)


def solution(mesh):
    fine = Mesh(mesh.devices.reshape(2, 2, 2, 4, 4), ("x1", "x0", "core", "z", "y"))
    leaf, panel = ("x1", "x0", "core"), ("z", "y")
    return jax.shard_map(
        local,
        mesh=fine,
        in_specs=(P(), P()) + (P(panel, leaf),) * 4 + (P(leaf, panel),) * 7,
        out_specs=(P(panel, leaf),) * 4,
        check_vma=False,
    )
```
